512 devices in a mesh: gx: 16 (over y_hi, z), gy: 4 (over y_lo), gz: 8 (over x, core).
Axes of the slice: x: 4, y: 8 (y_hi: 2, y_lo: 4; y = y_hi * 4 + y_lo), z: 8, core: 2. Of those that a mesh axis runs over, the one named last changes fastest.
Arguments:
- field: float32 [4, 128, 512, 512], P(None, ('gx', 'gz'), 'gy'), may hold values from -6 to 6
- brick_order: int32 [32], replicated, may hold values from 0 to 31, each once
- start_first: float32 [128, 32], replicated, may hold values from -6 to 6
- start_second: float32 [512, 32], replicated, may hold values from -6 to 6
- start_third: float32 [512, 32], replicated, may hold values from -6 to 6
Outputs:
- core: float32 [128, 32, 32], P(('gx', 'gy'), 'gz')
The draws below stay inside these ranges and needn't reach their ends.
Inputs may be any that keep to these rules, and one draw needn't show every extreme that they name: `brick_order`: each of 0 to 31 appears exactly once.
All inputs are finite; a program needn't handle non-finite values.
Results may differ from the reference program's by a relative error of at most 0.0003.
Values sent between devices are 32-bit elements; how exact they have to be, the bound alone decides.
No kernel may reach another device: no remote copies, remote signals or barrier semaphores. Data moves between devices by JAX's collectives and lax.ppermute only.
A program may use at most 64 MiB of HBM per device.

```python
import jax
import jax.numpy as jnp
from jax import lax

S = 4
NY = 512
R1 = 32
R2 = 32
R3 = 32
ITERS = 2
NX = 128
NZ = 512
BRICKS = 32


def block_levels(rng, extent, pieces, least, largest):
    def one(axis_at, parts):
        heights = jax.random.uniform(jax.random.fold_in(jax.random.fold_in(rng, 6), axis_at), (parts,), jnp.float32, least / len(pieces), largest / len(pieces))
        return jnp.repeat(jnp.exp(heights), extent[axis_at] // parts).reshape((-1,) + (1,) * (len(extent) - axis_at - 1))

    level = one(*pieces[0])
    for cut in pieces[1:]:
        level = level * one(*cut)
    return level


def scatter_about(stream_key, extent, deviation, limit, cuts=(), held_as=jnp.bfloat16):
    result = deviation * jax.random.normal(stream_key, extent, jnp.float32)
    if cuts:
        result = result * block_levels(stream_key, extent, cuts, -0.22, 0.18)
    return jnp.clip(result, -limit, limit).astype(held_as)


def setup_inputs(seed: int = 0) -> dict:
    streams_of = jax.random.split(jax.random.key(seed), 6)
    field = scatter_about(streams_of[0], (S, NX, NY, NZ), 1.0, 6.0, ((1, 128), (2, 4)), jnp.float32)
    brick_order = jax.random.permutation(streams_of[1], BRICKS).astype(jnp.int32)
    start_first = scatter_about(streams_of[2], (NX, R1), 1.0, 6.0, (), jnp.float32)
    start_second = scatter_about(streams_of[3], (NY, R2), 1.0, 6.0, (), jnp.float32)
    start_third = scatter_about(streams_of[4], (NZ, R3), 1.0, 6.0, (), jnp.float32)
    return {"field": field, "brick_order": brick_order, "start_first": start_first, "start_second": start_second, "start_third": start_third}


highest = lax.Precision.HIGHEST

def orthonormal(columns):
    inner_gram = jnp.dot(columns.T, columns, precision=highest)
    factor_low = jnp.linalg.cholesky(inner_gram)
    return jax.scipy.linalg.solve_triangular(factor_low, columns.T, lower=True).T

def subspace(gram_mat, initial):
    current = initial
    for repeat in range(ITERS):
        current = orthonormal(jnp.dot(gram_mat, current, precision=highest))
    return current

def reference(field, brick_order, start_first, start_second, start_third):
    stored = field.reshape(S, NX, NY, BRICKS, NZ // BRICKS)
    inverse = jnp.zeros((BRICKS,), jnp.int32).at[brick_order].set(jnp.arange(BRICKS, dtype=jnp.int32))
    taper = 0.5 + 1.5 * lax.iota(jnp.float32, NZ) / (NZ - 1)
    tensor = jnp.take(stored, inverse, axis=3).reshape(S, NX, NY, NZ) * taper
    gram_first = jnp.einsum('sxyz,swyz->xw', tensor, tensor, precision=highest)
    factor_first = subspace(gram_first, start_first)
    after_first = jnp.einsum('sxyz,xr->sryz', tensor, factor_first, precision=highest).reshape(S * R1, NY, NZ)
    gram_second = jnp.einsum('myz,muz->yu', after_first, after_first, precision=highest)
    factor_second = subspace(gram_second, start_second)
    after_second = jnp.einsum('myz,yq->mqz', after_first, factor_second, precision=highest)
    gram_third = jnp.einsum('mqz,mqw->zw', after_second, after_second, precision=highest)
    factor_third = subspace(gram_third, start_third)
    return jnp.einsum('mqz,zt->mqt', after_second, factor_third, precision=highest)
```

```python
import functools

import jax
import jax.numpy as jnp
from jax import lax
from jax.experimental import pallas as pl
from jax.experimental.pallas import tpu as pltpu
from jax.sharding import PartitionSpec as P

ITERS = 2
LANES = 128
ORDER = ("gy", "gx", "gz")

highest = lax.Precision.HIGHEST


def mm(a, b, dims):
    return lax.dot_general(a, b, (dims, ((), ())), precision=highest, preferred_element_type=jnp.float32)


def mm_nn(a, b):
    return mm(a, b, ((1,), (0,)))


def mm_nt(a, b):
    return mm(a, b, ((1,), (1,)))


def mm_tn(a, b):
    return mm(a, b, ((0,), (0,)))


def orthonormal_rows(wide):
    rank = wide.shape[0]
    inner = mm_nt(wide, wide)
    row_id = lax.broadcasted_iota(jnp.int32, (rank, rank), 0)
    col_id = lax.broadcasted_iota(jnp.int32, (rank, rank), 1)
    eye = (row_id == col_id).astype(jnp.float32)
    work = jnp.concatenate([inner, eye], axis=1)
    rows = lax.broadcasted_iota(jnp.int32, work.shape, 0)
    for k in range(rank - 1):
        factor = work[:, k : k + 1] / work[k : k + 1, k : k + 1]
        work = jnp.where(rows > k, work - factor * work[k : k + 1, :], work)
    diag = jnp.sum(work[:, :rank] * eye, axis=1, keepdims=True)
    inverse = work[:, rank:] * (1.0 / jnp.sqrt(diag))
    return mm_nn(inverse, wide)


def send_field_kernel(order_ref, field_ref, out_ref, *, brick_len):
    species, cells_y, cells_z = field_ref.shape
    lane = lax.broadcasted_iota(jnp.int32, (1, cells_z), 1)
    brick = lane // brick_len
    place = jnp.zeros((1, cells_z), jnp.int32)
    for b in range(cells_z // brick_len):
        place = jnp.where(brick == b, order_ref[b] * brick_len, place)
    grid_z = (place + lane % brick_len).astype(jnp.float32)
    taper = 0.5 + 1.5 * grid_z / (cells_z - 1)
    for s in range(species):
        for j in range(cells_z // LANES):
            cut = slice(j * LANES, (j + 1) * LANES)
            block = field_ref[s, :, cut] * taper[:, cut]
            out_ref[pl.ds(j * LANES * species + s, LANES, stride=species), :] = block.T


def fibre(ref, s, species, rows_x, parts):
    return jnp.concatenate(
        [ref[pl.ds(yq * rows_x * species + s, rows_x, stride=species), :] for yq in range(parts)], axis=1
    )


def gram_first_kernel(data_ref, out_ref, *, species, rows_x, parts):
    total = jnp.zeros(out_ref.shape, jnp.float32)
    for s in range(species):
        cut = fibre(data_ref, s, species, rows_x, parts)
        total = total + mm_nt(cut, cut)
    out_ref[...] = total


def second_kernel(gram_ref, start_ref, data_ref, merged_ref, out_ref, *, species, rows_x, parts):
    gram = gram_ref[...]
    wide = mm_tn(start_ref[...], gram)
    current = orthonormal_rows(wide)
    for repeat in range(ITERS - 1):
        current = orthonormal_rows(mm_nn(current, gram))
    rank = current.shape[0]
    for s in range(species):
        cut = fibre(data_ref, s, species, rows_x, parts)
        merged_ref[s * rank : (s + 1) * rank, :] = mm_nn(current, cut)
    merged = merged_ref[...]
    flipped = merged.T
    for j in range(parts):
        cut = slice(j * LANES, (j + 1) * LANES)
        out_ref[pl.ds(j, flipped.shape[0], stride=parts), :] = mm_nn(flipped, merged[:, cut])


def third_kernel(gram_ref, start_ref, merged_ref, out_ref, *, parts, copies):
    size = gram_ref.shape[0] // parts
    gram = jnp.concatenate([gram_ref[pl.ds(j, size, stride=parts), :] for j in range(parts)], axis=1)
    current = orthonormal_rows(mm_tn(start_ref[...], gram))
    for repeat in range(ITERS - 1):
        current = orthonormal_rows(mm_nn(current, gram))
    after = mm_nt(current, merged_ref[...])
    rank = after.shape[0]
    for i in range(copies):
        out_ref[i * rank : (i + 1) * rank, :] = after


def columns_of(ref, parts):
    size = ref.shape[0] // parts
    return jnp.concatenate([ref[pl.ds(q, size, stride=parts), :] for q in range(parts)], axis=1)


def spread(out_ref, wide):
    for i in range(out_ref.shape[0]):
        out_ref[i] = wide


def start_third_kernel(order_ref, start_ref, data_ref, out_ref, placed_ref, *, brick_len, parts):
    for b in range(start_ref.shape[0] // brick_len):
        at = pl.multiple_of(order_ref[b] * brick_len, brick_len)
        placed_ref[b * brick_len : (b + 1) * brick_len, :] = start_ref[pl.ds(at, brick_len), :]
    data = columns_of(data_ref, parts)
    spread(out_ref, mm_nt(mm_tn(placed_ref[...], data), data))


def total_of(parts_ref):
    total = parts_ref[0]
    for i in range(1, parts_ref.shape[0]):
        total = total + parts_ref[i]
    return total


def step_third_kernel(parts_ref, data_ref, out_ref, *, parts):
    current = orthonormal_rows(total_of(parts_ref))
    data = columns_of(data_ref, parts)
    spread(out_ref, mm_nt(mm_nn(current, data), data))


def core_kernel(at_ref, parts_ref, data_ref, out_ref, rows_ref, *, parts):
    current = orthonormal_rows(total_of(parts_ref))
    size = data_ref.shape[0] // parts
    count = out_ref.shape[0]
    for q in range(parts):
        data = data_ref[pl.ds(q, size, stride=parts), :]
        rows_ref[...] = mm_nn(current, data).T
        out_ref[:, q, :] = rows_ref[pl.ds(at_ref[0] * count, count), :]


def call(kernel, out_shape, *args, scratch=(), scalars=0):
    vmem = pl.BlockSpec(memory_space=pltpu.VMEM)
    smem = pl.BlockSpec(memory_space=pltpu.SMEM)
    return pl.pallas_call(
        kernel,
        out_shape=out_shape,
        in_specs=[smem] * scalars + [vmem] * (len(args) - scalars),
        out_specs=jax.tree.map(lambda _: vmem, out_shape),
        scratch_shapes=scratch,
    )(*args)


def f32(*shape):
    return jax.ShapeDtypeStruct(shape, jnp.float32)


def swap(pieces, axes):
    return lax.all_to_all(pieces, axes, split_axis=0, concat_axis=0, tiled=True)


def shards(field, brick_order, start_first, start_second, start_third):
    species, rows_here, cells_y, cells_z = field.shape
    count_gx = lax.axis_size("gx")
    count_gy = lax.axis_size("gy")
    count_gz = lax.axis_size("gz")
    devices = count_gx * count_gy * count_gz
    rows_x, rank_one = start_first.shape
    full_y, rank_two = start_second.shape
    rank_three = start_third.shape[1]
    brick_len = cells_z // brick_order.shape[0]
    merged_rows = species * rank_one
    q_here = rank_two // count_gz

    sent = call(
        functools.partial(send_field_kernel, brick_len=brick_len),
        f32(cells_z * species, cells_y),
        brick_order,
        field.reshape(species, cells_y, cells_z),
        scalars=1,
    )
    data = swap(sent.reshape(devices, species, cells_y), ORDER).reshape(devices * species, cells_y)

    gram = call(
        functools.partial(gram_first_kernel, species=species, rows_x=rows_x, parts=count_gy),
        f32(rows_x, rows_x),
        data,
    )
    gram = jnp.sum(swap(gram.reshape(count_gz, rows_x // count_gz, rows_x), "gz"), axis=0)
    others = count_gx * count_gy
    gram = jnp.sum(swap(jnp.broadcast_to(gram, (others,) + gram.shape), ("gx", "gy")), axis=0)
    gram = swap(jnp.broadcast_to(gram, (count_gz,) + gram.shape), "gz").reshape(rows_x, rows_x)

    parts_y = full_y // LANES
    merged, gram = call(
        functools.partial(second_kernel, species=species, rows_x=rows_x, parts=parts_y),
        (f32(merged_rows, full_y), f32(full_y * parts_y, LANES)),
        gram,
        start_first,
        data,
    )
    gram = jnp.sum(swap(gram.reshape(devices, full_y * parts_y // devices, LANES), ORDER), axis=0)
    gram = swap(jnp.broadcast_to(gram, (devices,) + gram.shape), ORDER).reshape(full_y * parts_y, LANES)

    sent = call(
        functools.partial(third_kernel, parts=parts_y, copies=others),
        f32(others * rank_two, merged_rows),
        gram,
        start_second,
        merged,
    )
    data = swap(sent.reshape(devices, q_here, merged_rows), ORDER).reshape(devices * q_here, merged_rows)

    spread_shape = f32(count_gz, rank_three, cells_z)
    pieces = call(
        functools.partial(start_third_kernel, brick_len=brick_len, parts=q_here),
        spread_shape,
        brick_order,
        start_third,
        data,
        scratch=[pltpu.VMEM(start_third.shape, jnp.float32)],
        scalars=1,
    )
    for repeat in range(ITERS - 1):
        pieces = call(functools.partial(step_third_kernel, parts=q_here), spread_shape, swap(pieces, "gz"), data)
    at = (lax.axis_index("gx") * count_gy + lax.axis_index("gy")).astype(jnp.int32).reshape(1)
    return call(
        functools.partial(core_kernel, parts=q_here),
        f32(merged_rows // others, q_here, rank_three),
        at,
        swap(pieces, "gz"),
        data,
        scratch=[pltpu.VMEM((merged_rows, rank_three), jnp.float32)],
        scalars=1,
    )


def solution(mesh):
    in_specs = (P(None, ("gx", "gz"), "gy", None), P(), P(), P(), P())
    out_specs = P(("gx", "gy"), "gz", None)
    return jax.shard_map(shards, mesh=mesh, in_specs=in_specs, out_specs=out_specs, check_vma=False)
```

```python
import functools

import jax
import jax.numpy as jnp
from jax import lax
from jax.experimental import pallas as pl
from jax.experimental.pallas import tpu as pltpu
from jax.sharding import Mesh, PartitionSpec as P

ITERS = 2
LANES = 128
PANEL = 8
FINE = ("gu", "gv", "gh", "gl", "gw", "gc")
CHIPS = ("gh", "gl", "gu", "gv", "gw")
ORDER = CHIPS + ("gc",)
NEAR = ("gl", "gw")
ACROSS = ("gv", "gc")
ALONG = ("gu", "gh", "gl", "gw")

highest = lax.Precision.HIGHEST
NN = ((1,), (0,))
NT = ((1,), (1,))
TN = ((0,), (0,))


def mm(a, b, dims):
    return lax.dot_general(a, b, (dims, ((), ())), precision=highest, preferred_element_type=jnp.float32)


def halves(x):
    high = x.astype(jnp.bfloat16)
    return high, (x - high.astype(jnp.float32)).astype(jnp.bfloat16)


def mm3(a, b, dims):
    def dot(x, y):
        return lax.dot_general(x, y, (dims, ((), ())), preferred_element_type=jnp.float32)

    return dot(a[0], b[0]) + (dot(a[0], b[1]) + dot(a[1], b[0]))


def orthonormal_rows(wide):
    rank = wide.shape[0]
    inner = mm(wide, wide, NT)
    shape = (rank, rank)
    row_id = lax.broadcasted_iota(jnp.int32, shape, 0)
    inverse = (row_id == lax.broadcasted_iota(jnp.int32, shape, 1)).astype(jnp.float32)
    pivots = jnp.ones(shape, jnp.float32)
    for start in range(0, rank, PANEL):
        columns = [jnp.broadcast_to(inner[:, start + j : start + j + 1], shape) for j in range(PANEL)]
        for j in range(PANEL):
            k = start + j
            pivot = jnp.broadcast_to(columns[j][k : k + 1, :], shape)
            pivots = jnp.where(row_id == k, pivot, pivots)
            if k == rank - 1:
                break
            factor = jnp.where(row_id > k, columns[j] * (1.0 / pivot), 0.0)
            for i in range(j + 1, PANEL):
                columns[i] = columns[i] - factor * columns[i][k : k + 1, :]
            if start + PANEL < rank:
                inner = inner - factor * inner[k : k + 1, :]
            inverse = inverse - factor * inverse[k : k + 1, :]
    return mm(inverse * (1.0 / jnp.sqrt(pivots)), wide, NN)


def send_field_kernel(order_ref, field_ref, out_ref, *, brick_len):
    species, cells_y, cells_z = field_ref.shape
    lane = lax.broadcasted_iota(jnp.int32, (1, cells_z), 1)
    brick = lane // brick_len
    place = jnp.zeros((1, cells_z), jnp.int32)
    for b in range(cells_z // brick_len):
        place = jnp.where(brick == b, order_ref[b] * brick_len, place)
    grid_z = (place + lane % brick_len).astype(jnp.float32)
    taper = 0.5 + 1.5 * grid_z / (cells_z - 1)
    for s in range(species):
        for j in range(cells_z // LANES):
            cut = slice(j * LANES, (j + 1) * LANES)
            block = field_ref[s, :, cut] * taper[:, cut]
            out_ref[pl.ds(j * LANES * species + s, LANES, stride=species), :] = block.T


def fibre(ref, s, species, rows_x, parts):
    return jnp.concatenate(
        [ref[pl.ds(yq * rows_x * species + s, rows_x, stride=species), :] for yq in range(parts)], axis=1
    )


def gram_first_kernel(data_ref, out_ref, *, species, rows_x, parts):
    total = jnp.zeros(out_ref.shape, jnp.float32)
    for s in range(species):
        cut = halves(fibre(data_ref, s, species, rows_x, parts))
        total = total + mm3(cut, cut, NT)
    out_ref[...] = total


def second_kernel(gram_ref, start_ref, data_ref, merged_ref, out_ref, rows_ref, *, species, rows_x, parts):
    gram = gram_ref[...]
    current = start_ref[...]
    for repeat in range(ITERS):
        current = orthonormal_rows(mm(current, gram, NN))
    rank = current.shape[0]
    rows_ref[...] = current
    current = halves(jnp.concatenate([rows_ref[pl.ds(i, rank // 4, stride=4), :] for i in range(4)], axis=0))
    half = rank // 2
    for s in range(species):
        product = mm3(current, halves(fibre(data_ref, s, species, rows_x, parts)), NN)
        merged_ref[s * half : (s + 1) * half, :] = product[:half]
        merged_ref[(species + s) * half : (species + s + 1) * half, :] = product[half:]
    merged = merged_ref[...]
    flipped = halves(merged.T)
    merged = halves(merged)
    size = merged_ref.shape[1]
    product = mm3(flipped, merged, NN)
    for j in range(parts):
        out_ref[pl.ds(j, size, stride=parts), :] = product[:, j * LANES : (j + 1) * LANES]


def third_kernel(core_ref, own_ref, other_ref, start_ref, merged_ref, out_ref, gram_ref, rows_ref, *, parts):
    half = own_ref.shape[0]
    core = core_ref[0]
    gram_ref[pl.ds(pl.multiple_of(core * half, half), half), :] = own_ref[...]
    gram_ref[pl.ds(pl.multiple_of((1 - core) * half, half), half), :] = other_ref[...]
    size = gram_ref.shape[0] // parts
    gram = halves(jnp.concatenate([gram_ref[pl.ds(j, size, stride=parts), :] for j in range(parts)], axis=1))
    current = start_ref[...]
    for repeat in range(ITERS):
        current = orthonormal_rows(mm3(halves(current), gram, NN))
    rows_ref[...] = mm(current, merged_ref[...], NT)
    rank = rows_ref.shape[0]
    even = rows_ref[pl.ds(0, rank // 2, stride=2), :]
    odd = rows_ref[pl.ds(1, rank // 2, stride=2), :]
    low = lax.broadcasted_iota(jnp.int32, even.shape, 1) < LANES // 2
    first = jnp.where(low, even, pltpu.roll(odd, LANES // 2, 1))
    second = jnp.where(low, pltpu.roll(even, LANES // 2, 1), odd)
    per_low = out_ref.shape[2]
    for h in range(out_ref.shape[0]):
        for i in range(per_low):
            out_ref[h, 0, i] = first
            out_ref[h, 1, i] = second


def columns_of(own_ref, other_ref, parts):
    size = own_ref.shape[0] // parts
    return jnp.concatenate(
        [
            jnp.concatenate([ref[pl.ds(q, size, stride=parts), :] for q in range(parts)], axis=1)
            for ref in (own_ref, other_ref)
        ],
        axis=0,
    )


def spread(out_ref, wide):
    for i in range(out_ref.shape[0]):
        out_ref[i] = wide


def start_third_kernel(order_ref, core_ref, start_ref, own_ref, other_ref, out_ref, rows_ref, placed_ref, *, brick_len, parts):
    rows_ref[...] = start_ref[...].T
    size = rows_ref.shape[0]
    for b in range(size // brick_len):
        at = pl.multiple_of(order_ref[b] * brick_len, brick_len)
        placed_ref[b * brick_len : (b + 1) * brick_len, :] = rows_ref[pl.ds(at, brick_len), :]
    core = core_ref[0]
    start = jnp.concatenate(
        [placed_ref[pl.ds(core, size // 2, stride=2), :], placed_ref[pl.ds(1 - core, size // 2, stride=2), :]], axis=0
    )
    data = halves(columns_of(own_ref, other_ref, parts))
    inner = mm3(halves(start.T), data, NN)
    spread(out_ref, mm3(halves(inner), data, NT))


def total_of(parts_ref):
    total = parts_ref[0]
    for i in range(1, parts_ref.shape[0]):
        total = total + parts_ref[i]
    return total


def step_third_kernel(parts_ref, own_ref, other_ref, out_ref, *, parts):
    current = orthonormal_rows(total_of(parts_ref))
    data = halves(columns_of(own_ref, other_ref, parts))
    inner = mm3(halves(current), data, NN)
    spread(out_ref, mm3(halves(inner), data, NT))


def core_kernel(core_ref, at_ref, parts_ref, own_ref, other_ref, out_ref, rows_ref, *, parts):
    current = halves(orthonormal_rows(total_of(parts_ref)))
    size = own_ref.shape[0] // parts
    here = parts // 2
    for jj in range(here):
        at = core_ref[0] * here + jj
        data = jnp.concatenate([ref[pl.ds(at, size, stride=parts), :] for ref in (own_ref, other_ref)], axis=0)
        rows_ref[...] = mm3(current, halves(data), NN).T
        for e in range(2):
            for b in range(out_ref.shape[0]):
                out_ref[b, 2 * jj + e, :] = rows_ref[at_ref[0] + e * (LANES // 2) + 8 * b, :]


def call(kernel, out_shape, *args, scratch=(), scalars=0):
    vmem = pl.BlockSpec(memory_space=pltpu.VMEM)
    smem = pl.BlockSpec(memory_space=pltpu.SMEM)
    return pl.pallas_call(
        kernel,
        out_shape=out_shape,
        in_specs=[smem] * scalars + [vmem] * (len(args) - scalars),
        out_specs=jax.tree.map(lambda _: vmem, out_shape),
        scratch_shapes=[pltpu.VMEM(s, jnp.float32) for s in scratch],
    )(*args)


def f32(*shape):
    return jax.ShapeDtypeStruct(shape, jnp.float32)


def swap(pieces, axes):
    return lax.all_to_all(pieces, axes, split_axis=0, concat_axis=0, tiled=True)


def copies(piece, axes):
    return jnp.broadcast_to(piece, (lax.axis_size(axes),) + piece.shape)


def shards(field, brick_order, start_first, start_second, start_third):
    species, rows_here, cells_y, cells_z = field.shape
    rows_x, rank_one = start_first.shape
    full_y, rank_two = start_second.shape
    rank_three = start_third.shape[1]
    brick_len = cells_z // brick_order.shape[0]
    merged_rows = species * rank_one
    devices = lax.axis_size(ORDER)
    chips = lax.axis_size(CHIPS)
    parts_y = full_y // LANES
    core = lax.axis_index("gc").astype(jnp.int32).reshape(1)
    exchange = [(0, 1), (1, 0)]

    sent = call(
        functools.partial(send_field_kernel, brick_len=brick_len),
        f32(cells_z * species, cells_y),
        brick_order,
        field.reshape(species, cells_y, cells_z),
        scalars=1,
    )
    data = swap(sent.reshape(devices, species, cells_y), ORDER).reshape(devices * species, cells_y)

    gram = call(
        functools.partial(gram_first_kernel, species=species, rows_x=rows_x, parts=parts_y), f32(rows_x, rows_x), data
    )
    gram = jnp.sum(swap(gram.reshape(lax.axis_size(ACROSS), -1, rows_x), ACROSS), axis=0)
    gram = jnp.sum(swap(copies(gram, ALONG), ALONG), axis=0)
    gram = swap(copies(gram, ACROSS), ACROSS).reshape(rows_x, rows_x)

    merged, gram = call(
        functools.partial(second_kernel, species=species, rows_x=rows_x, parts=parts_y),
        (f32(merged_rows, full_y), f32(full_y * parts_y, LANES)),
        gram,
        start_first.T,
        data,
        scratch=[(rank_one, rows_x)],
    )
    gram = jnp.sum(swap(gram.reshape(2, -1, LANES), "gc"), axis=0)
    gram = jnp.sum(swap(gram.reshape(chips, -1, LANES), CHIPS), axis=0)
    own = swap(copies(gram, CHIPS), CHIPS).reshape(-1, LANES)
    other = lax.ppermute(own, "gc", exchange)

    near = lax.axis_size("gl")
    row_groups = lax.axis_size("gw") * 4
    sent = call(
        functools.partial(third_kernel, parts=parts_y),
        f32(lax.axis_size("gh"), near, lax.axis_size(("gu", "gv")), row_groups, LANES),
        core,
        own,
        other,
        start_second.T,
        merged,
        scratch=[(full_y * parts_y, LANES), (rank_two, merged_rows)],
        scalars=1,
    )
    own = swap(sent.reshape(chips, 4, LANES), CHIPS).reshape(chips * 4, LANES)
    other = lax.ppermute(own, "gc", exchange)

    spread_shape = f32(lax.axis_size(NEAR), rank_three, cells_z)
    pieces = call(
        functools.partial(start_third_kernel, brick_len=brick_len, parts=4),
        spread_shape,
        brick_order,
        core,
        start_third.T,
        own,
        other,
        scratch=[start_third.shape, start_third.shape],
        scalars=2,
    )
    for repeat in range(ITERS - 1):
        pieces = call(functools.partial(step_third_kernel, parts=4), spread_shape, swap(pieces, NEAR), own, other)
    gx = lax.axis_index(("gu", "gv"))
    at = ((gx // 4) * 16 + (gx % 4) * 2 + lax.axis_index("gh")).astype(jnp.int32).reshape(1)
    return call(
        functools.partial(core_kernel, parts=4),
        f32(2, 4, rank_three),
        core,
        at,
        swap(pieces, NEAR),
        own,
        other,
        scratch=[(merged_rows, rank_three)],
        scalars=2,
    )


def solution(mesh):
    gx, gy, gz = mesh.devices.shape
    fine = Mesh(mesh.devices.reshape(2, gx // 2, 2, gy // 2, gz // 2, 2), FINE)
    in_specs = (P(None, ("gu", "gv", "gw", "gc"), ("gh", "gl"), None), P(), P(), P(), P())
    out_specs = P(("gu", "gv", "gh", "gl"), ("gw", "gc"), None)
    return jax.shard_map(shards, mesh=fine, in_specs=in_specs, out_specs=out_specs, check_vma=False)
```

```python
import functools

import jax
import jax.numpy as jnp
from jax import lax
from jax.experimental import pallas as pl
from jax.experimental.pallas import tpu as pltpu
from jax.sharding import Mesh, PartitionSpec as P

ITERS = 2
LANES = 128
PANEL = 8
VMEM_BYTES = 20 << 20
FINE = ("gu", "gv", "gh", "gl", "gw", "gc")
CHIPS = ("gh", "gl", "gu", "gv", "gw")
ORDER = CHIPS + ("gc",)
NEAR = ("gl", "gw")
ACROSS = ("gv", "gc")
ALONG = ("gu", "gh", "gl", "gw")
FAR = ("gh", "gu", "gv")

highest = lax.Precision.HIGHEST
NN = ((1,), (0,))
NT = ((1,), (1,))
TN = ((0,), (0,))


def mm(a, b, dims):
    return lax.dot_general(a, b, (dims, ((), ())), precision=highest, preferred_element_type=jnp.float32)


def halves(x):
    high = x.astype(jnp.bfloat16)
    return high, (x - high.astype(jnp.float32)).astype(jnp.bfloat16)


def mm3(a, b, dims):
    def dot(x, y):
        return lax.dot_general(x, y, (dims, ((), ())), preferred_element_type=jnp.float32)

    return dot(a[0], b[0]) + (dot(a[0], b[1]) + dot(a[1], b[0]))


def orthonormal_rows(wide):
    rank = wide.shape[0]
    inner = mm(wide, wide, NT)
    shape = (rank, rank)
    row_id = lax.broadcasted_iota(jnp.int32, shape, 0)
    inverse = (row_id == lax.broadcasted_iota(jnp.int32, shape, 1)).astype(jnp.float32)
    pivots = jnp.ones(shape, jnp.float32)
    for start in range(0, rank, PANEL):
        columns = [jnp.broadcast_to(inner[:, start + j : start + j + 1], shape) for j in range(PANEL)]
        for j in range(PANEL):
            k = start + j
            pivot = jnp.broadcast_to(columns[j][k : k + 1, :], shape)
            pivots = jnp.where(row_id == k, pivot, pivots)
            if k == rank - 1:
                break
            factor = jnp.where(row_id > k, columns[j] * (1.0 / pivot), 0.0)
            for i in range(j + 1, PANEL):
                columns[i] = columns[i] - factor * columns[i][k : k + 1, :]
            if start + PANEL < rank:
                inner = inner - factor * inner[k : k + 1, :]
            inverse = inverse - factor * inverse[k : k + 1, :]
    return mm(inverse * (1.0 / jnp.sqrt(pivots)), wide, NN)


def send_field_kernel(order_ref, field_hbm, out_ref, field_ref, sems, *, brick_len):
    species, cells_y, cells_z = field_hbm.shape
    loads = [pltpu.make_async_copy(field_hbm.at[s], field_ref.at[s], sems.at[s]) for s in range(species)]
    for load in loads:
        load.start()
    lane = lax.broadcasted_iota(jnp.int32, (1, cells_z), 1)
    brick = lane // brick_len
    place = jnp.zeros((1, cells_z), jnp.int32)
    for b in range(cells_z // brick_len):
        place = jnp.where(brick == b, order_ref[b] * brick_len, place)
    grid_z = (place + lane % brick_len).astype(jnp.float32)
    taper = 0.5 + 1.5 * grid_z / (cells_z - 1)
    for s in range(species):
        loads[s].wait()
        for j in range(cells_z // LANES):
            cut = slice(j * LANES, (j + 1) * LANES)
            block = field_ref[s, :, cut] * taper[:, cut]
            out_ref[pl.ds(j * LANES * species + s, LANES, stride=species), :] = block.T


def fibre(ref, s, species, rows_x, parts):
    return jnp.concatenate(
        [ref[pl.ds(yq * rows_x * species + s, rows_x, stride=species), :] for yq in range(parts)], axis=1
    )


def gram_first_kernel(data_ref, out_ref, *, species, rows_x, parts):
    total = jnp.zeros(out_ref.shape, jnp.float32)
    for s in range(species):
        cut = halves(fibre(data_ref, s, species, rows_x, parts))
        total = total + mm3(cut, cut, NT)
    out_ref[...] = total


def second_kernel(
    core_ref, gram_ref, start_ref, data_ref, merged_ref, kept_ref, sent_ref, rows_ref, flipped_ref, *, species, rows_x, parts
):
    gram = gram_ref[...]
    current = start_ref[...]
    for repeat in range(ITERS):
        current = orthonormal_rows(mm(current, gram, NN))
    rank = current.shape[0]
    rows_ref[...] = current
    current = halves(jnp.concatenate([rows_ref[pl.ds(i, rank // 4, stride=4), :] for i in range(4)], axis=0))
    half = rank // 2
    for s in range(species):
        product = mm3(current, halves(fibre(data_ref, s, species, rows_x, parts)), NN)
        merged_ref[s * half : (s + 1) * half, :] = product[:half]
        merged_ref[(species + s) * half : (species + s + 1) * half, :] = product[half:]
    merged = merged_ref[...]
    flipped_ref[...] = merged.T
    merged = halves(merged)
    size = merged_ref.shape[1] // 2
    for out_ref, at in ((sent_ref, 1 - core_ref[0]), (kept_ref, core_ref[0])):
        rows = flipped_ref[pl.ds(pl.multiple_of(at * size, size), size), :]
        product = mm3(halves(rows), merged, NN)
        for j in range(parts):
            out_ref[pl.ds(j, size, stride=parts), :] = product[:, j * LANES : (j + 1) * LANES]


def third_kernel(core_ref, own_ref, other_ref, start_ref, merged_ref, out_ref, rows_ref, *, parts):
    gram = halves(columns_of(own_ref, other_ref, parts))
    current = start_ref[...]
    size = current.shape[1] // 2
    for repeat in range(ITERS):
        swapped = jnp.concatenate([current[:, size:], current[:, :size]], axis=1)
        current = jnp.where(core_ref[0] == 0, current, swapped)
        current = orthonormal_rows(mm3(halves(current), gram, NN))
    rows_ref[...] = mm(current, merged_ref[...], NT)
    rank = rows_ref.shape[0]
    even = rows_ref[pl.ds(0, rank // 2, stride=2), :]
    odd = rows_ref[pl.ds(1, rank // 2, stride=2), :]
    low = lax.broadcasted_iota(jnp.int32, even.shape, 1) < LANES // 2
    first = jnp.where(low, even, pltpu.roll(odd, LANES // 2, 1))
    second = jnp.where(low, pltpu.roll(even, LANES // 2, 1), odd)
    per_low = out_ref.shape[2]
    for h in range(out_ref.shape[0]):
        for i in range(per_low):
            out_ref[h, 0, i] = first
            out_ref[h, 1, i] = second


def columns_of(own_ref, other_ref, parts):
    size = own_ref.shape[0] // parts
    return jnp.concatenate(
        [
            jnp.concatenate([ref[pl.ds(q, size, stride=parts), :] for q in range(parts)], axis=1)
            for ref in (own_ref, other_ref)
        ],
        axis=0,
    )


def spread(out_ref, wide):
    for i in range(out_ref.shape[0]):
        out_ref[i] = wide


def start_third_kernel(order_ref, core_ref, start_ref, own_ref, other_ref, out_ref, high_ref, low_ref, rows_ref, placed_ref, *, brick_len, parts):
    rows_ref[...] = start_ref[...].T
    size = rows_ref.shape[0]
    for b in range(size // brick_len):
        at = pl.multiple_of(order_ref[b] * brick_len, brick_len)
        placed_ref[b * brick_len : (b + 1) * brick_len, :] = rows_ref[pl.ds(at, brick_len), :]
    core = core_ref[0]
    start = jnp.concatenate(
        [placed_ref[pl.ds(core, size // 2, stride=2), :], placed_ref[pl.ds(1 - core, size // 2, stride=2), :]], axis=0
    )
    data = halves(columns_of(own_ref, other_ref, parts))
    high_ref[...], low_ref[...] = data
    inner = mm3(halves(start.T), data, NN)
    spread(out_ref, mm3(halves(inner), data, NT))


def total_of(parts_ref):
    total = parts_ref[0]
    for i in range(1, parts_ref.shape[0]):
        total = total + parts_ref[i]
    return total


def step_third_kernel(parts_ref, high_ref, low_ref, out_ref):
    current = orthonormal_rows(total_of(parts_ref))
    data = high_ref[...], low_ref[...]
    inner = mm3(halves(current), data, NN)
    spread(out_ref, mm3(halves(inner), data, NT))


def core_kernel(core_ref, at_ref, parts_ref, high_ref, low_ref, out_ref, rows_ref, *, parts):
    current = halves(orthonormal_rows(total_of(parts_ref)))
    here = parts // 2
    for jj in range(here):
        cut = pl.ds(pl.multiple_of((core_ref[0] * here + jj) * LANES, LANES), LANES)
        rows_ref[...] = mm3(current, (high_ref[:, cut], low_ref[:, cut]), NN).T
        for e in range(2):
            for b in range(out_ref.shape[0]):
                out_ref[b, 2 * jj + e, :] = rows_ref[at_ref[0] + e * (LANES // 2) + 8 * b, :]


def call(kernel, out_shape, *args, scratch=(), scalars=0, in_hbm=0):
    vmem = pl.BlockSpec(memory_space=pltpu.VMEM)
    smem = pl.BlockSpec(memory_space=pltpu.SMEM)
    hbm = pl.BlockSpec(memory_space=pltpu.HBM)
    lead = scalars + in_hbm
    return pl.pallas_call(
        kernel,
        out_shape=out_shape,
        in_specs=[smem] * scalars + [hbm] * in_hbm + [vmem] * (len(args) - lead),
        out_specs=jax.tree.map(lambda _: vmem, out_shape),
        compiler_params=pltpu.CompilerParams(vmem_limit_bytes=None if in_hbm else VMEM_BYTES),
        scratch_shapes=[pltpu.VMEM(s, jnp.float32) if isinstance(s, tuple) else s for s in scratch],
    )(*args[:lead], *[pltpu.with_memory_space_constraint(a, pltpu.VMEM) for a in args[lead:]])


def vm(*shape, dtype=jnp.float32):
    return pltpu.VMEM(shape, dtype)


def swap(pieces, axes):
    return lax.all_to_all(pieces, axes, split_axis=0, concat_axis=0, tiled=True)


def copies(piece, axes):
    return jnp.broadcast_to(piece, (lax.axis_size(axes),) + piece.shape)


def shards(field, brick_order, start_first, start_second, start_third):
    species, rows_here, cells_y, cells_z = field.shape
    rows_x, rank_one = start_first.shape
    full_y, rank_two = start_second.shape
    rank_three = start_third.shape[1]
    brick_len = cells_z // brick_order.shape[0]
    merged_rows = species * rank_one
    devices = lax.axis_size(ORDER)
    chips = lax.axis_size(CHIPS)
    parts_y = full_y // LANES
    core = lax.axis_index("gc").astype(jnp.int32).reshape(1)
    exchange = [(0, 1), (1, 0)]

    sent = call(
        functools.partial(send_field_kernel, brick_len=brick_len),
        vm(cells_z * species, cells_y),
        brick_order,
        field.reshape(species, cells_y, cells_z),
        scratch=[(species, cells_y, cells_z), pltpu.SemaphoreType.DMA((species,))],
        scalars=1,
        in_hbm=1,
    )
    data = swap(sent.reshape(devices, species, cells_y), ORDER).reshape(devices * species, cells_y)

    gram = call(
        functools.partial(gram_first_kernel, species=species, rows_x=rows_x, parts=parts_y), vm(rows_x, rows_x), data
    )
    gram = jnp.sum(swap(gram.reshape(lax.axis_size(ACROSS), -1, rows_x), ACROSS), axis=0)
    gram = jnp.sum(swap(copies(gram, ALONG), ALONG), axis=0)
    gram = swap(copies(gram, ACROSS), ACROSS).reshape(rows_x, rows_x)

    merged, kept, sent = call(
        functools.partial(second_kernel, species=species, rows_x=rows_x, parts=parts_y),
        (vm(merged_rows, full_y),) + (vm(full_y * parts_y // 2, LANES),) * 2,
        core,
        gram,
        start_first.T,
        data,
        scratch=[(rank_one, rows_x), (full_y, merged_rows)],
        scalars=1,
    )
    gram = kept + lax.ppermute(sent, "gc", exchange)
    gram = jnp.sum(swap(gram.reshape(lax.axis_size(NEAR), -1, LANES), NEAR), axis=0)
    gram = jnp.sum(swap(gram.reshape(lax.axis_size(FAR), -1, LANES), FAR), axis=0)
    gram = swap(copies(gram, FAR), FAR).reshape(-1, LANES)
    own = swap(copies(gram, NEAR), NEAR).reshape(-1, LANES)
    other = lax.ppermute(own, "gc", exchange)

    near = lax.axis_size("gl")
    row_groups = lax.axis_size("gw") * 4
    sent = call(
        functools.partial(third_kernel, parts=parts_y),
        vm(lax.axis_size("gh"), near, lax.axis_size(("gu", "gv")), row_groups, LANES),
        core,
        own,
        other,
        start_second.T,
        merged,
        scratch=[(rank_two, merged_rows)],
        scalars=1,
    )
    own = swap(sent.reshape(chips, 4, LANES), CHIPS).reshape(chips * 4, LANES)
    other = lax.ppermute(own, "gc", exchange)

    spread_shape = vm(lax.axis_size(NEAR), rank_three, cells_z)
    cut = vm(cells_z, 4 * LANES, dtype=jnp.bfloat16)
    pieces, high, low = call(
        functools.partial(start_third_kernel, brick_len=brick_len, parts=4),
        (spread_shape, cut, cut),
        brick_order,
        core,
        start_third.T,
        own,
        other,
        scratch=[start_third.shape, start_third.shape],
        scalars=2,
    )
    for repeat in range(ITERS - 1):
        pieces = call(step_third_kernel, spread_shape, swap(pieces, NEAR), high, low)
    gx = lax.axis_index(("gu", "gv"))
    at = ((gx // 4) * 16 + (gx % 4) * 2 + lax.axis_index("gh")).astype(jnp.int32).reshape(1)
    return call(
        functools.partial(core_kernel, parts=4),
        jax.ShapeDtypeStruct((2, 4, rank_three), jnp.float32),
        core,
        at,
        swap(pieces, NEAR),
        high,
        low,
        scratch=[(merged_rows, rank_three)],
        scalars=2,
    )


def solution(mesh):
    gx, gy, gz = mesh.devices.shape
    fine = Mesh(mesh.devices.reshape(2, gx // 2, 2, gy // 2, gz // 2, 2), FINE)
    in_specs = (P(None, ("gu", "gv", "gw", "gc"), ("gh", "gl"), None), P(), P(), P(), P())
    out_specs = P(("gu", "gv", "gh", "gl"), ("gw", "gc"), None)
    return jax.shard_map(shards, mesh=fine, in_specs=in_specs, out_specs=out_specs, check_vma=False)
```

```python
import functools

import jax
import jax.numpy as jnp
from jax import lax
from jax.experimental import pallas as pl
from jax.experimental.pallas import tpu as pltpu
from jax.sharding import Mesh, PartitionSpec as P

ITERS = 2
LANES = 128
PANEL = 8
VMEM_BYTES = 20 << 20
FINE = ("gu", "gv", "gh", "gl", "gw", "gc")
CHIPS = ("gh", "gl", "gu", "gv", "gw")
ORDER = CHIPS + ("gc",)
NEAR = ("gl", "gw")
CLOSE = ("gl", "gw", "gc")
FAR = ("gh", "gu", "gv")
PLANE = ("gw", "gv")
RING = ("gu", "gh", "gl")

highest = lax.Precision.HIGHEST
NN = ((1,), (0,))
NT = ((1,), (1,))
TN = ((0,), (0,))


def mm(a, b, dims):
    return lax.dot_general(a, b, (dims, ((), ())), precision=highest, preferred_element_type=jnp.float32)


def halves(x):
    high = x.astype(jnp.bfloat16)
    return high, (x - high.astype(jnp.float32)).astype(jnp.bfloat16)


def mm3(a, b, dims):
    def dot(x, y):
        return lax.dot_general(x, y, (dims, ((), ())), preferred_element_type=jnp.float32)

    return dot(a[0], b[0]) + (dot(a[0], b[1]) + dot(a[1], b[0]))


def orthonormal_rows(wide):
    rank = wide.shape[0]
    inner = mm(wide, wide, NT)
    shape = (rank, rank)
    row_id = lax.broadcasted_iota(jnp.int32, shape, 0)
    inverse = (row_id == lax.broadcasted_iota(jnp.int32, shape, 1)).astype(jnp.float32)
    pivots = jnp.ones(shape, jnp.float32)
    for start in range(0, rank, PANEL):
        columns = [jnp.broadcast_to(inner[:, start + j : start + j + 1], shape) for j in range(PANEL)]
        for j in range(PANEL):
            k = start + j
            pivot = jnp.broadcast_to(columns[j][k : k + 1, :], shape)
            pivots = jnp.where(row_id == k, pivot, pivots)
            if k == rank - 1:
                break
            factor = jnp.where(row_id > k, columns[j] * (1.0 / pivot), 0.0)
            for i in range(j + 1, PANEL):
                columns[i] = columns[i] - factor * columns[i][k : k + 1, :]
            if start + PANEL < rank:
                inner = inner - factor * inner[k : k + 1, :]
            inverse = inverse - factor * inverse[k : k + 1, :]
    return mm(inverse * (1.0 / jnp.sqrt(pivots)), wide, NN)


def send_field_kernel(order_ref, field_hbm, out_ref, field_ref, sems, *, brick_len):
    species, cells_y, cells_z = field_hbm.shape
    loads = [pltpu.make_async_copy(field_hbm.at[s], field_ref.at[s], sems.at[s]) for s in range(species)]
    for load in loads:
        load.start()
    lane = lax.broadcasted_iota(jnp.int32, (1, cells_z), 1)
    brick = lane // brick_len
    place = jnp.zeros((1, cells_z), jnp.int32)
    for b in range(cells_z // brick_len):
        place = jnp.where(brick == b, order_ref[b] * brick_len, place)
    grid_z = (place + lane % brick_len).astype(jnp.float32)
    taper = 0.5 + 1.5 * grid_z / (cells_z - 1)
    for s in range(species):
        loads[s].wait()
        for j in range(cells_z // LANES):
            cut = slice(j * LANES, (j + 1) * LANES)
            block = field_ref[s, :, cut] * taper[:, cut]
            out_ref[pl.ds(j * LANES * species + s, LANES, stride=species), :] = block.T


def fibre(ref, s, species, rows_x, parts):
    return jnp.concatenate(
        [ref[pl.ds(yq * rows_x * species + s, rows_x, stride=species), :] for yq in range(parts)], axis=1
    )


def gram_first_kernel(data_ref, out_ref, *, species, rows_x, parts):
    total = jnp.zeros(out_ref.shape, jnp.float32)
    for s in range(species):
        cut = halves(fibre(data_ref, s, species, rows_x, parts))
        total = total + mm3(cut, cut, NT)
    out_ref[...] = total


def second_kernel(
    core_ref, gram_ref, start_ref, data_ref, merged_ref, kept_ref, sent_ref, rows_ref, *, species, rows_x, parts
):
    gram = gram_ref[...]
    current = start_ref[...]
    for repeat in range(ITERS):
        current = orthonormal_rows(mm(current, gram, NN))
    rank = current.shape[0]
    rows_ref[...] = current
    current = halves(jnp.concatenate([rows_ref[pl.ds(i, rank // 4, stride=4), :] for i in range(4)], axis=0))
    half = rank // 2
    for s in range(species):
        product = mm3(current, halves(fibre(data_ref, s, species, rows_x, parts)), NN)
        merged_ref[s * half : (s + 1) * half, :] = product[:half]
        merged_ref[(species + s) * half : (species + s + 1) * half, :] = product[half:]
    merged = merged_ref[...]
    flipped = halves(merged.T)
    merged = halves(merged)
    blocks = []
    for i in range(parts):
        cut = slice(i * LANES, (i + 1) * LANES)
        product = mm3([x[cut] for x in flipped], [x[:, i * LANES :] for x in merged], NN)
        blocks += [product[:, j * LANES : (j + 1) * LANES] for j in range(parts - i)]
    count = len(blocks) // 2
    for i in range(count):
        rows = slice(i * LANES, (i + 1) * LANES)
        kept_ref[rows, :] = jnp.where(core_ref[0] == 0, blocks[i], blocks[count + i])
        sent_ref[rows, :] = jnp.where(core_ref[0] == 0, blocks[count + i], blocks[i])


def symmetric_of(core, own_ref, other_ref, parts):
    pairs = (own_ref, other_ref), (other_ref, own_ref)
    blocks = []
    for first, second in pairs:
        for i in range(own_ref.shape[0] // LANES):
            rows = slice(i * LANES, (i + 1) * LANES)
            blocks.append(jnp.where(core == 0, first[rows, :], second[rows, :]))
    upper = {}
    for i in range(parts):
        for j in range(i, parts):
            upper[i, j] = blocks[len(upper)]
    lines = [[upper[i, j] if i <= j else upper[j, i].T for j in range(parts)] for i in range(parts)]
    return jnp.concatenate([jnp.concatenate(line, axis=1) for line in lines], axis=0)


def third_kernel(core_ref, own_ref, other_ref, start_ref, merged_ref, out_ref, rows_ref, *, parts):
    gram = halves(symmetric_of(core_ref[0], own_ref, other_ref, parts))
    current = start_ref[...]
    for repeat in range(ITERS):
        current = orthonormal_rows(mm3(halves(current), gram, NN))
    rows_ref[...] = mm(current, merged_ref[...], NT)
    rank = rows_ref.shape[0]
    even = rows_ref[pl.ds(0, rank // 2, stride=2), :]
    odd = rows_ref[pl.ds(1, rank // 2, stride=2), :]
    low = lax.broadcasted_iota(jnp.int32, even.shape, 1) < LANES // 2
    first = jnp.where(low, even, pltpu.roll(odd, LANES // 2, 1))
    second = jnp.where(low, pltpu.roll(even, LANES // 2, 1), odd)
    per_low = out_ref.shape[2]
    for h in range(out_ref.shape[0]):
        for i in range(per_low):
            out_ref[h, 0, i] = first
            out_ref[h, 1, i] = second


def columns_of(own_ref, other_ref, parts):
    size = own_ref.shape[0] // parts
    return jnp.concatenate(
        [
            jnp.concatenate([ref[pl.ds(q, size, stride=parts), :] for q in range(parts)], axis=1)
            for ref in (own_ref, other_ref)
        ],
        axis=0,
    )


def spread(out_ref, wide):
    for i in range(out_ref.shape[0]):
        out_ref[i] = wide


def start_third_kernel(order_ref, core_ref, start_ref, own_ref, other_ref, out_ref, high_ref, low_ref, rows_ref, placed_ref, *, brick_len, parts):
    rows_ref[...] = start_ref[...].T
    size = rows_ref.shape[0]
    for b in range(size // brick_len):
        at = pl.multiple_of(order_ref[b] * brick_len, brick_len)
        placed_ref[b * brick_len : (b + 1) * brick_len, :] = rows_ref[pl.ds(at, brick_len), :]
    core = core_ref[0]
    start = jnp.concatenate(
        [placed_ref[pl.ds(core, size // 2, stride=2), :], placed_ref[pl.ds(1 - core, size // 2, stride=2), :]], axis=0
    )
    data = halves(columns_of(own_ref, other_ref, parts))
    high_ref[...], low_ref[...] = data
    inner = mm3(halves(start.T), data, NN)
    spread(out_ref, mm3(halves(inner), data, NT))


def total_of(parts_ref):
    total = parts_ref[0]
    for i in range(1, parts_ref.shape[0]):
        total = total + parts_ref[i]
    return total


def step_third_kernel(parts_ref, high_ref, low_ref, out_ref):
    current = orthonormal_rows(total_of(parts_ref))
    data = high_ref[...], low_ref[...]
    inner = mm3(halves(current), data, NN)
    spread(out_ref, mm3(halves(inner), data, NT))


def core_kernel(core_ref, at_ref, parts_ref, high_ref, low_ref, out_ref, rows_ref, *, parts):
    current = halves(orthonormal_rows(total_of(parts_ref)))
    here = parts // 2
    for jj in range(here):
        cut = pl.ds(pl.multiple_of((core_ref[0] * here + jj) * LANES, LANES), LANES)
        rows_ref[...] = mm3(current, (high_ref[:, cut], low_ref[:, cut]), NN).T
        for e in range(2):
            for b in range(out_ref.shape[0]):
                out_ref[b, 2 * jj + e, :] = rows_ref[at_ref[0] + e * (LANES // 2) + 8 * b, :]


def call(kernel, out_shape, *args, scratch=(), scalars=0, in_hbm=0):
    vmem = pl.BlockSpec(memory_space=pltpu.VMEM)
    smem = pl.BlockSpec(memory_space=pltpu.SMEM)
    hbm = pl.BlockSpec(memory_space=pltpu.HBM)
    lead = scalars + in_hbm
    return pl.pallas_call(
        kernel,
        out_shape=out_shape,
        in_specs=[smem] * scalars + [hbm] * in_hbm + [vmem] * (len(args) - lead),
        out_specs=jax.tree.map(lambda _: vmem, out_shape),
        compiler_params=pltpu.CompilerParams(vmem_limit_bytes=None if in_hbm else VMEM_BYTES),
        scratch_shapes=[pltpu.VMEM(s, jnp.float32) if isinstance(s, tuple) else s for s in scratch],
    )(*args[:lead], *[pltpu.with_memory_space_constraint(a, pltpu.VMEM) for a in args[lead:]])


def vm(*shape, dtype=jnp.float32):
    return pltpu.VMEM(shape, dtype)


def swap(pieces, axes):
    return lax.all_to_all(pieces, axes, split_axis=0, concat_axis=0, tiled=True)


def copies(piece, axes):
    return jnp.broadcast_to(piece, (lax.axis_size(axes),) + piece.shape)


def shards(field, brick_order, start_first, start_second, start_third):
    species, rows_here, cells_y, cells_z = field.shape
    rows_x, rank_one = start_first.shape
    full_y, rank_two = start_second.shape
    rank_three = start_third.shape[1]
    brick_len = cells_z // brick_order.shape[0]
    merged_rows = species * rank_one
    devices = lax.axis_size(ORDER)
    chips = lax.axis_size(CHIPS)
    parts_y = full_y // LANES
    core = lax.axis_index("gc").astype(jnp.int32).reshape(1)
    exchange = [(0, 1), (1, 0)]

    sent = call(
        functools.partial(send_field_kernel, brick_len=brick_len),
        vm(cells_z * species, cells_y),
        brick_order,
        field.reshape(species, cells_y, cells_z),
        scratch=[(species, cells_y, cells_z), pltpu.SemaphoreType.DMA((species,))],
        scalars=1,
        in_hbm=1,
    )
    data = swap(sent.reshape(devices, species, cells_y), ORDER).reshape(devices * species, cells_y)

    gram = call(
        functools.partial(gram_first_kernel, species=species, rows_x=rows_x, parts=parts_y), vm(rows_x, rows_x), data
    )
    gram = jnp.sum(swap(gram.reshape(lax.axis_size(CLOSE), -1, rows_x), CLOSE), axis=0)
    gram = jnp.sum(swap(copies(gram, FAR), FAR), axis=0)
    gram = swap(copies(gram, CLOSE), CLOSE).reshape(rows_x, rows_x)

    merged, kept, sent = call(
        functools.partial(second_kernel, species=species, rows_x=rows_x, parts=parts_y),
        (vm(merged_rows, full_y),) + (vm(parts_y * (parts_y + 1) // 4 * LANES, LANES),) * 2,
        core,
        gram,
        start_first.T,
        data,
        scratch=[(rank_one, rows_x)],
        scalars=1,
    )
    gram = kept + lax.ppermute(sent, "gc", exchange)
    plane = lax.axis_size(PLANE)
    gram = jnp.sum(swap(gram.reshape(-1, 4, LANES), PLANE).reshape(plane, -1, 4, LANES), axis=0)
    gram = jnp.sum(swap(copies(gram, RING), RING), axis=0)
    own = swap(copies(gram, PLANE).reshape(-1, 4, LANES), PLANE).reshape(-1, LANES)
    other = lax.ppermute(own, "gc", exchange)

    near = lax.axis_size("gl")
    row_groups = lax.axis_size("gw") * 4
    sent = call(
        functools.partial(third_kernel, parts=parts_y),
        vm(lax.axis_size("gh"), near, lax.axis_size(("gu", "gv")), row_groups, LANES),
        core,
        own,
        other,
        start_second.T,
        merged,
        scratch=[(rank_two, merged_rows)],
        scalars=1,
    )
    own = swap(sent.reshape(chips, 4, LANES), CHIPS).reshape(chips * 4, LANES)
    other = lax.ppermute(own, "gc", exchange)

    spread_shape = vm(lax.axis_size(NEAR), rank_three, cells_z)
    cut = vm(cells_z, 4 * LANES, dtype=jnp.bfloat16)
    pieces, high, low = call(
        functools.partial(start_third_kernel, brick_len=brick_len, parts=4),
        (spread_shape, cut, cut),
        brick_order,
        core,
        start_third.T,
        own,
        other,
        scratch=[start_third.shape, start_third.shape],
        scalars=2,
    )
    for repeat in range(ITERS - 1):
        pieces = call(step_third_kernel, spread_shape, swap(pieces, NEAR), high, low)
    gx = lax.axis_index(("gu", "gv"))
    at = ((gx // 4) * 16 + (gx % 4) * 2 + lax.axis_index("gh")).astype(jnp.int32).reshape(1)
    return call(
        functools.partial(core_kernel, parts=4),
        jax.ShapeDtypeStruct((2, 4, rank_three), jnp.float32),
        core,
        at,
        swap(pieces, NEAR),
        high,
        low,
        scratch=[(merged_rows, rank_three)],
        scalars=2,
    )


def solution(mesh):
    gx, gy, gz = mesh.devices.shape
    fine = Mesh(mesh.devices.reshape(2, gx // 2, 2, gy // 2, gz // 2, 2), FINE)
    in_specs = (P(None, ("gu", "gv", "gw", "gc"), ("gh", "gl"), None), P(), P(), P(), P())
    out_specs = P(("gu", "gv", "gh", "gl"), ("gw", "gc"), None)
    return jax.shard_map(shards, mesh=fine, in_specs=in_specs, out_specs=out_specs, check_vma=False)
```

```python
import functools

import jax
import jax.numpy as jnp
from jax import lax
from jax.experimental import pallas as pl
from jax.experimental.pallas import tpu as pltpu
from jax.sharding import Mesh, PartitionSpec as P

ITERS = 2
LANES = 128
PANEL = 16
VMEM_BYTES = 20 << 20
FINE = ("gu", "gv", "gh", "gl", "gw", "gc")
CHIPS = ("gh", "gl", "gu", "gv", "gw")
ORDER = CHIPS + ("gc",)
NEAR = ("gl", "gw")
CLOSE = ("gl", "gw", "gc")
FAR = ("gh", "gu", "gv")
PLANE = ("gw", "gv")
RING = ("gu", "gh", "gl")

highest = lax.Precision.HIGHEST
NN = ((1,), (0,))
NT = ((1,), (1,))
TN = ((0,), (0,))


def mm(a, b, dims):
    return lax.dot_general(a, b, (dims, ((), ())), precision=highest, preferred_element_type=jnp.float32)


def halves(x):
    high = x.astype(jnp.bfloat16)
    return high, (x - high.astype(jnp.float32)).astype(jnp.bfloat16)


def mm3(a, b, dims):
    def dot(x, y):
        return lax.dot_general(x, y, (dims, ((), ())), preferred_element_type=jnp.float32)

    size = a[0].shape[0]
    both = dot(jnp.concatenate(a, axis=0), b[0])
    return both[:size] + (both[size:] + dot(a[0], b[1]))


def orthonormal_rows(wide):
    rank = wide.shape[0]
    inner = mm(wide, wide, NT)
    shape = (rank, rank)
    row_id = lax.broadcasted_iota(jnp.int32, shape, 0)
    inverse = (row_id == lax.broadcasted_iota(jnp.int32, shape, 1)).astype(jnp.float32)
    pivots = jnp.ones(shape, jnp.float32)
    for start in range(0, rank, PANEL):
        columns = [jnp.broadcast_to(inner[:, start + j : start + j + 1], shape) for j in range(PANEL)]
        for j in range(PANEL):
            k = start + j
            pivot = jnp.broadcast_to(columns[j][k : k + 1, :], shape)
            pivots = jnp.where(row_id == k, pivot, pivots)
            if k == rank - 1:
                break
            factor = jnp.where(row_id > k, columns[j] * (1.0 / pivot), 0.0)
            for i in range(j + 1, PANEL):
                columns[i] = columns[i] - factor * columns[i][k : k + 1, :]
            if start + PANEL < rank:
                inner = inner - factor * inner[k : k + 1, :]
            inverse = inverse - factor * inverse[k : k + 1, :]
    return mm(inverse * (1.0 / jnp.sqrt(pivots)), wide, NN)


def send_field_kernel(
    order_ref, core_ref, field_hbm, first_hbm, second_hbm, third_hbm, out_ref, first_ref, second_ref, third_ref, field_ref,
    raw_ref, rows_ref, placed_ref, sems, start_sems, *, brick_len
):
    species, cells_y, cells_z = field_hbm.shape
    loads = [pltpu.make_async_copy(field_hbm.at[s], field_ref.at[s], sems.at[s]) for s in range(species)]
    pairs = (third_hbm, raw_ref), (second_hbm, second_ref), (first_hbm, first_ref)
    starts = [pltpu.make_async_copy(source, target, start_sems.at[i]) for i, (source, target) in enumerate(pairs)]
    for load in starts[:1] + loads + starts[1:]:
        load.start()
    lane = lax.broadcasted_iota(jnp.int32, (1, cells_z), 1)
    brick = lane // brick_len
    place = jnp.zeros((1, cells_z), jnp.int32)
    for b in range(cells_z // brick_len):
        place = jnp.where(brick == b, order_ref[b] * brick_len, place)
    grid_z = (place + lane % brick_len).astype(jnp.float32)
    taper = 0.5 + 1.5 * grid_z / (cells_z - 1)
    starts[0].wait()
    rows_ref[...] = raw_ref[...].T
    for b in range(cells_z // brick_len):
        at = pl.multiple_of(order_ref[b] * brick_len, brick_len)
        placed_ref[b * brick_len : (b + 1) * brick_len, :] = rows_ref[pl.ds(at, brick_len), :]
    core = core_ref[0]
    half = cells_z // 2
    third_ref[:, :half] = placed_ref[pl.ds(core, half, stride=2), :].T
    third_ref[:, half:] = placed_ref[pl.ds(1 - core, half, stride=2), :].T
    for s in range(species):
        loads[s].wait()
        for j in range(cells_z // LANES):
            cut = slice(j * LANES, (j + 1) * LANES)
            block = field_ref[s, :, cut] * taper[:, cut]
            out_ref[pl.ds(j * LANES * species + s, LANES, stride=species), :] = block.T
    for load in starts[1:]:
        load.wait()


def fibre(ref, s, species, rows_x, parts):
    return jnp.concatenate(
        [ref[pl.ds(yq * rows_x * species + s, rows_x, stride=species), :] for yq in range(parts)], axis=1
    )


def gram_first_kernel(data_ref, out_ref, *, species, rows_x, parts):
    total = jnp.zeros(out_ref.shape, jnp.float32)
    for s in range(species):
        cut = halves(fibre(data_ref, s, species, rows_x, parts))
        total = total + mm3(cut, cut, NT)
    out_ref[...] = total


def second_kernel(
    core_ref, gram_ref, start_ref, data_ref, merged_ref, kept_ref, sent_ref, rows_ref, *, species, rows_x, parts
):
    gram = gram_ref[...]
    current = start_ref[...]
    for repeat in range(ITERS):
        current = orthonormal_rows(mm(current, gram, NN))
    rank = current.shape[0]
    rows_ref[...] = current
    current = halves(jnp.concatenate([rows_ref[pl.ds(i, rank // 4, stride=4), :] for i in range(4)], axis=0))
    half = rank // 2
    for s in range(species):
        product = mm3(current, halves(fibre(data_ref, s, species, rows_x, parts)), NN)
        merged_ref[s * half : (s + 1) * half, :] = product[:half]
        merged_ref[(species + s) * half : (species + s + 1) * half, :] = product[half:]
    merged = merged_ref[...]
    flipped = halves(merged.T)
    merged = halves(merged)
    blocks = []
    for i in range(parts):
        cut = slice(i * LANES, (i + 1) * LANES)
        product = mm3([x[cut] for x in flipped], [x[:, i * LANES :] for x in merged], NN)
        blocks += [product[:, j * LANES : (j + 1) * LANES] for j in range(parts - i)]
    count = len(blocks) // 2
    for i in range(count):
        rows = slice(i * LANES, (i + 1) * LANES)
        kept_ref[rows, :] = jnp.where(core_ref[0] == 0, blocks[i], blocks[count + i])
        sent_ref[rows, :] = jnp.where(core_ref[0] == 0, blocks[count + i], blocks[i])


def symmetric_of(core, own_ref, other_ref, parts):
    pairs = (own_ref, other_ref), (other_ref, own_ref)
    blocks = []
    for first, second in pairs:
        for i in range(own_ref.shape[0] // LANES):
            rows = slice(i * LANES, (i + 1) * LANES)
            blocks.append(jnp.where(core == 0, first[rows, :], second[rows, :]))
    upper = {}
    for i in range(parts):
        for j in range(i, parts):
            upper[i, j] = blocks[len(upper)]
    lines = [[upper[i, j] if i <= j else upper[j, i].T for j in range(parts)] for i in range(parts)]
    return jnp.concatenate([jnp.concatenate(line, axis=1) for line in lines], axis=0)


def third_kernel(core_ref, own_ref, other_ref, start_ref, merged_ref, out_ref, rows_ref, *, parts):
    gram = halves(symmetric_of(core_ref[0], own_ref, other_ref, parts))
    current = start_ref[...]
    for repeat in range(ITERS):
        current = orthonormal_rows(mm3(halves(current), gram, NN))
    rows_ref[...] = mm(current, merged_ref[...], NT)
    rank = rows_ref.shape[0]
    even = rows_ref[pl.ds(0, rank // 2, stride=2), :]
    odd = rows_ref[pl.ds(1, rank // 2, stride=2), :]
    low = lax.broadcasted_iota(jnp.int32, even.shape, 1) < LANES // 2
    first = jnp.where(low, even, pltpu.roll(odd, LANES // 2, 1))
    second = jnp.where(low, pltpu.roll(even, LANES // 2, 1), odd)
    per_low = out_ref.shape[2]
    for h in range(out_ref.shape[0]):
        for i in range(per_low):
            out_ref[h, 0, i] = first
            out_ref[h, 1, i] = second


def columns_of(own_ref, other_ref, parts):
    size = own_ref.shape[0] // parts
    return jnp.concatenate(
        [
            jnp.concatenate([ref[pl.ds(q, size, stride=parts), :] for q in range(parts)], axis=1)
            for ref in (own_ref, other_ref)
        ],
        axis=0,
    )


def spread(out_ref, wide):
    for i in range(out_ref.shape[0]):
        out_ref[i] = wide


def start_third_kernel(start_ref, own_ref, other_ref, out_ref, high_ref, low_ref, *, parts):
    data = halves(columns_of(own_ref, other_ref, parts))
    high_ref[...], low_ref[...] = data
    inner = mm3(halves(start_ref[...]), data, NN)
    spread(out_ref, mm3(halves(inner), data, NT))


def total_of(parts_ref):
    total = parts_ref[0]
    for i in range(1, parts_ref.shape[0]):
        total = total + parts_ref[i]
    return total


def step_third_kernel(parts_ref, high_ref, low_ref, out_ref):
    current = orthonormal_rows(total_of(parts_ref))
    data = high_ref[...], low_ref[...]
    inner = mm3(halves(current), data, NN)
    spread(out_ref, mm3(halves(inner), data, NT))


def core_kernel(core_ref, at_ref, parts_ref, high_ref, low_ref, out_ref, rows_ref, *, parts):
    current = halves(orthonormal_rows(total_of(parts_ref)))
    here = parts // 2
    for jj in range(here):
        cut = pl.ds(pl.multiple_of((core_ref[0] * here + jj) * LANES, LANES), LANES)
        rows_ref[...] = mm3(current, (high_ref[:, cut], low_ref[:, cut]), NN).T
        for e in range(2):
            for b in range(out_ref.shape[0]):
                out_ref[b, 2 * jj + e, :] = rows_ref[at_ref[0] + e * (LANES // 2) + 8 * b, :]


def call(kernel, out_shape, *args, scratch=(), scalars=0, in_hbm=0):
    vmem = pl.BlockSpec(memory_space=pltpu.VMEM)
    smem = pl.BlockSpec(memory_space=pltpu.SMEM)
    hbm = pl.BlockSpec(memory_space=pltpu.HBM)
    lead = scalars + in_hbm
    return pl.pallas_call(
        kernel,
        out_shape=out_shape,
        in_specs=[smem] * scalars + [hbm] * in_hbm + [vmem] * (len(args) - lead),
        out_specs=jax.tree.map(lambda _: vmem, out_shape),
        compiler_params=pltpu.CompilerParams(vmem_limit_bytes=None if in_hbm else VMEM_BYTES),
        scratch_shapes=[pltpu.VMEM(s, jnp.float32) if isinstance(s, tuple) else s for s in scratch],
    )(*args[:lead], *[pltpu.with_memory_space_constraint(a, pltpu.VMEM) for a in args[lead:]])


def vm(*shape, dtype=jnp.float32):
    return pltpu.VMEM(shape, dtype)


def swap(pieces, axes):
    return lax.all_to_all(pieces, axes, split_axis=0, concat_axis=0, tiled=True)


def copies(piece, axes):
    return jnp.broadcast_to(piece, (lax.axis_size(axes),) + piece.shape)


def shards(field, brick_order, start_first, start_second, start_third):
    species, rows_here, cells_y, cells_z = field.shape
    rows_x, rank_one = start_first.shape
    full_y, rank_two = start_second.shape
    rank_three = start_third.shape[1]
    brick_len = cells_z // brick_order.shape[0]
    merged_rows = species * rank_one
    devices = lax.axis_size(ORDER)
    chips = lax.axis_size(CHIPS)
    parts_y = full_y // LANES
    core = lax.axis_index("gc").astype(jnp.int32).reshape(1)
    exchange = [(0, 1), (1, 0)]

    sent, start_first, start_second, start_third = call(
        functools.partial(send_field_kernel, brick_len=brick_len),
        (vm(cells_z * species, cells_y), vm(rank_one, rows_x), vm(rank_two, full_y), vm(rank_three, cells_z)),
        brick_order,
        core,
        field.reshape(species, cells_y, cells_z),
        start_first.T,
        start_second.T,
        start_third.T,
        scratch=[
            (species, cells_y, cells_z),
            (rank_three, cells_z),
            (cells_z, rank_three),
            (cells_z, rank_three),
            pltpu.SemaphoreType.DMA((species,)),
            pltpu.SemaphoreType.DMA((3,)),
        ],
        scalars=2,
        in_hbm=4,
    )
    data = swap(sent.reshape(devices, species, cells_y), ORDER).reshape(devices * species, cells_y)

    gram = call(
        functools.partial(gram_first_kernel, species=species, rows_x=rows_x, parts=parts_y), vm(rows_x, rows_x), data
    )
    gram = jnp.sum(swap(gram.reshape(lax.axis_size(CLOSE), -1, rows_x), CLOSE), axis=0)
    gram = jnp.sum(swap(copies(gram, FAR), FAR), axis=0)
    gram = swap(copies(gram, CLOSE), CLOSE).reshape(rows_x, rows_x)

    merged, kept, sent = call(
        functools.partial(second_kernel, species=species, rows_x=rows_x, parts=parts_y),
        (vm(merged_rows, full_y),) + (vm(parts_y * (parts_y + 1) // 4 * LANES, LANES),) * 2,
        core,
        gram,
        start_first,
        data,
        scratch=[(rank_one, rows_x)],
        scalars=1,
    )
    gram = kept + lax.ppermute(sent, "gc", exchange)
    plane = lax.axis_size(PLANE)
    gram = jnp.sum(swap(gram.reshape(-1, 4, LANES), PLANE).reshape(plane, -1, 4, LANES), axis=0)
    gram = jnp.sum(swap(copies(gram, RING), RING), axis=0)
    own = swap(copies(gram, PLANE).reshape(-1, 4, LANES), PLANE).reshape(-1, LANES)
    other = lax.ppermute(own, "gc", exchange)

    near = lax.axis_size("gl")
    row_groups = lax.axis_size("gw") * 4
    sent = call(
        functools.partial(third_kernel, parts=parts_y),
        vm(lax.axis_size("gh"), near, lax.axis_size(("gu", "gv")), row_groups, LANES),
        core,
        own,
        other,
        start_second,
        merged,
        scratch=[(rank_two, merged_rows)],
        scalars=1,
    )
    own = swap(sent.reshape(chips, 4, LANES), CHIPS).reshape(chips * 4, LANES)
    other = lax.ppermute(own, "gc", exchange)

    spread_shape = vm(lax.axis_size(NEAR), rank_three, cells_z)
    cut = vm(cells_z, 4 * LANES, dtype=jnp.bfloat16)
    pieces, high, low = call(
        functools.partial(start_third_kernel, parts=4),
        (spread_shape, cut, cut),
        start_third,
        own,
        other,
    )
    for repeat in range(ITERS - 1):
        pieces = call(step_third_kernel, spread_shape, swap(pieces, NEAR), high, low)
    gx = lax.axis_index(("gu", "gv"))
    at = ((gx // 4) * 16 + (gx % 4) * 2 + lax.axis_index("gh")).astype(jnp.int32).reshape(1)
    return call(
        functools.partial(core_kernel, parts=4),
        jax.ShapeDtypeStruct((2, 4, rank_three), jnp.float32),
        core,
        at,
        swap(pieces, NEAR),
        high,
        low,
        scratch=[(merged_rows, rank_three)],
        scalars=2,
    )


def solution(mesh):
    gx, gy, gz = mesh.devices.shape
    fine = Mesh(mesh.devices.reshape(2, gx // 2, 2, gy // 2, gz // 2, 2), FINE)
    in_specs = (P(None, ("gu", "gv", "gw", "gc"), ("gh", "gl"), None), P(), P(), P(), P())
    out_specs = P(("gu", "gv", "gh", "gl"), ("gw", "gc"), None)
    return jax.shard_map(shards, mesh=fine, in_specs=in_specs, out_specs=out_specs, check_vma=False)
```

```python
import functools

import jax
import jax.numpy as jnp
from jax import lax
from jax.experimental import pallas as pl
from jax.experimental.pallas import tpu as pltpu
from jax.sharding import Mesh, PartitionSpec as P

ITERS = 2
LANES = 128
PANEL = 16
VMEM_BYTES = 20 << 20
FINE = ("gu", "gv", "gh", "gl", "gw", "gc")
CHIPS = ("gh", "gl", "gu", "gv", "gw")
ORDER = CHIPS + ("gc",)
NEAR = ("gl", "gw")
CLOSE = ("gl", "gw", "gc")
FAR = ("gh", "gu", "gv")
PLANE = ("gu", "gh", "gl", "gw")
RING = ("gv",)

highest = lax.Precision.HIGHEST
NN = ((1,), (0,))
NT = ((1,), (1,))
TN = ((0,), (0,))


def mm(a, b, dims):
    return lax.dot_general(a, b, (dims, ((), ())), precision=highest, preferred_element_type=jnp.float32)


def halves(x):
    high = x.astype(jnp.bfloat16)
    return high, (x - high.astype(jnp.float32)).astype(jnp.bfloat16)


def mm3(a, b, dims):
    def dot(x, y):
        return lax.dot_general(x, y, (dims, ((), ())), preferred_element_type=jnp.float32)

    size = a[0].shape[0]
    both = dot(jnp.concatenate(a, axis=0), b[0])
    return both[:size] + (both[size:] + dot(a[0], b[1]))


def orthonormal_rows(wide):
    rank = wide.shape[0]
    inner = mm(wide, wide, NT)
    shape = (rank, rank)
    row_id = lax.broadcasted_iota(jnp.int32, shape, 0)
    inverse = (row_id == lax.broadcasted_iota(jnp.int32, shape, 1)).astype(jnp.float32)
    pivots = jnp.ones(shape, jnp.float32)
    for start in range(0, rank, PANEL):
        columns = [jnp.broadcast_to(inner[:, start + j : start + j + 1], shape) for j in range(PANEL)]
        for j in range(PANEL):
            k = start + j
            pivot = jnp.broadcast_to(columns[j][k : k + 1, :], shape)
            pivots = jnp.where(row_id == k, pivot, pivots)
            if k == rank - 1:
                break
            factor = jnp.where(row_id > k, columns[j] * (1.0 / pivot), 0.0)
            for i in range(j + 1, PANEL):
                columns[i] = columns[i] - factor * columns[i][k : k + 1, :]
            if start + PANEL < rank:
                inner = inner - factor * inner[k : k + 1, :]
            inverse = inverse - factor * inverse[k : k + 1, :]
    return mm(inverse * (1.0 / jnp.sqrt(pivots)), wide, NN)


def send_field_kernel(
    order_ref, core_ref, field_hbm, first_hbm, second_hbm, third_hbm, out_ref, first_ref, second_ref, third_ref, field_ref,
    raw_ref, rows_ref, placed_ref, sems, start_sems, *, brick_len
):
    species, cells_y, cells_z = field_hbm.shape
    loads = [pltpu.make_async_copy(field_hbm.at[s], field_ref.at[s], sems.at[s]) for s in range(species)]
    pairs = (third_hbm, raw_ref), (second_hbm, second_ref), (first_hbm, first_ref)
    starts = [pltpu.make_async_copy(source, target, start_sems.at[i]) for i, (source, target) in enumerate(pairs)]
    for load in starts[:1] + loads + starts[1:]:
        load.start()
    lane = lax.broadcasted_iota(jnp.int32, (1, cells_z), 1)
    brick = lane // brick_len
    place = jnp.zeros((1, cells_z), jnp.int32)
    for b in range(cells_z // brick_len):
        place = jnp.where(brick == b, order_ref[b] * brick_len, place)
    grid_z = (place + lane % brick_len).astype(jnp.float32)
    taper = 0.5 + 1.5 * grid_z / (cells_z - 1)
    starts[0].wait()
    rows_ref[...] = raw_ref[...].T
    for b in range(cells_z // brick_len):
        at = pl.multiple_of(order_ref[b] * brick_len, brick_len)
        placed_ref[b * brick_len : (b + 1) * brick_len, :] = rows_ref[pl.ds(at, brick_len), :]
    core = core_ref[0]
    half = cells_z // 2
    third_ref[:, :half] = placed_ref[pl.ds(core, half, stride=2), :].T
    third_ref[:, half:] = placed_ref[pl.ds(1 - core, half, stride=2), :].T
    for s in range(species):
        loads[s].wait()
        for j in range(cells_z // LANES):
            cut = slice(j * LANES, (j + 1) * LANES)
            block = field_ref[s, :, cut] * taper[:, cut]
            out_ref[pl.ds(j * LANES * species + s, LANES, stride=species), :] = block.T
    for load in starts[1:]:
        load.wait()


def fibre(ref, s, species, rows_x, parts):
    return jnp.concatenate(
        [ref[pl.ds(yq * rows_x * species + s, rows_x, stride=species), :] for yq in range(parts)], axis=1
    )


def gram_first_kernel(data_ref, out_ref, *, species, rows_x, parts):
    total = jnp.zeros(out_ref.shape, jnp.float32)
    for s in range(species):
        cut = halves(fibre(data_ref, s, species, rows_x, parts))
        total = total + mm3(cut, cut, NT)
    out_ref[...] = total


def second_kernel(
    core_ref, gram_ref, start_ref, data_ref, merged_ref, kept_ref, sent_ref, rows_ref, *, species, rows_x, parts
):
    gram = gram_ref[...]
    current = start_ref[...]
    for repeat in range(ITERS):
        current = orthonormal_rows(mm(current, gram, NN))
    rank = current.shape[0]
    rows_ref[...] = current
    current = halves(jnp.concatenate([rows_ref[pl.ds(i, rank // 4, stride=4), :] for i in range(4)], axis=0))
    half = rank // 2
    for s in range(species):
        product = mm3(current, halves(fibre(data_ref, s, species, rows_x, parts)), NN)
        merged_ref[s * half : (s + 1) * half, :] = product[:half]
        merged_ref[(species + s) * half : (species + s + 1) * half, :] = product[half:]
    merged = merged_ref[...]
    flipped = halves(merged.T)
    merged = halves(merged)
    blocks = []
    for i in range(parts):
        cut = slice(i * LANES, (i + 1) * LANES)
        product = mm3([x[cut] for x in flipped], [x[:, i * LANES :] for x in merged], NN)
        blocks += [product[:, j * LANES : (j + 1) * LANES] for j in range(parts - i)]
    count = len(blocks) // 2
    for i in range(count):
        rows = slice(i * LANES, (i + 1) * LANES)
        kept_ref[rows, :] = jnp.where(core_ref[0] == 0, blocks[i], blocks[count + i])
        sent_ref[rows, :] = jnp.where(core_ref[0] == 0, blocks[count + i], blocks[i])


def symmetric_of(core, own_ref, other_ref, parts):
    pairs = (own_ref, other_ref), (other_ref, own_ref)
    blocks = []
    for first, second in pairs:
        for i in range(own_ref.shape[0] // LANES):
            rows = slice(i * LANES, (i + 1) * LANES)
            blocks.append(jnp.where(core == 0, first[rows, :], second[rows, :]))
    upper = {}
    for i in range(parts):
        for j in range(i, parts):
            upper[i, j] = blocks[len(upper)]
    lines = [[upper[i, j] if i <= j else upper[j, i].T for j in range(parts)] for i in range(parts)]
    return jnp.concatenate([jnp.concatenate(line, axis=1) for line in lines], axis=0)


def third_kernel(core_ref, own_ref, other_ref, start_ref, merged_ref, out_ref, rows_ref, *, parts):
    gram = halves(symmetric_of(core_ref[0], own_ref, other_ref, parts))
    current = start_ref[...]
    for repeat in range(ITERS):
        current = orthonormal_rows(mm3(halves(current), gram, NN))
    rows_ref[...] = mm(current, merged_ref[...], NT)
    rank = rows_ref.shape[0]
    even = rows_ref[pl.ds(0, rank // 2, stride=2), :]
    odd = rows_ref[pl.ds(1, rank // 2, stride=2), :]
    low = lax.broadcasted_iota(jnp.int32, even.shape, 1) < LANES // 2
    first = jnp.where(low, even, pltpu.roll(odd, LANES // 2, 1))
    second = jnp.where(low, pltpu.roll(even, LANES // 2, 1), odd)
    per_low = out_ref.shape[2]
    for h in range(out_ref.shape[0]):
        for i in range(per_low):
            out_ref[h, 0, i] = first
            out_ref[h, 1, i] = second


def columns_of(own_ref, other_ref, parts):
    size = own_ref.shape[0] // parts
    return jnp.concatenate(
        [
            jnp.concatenate([ref[pl.ds(q, size, stride=parts), :] for q in range(parts)], axis=1)
            for ref in (own_ref, other_ref)
        ],
        axis=0,
    )


def spread(out_ref, wide):
    for i in range(out_ref.shape[0]):
        out_ref[i] = wide


def start_third_kernel(start_ref, own_ref, other_ref, out_ref, high_ref, low_ref, *, parts):
    data = halves(columns_of(own_ref, other_ref, parts))
    high_ref[...], low_ref[...] = data
    inner = mm3(halves(start_ref[...]), data, NN)
    spread(out_ref, mm3(halves(inner), data, NT))


def total_of(parts_ref):
    total = parts_ref[0]
    for i in range(1, parts_ref.shape[0]):
        total = total + parts_ref[i]
    return total


def step_third_kernel(parts_ref, high_ref, low_ref, out_ref):
    current = orthonormal_rows(total_of(parts_ref))
    data = high_ref[...], low_ref[...]
    inner = mm3(halves(current), data, NN)
    spread(out_ref, mm3(halves(inner), data, NT))


def core_kernel(core_ref, at_ref, parts_ref, high_ref, low_ref, out_ref, rows_ref, *, parts):
    current = halves(orthonormal_rows(total_of(parts_ref)))
    here = parts // 2
    for jj in range(here):
        cut = pl.ds(pl.multiple_of((core_ref[0] * here + jj) * LANES, LANES), LANES)
        rows_ref[...] = mm3(current, (high_ref[:, cut], low_ref[:, cut]), NN).T
        for e in range(2):
            for b in range(out_ref.shape[0]):
                out_ref[b, 2 * jj + e, :] = rows_ref[at_ref[0] + e * (LANES // 2) + 8 * b, :]


def call(kernel, out_shape, *args, scratch=(), scalars=0, in_hbm=0):
    vmem = pl.BlockSpec(memory_space=pltpu.VMEM)
    smem = pl.BlockSpec(memory_space=pltpu.SMEM)
    hbm = pl.BlockSpec(memory_space=pltpu.HBM)
    lead = scalars + in_hbm
    return pl.pallas_call(
        kernel,
        out_shape=out_shape,
        in_specs=[smem] * scalars + [hbm] * in_hbm + [vmem] * (len(args) - lead),
        out_specs=jax.tree.map(lambda _: vmem, out_shape),
        compiler_params=pltpu.CompilerParams(vmem_limit_bytes=None if in_hbm else VMEM_BYTES),
        scratch_shapes=[pltpu.VMEM(s, jnp.float32) if isinstance(s, tuple) else s for s in scratch],
    )(*args[:lead], *[pltpu.with_memory_space_constraint(a, pltpu.VMEM) for a in args[lead:]])


def vm(*shape, dtype=jnp.float32):
    return pltpu.VMEM(shape, dtype)


def swap(pieces, axes):
    return lax.all_to_all(pieces, axes, split_axis=0, concat_axis=0, tiled=True)


def copies(piece, axes):
    return jnp.broadcast_to(piece, (lax.axis_size(axes),) + piece.shape)


def shards(field, brick_order, start_first, start_second, start_third):
    species, rows_here, cells_y, cells_z = field.shape
    rows_x, rank_one = start_first.shape
    full_y, rank_two = start_second.shape
    rank_three = start_third.shape[1]
    brick_len = cells_z // brick_order.shape[0]
    merged_rows = species * rank_one
    devices = lax.axis_size(ORDER)
    chips = lax.axis_size(CHIPS)
    parts_y = full_y // LANES
    core = lax.axis_index("gc").astype(jnp.int32).reshape(1)
    exchange = [(0, 1), (1, 0)]

    sent, start_first, start_second, start_third = call(
        functools.partial(send_field_kernel, brick_len=brick_len),
        (vm(cells_z * species, cells_y), vm(rank_one, rows_x), vm(rank_two, full_y), vm(rank_three, cells_z)),
        brick_order,
        core,
        field.reshape(species, cells_y, cells_z),
        start_first.T,
        start_second.T,
        start_third.T,
        scratch=[
            (species, cells_y, cells_z),
            (rank_three, cells_z),
            (cells_z, rank_three),
            (cells_z, rank_three),
            pltpu.SemaphoreType.DMA((species,)),
            pltpu.SemaphoreType.DMA((3,)),
        ],
        scalars=2,
        in_hbm=4,
    )
    data = swap(sent.reshape(devices, species, cells_y), ORDER).reshape(devices * species, cells_y)

    gram = call(
        functools.partial(gram_first_kernel, species=species, rows_x=rows_x, parts=parts_y), vm(rows_x, rows_x), data
    )
    gram = jnp.sum(swap(gram.reshape(lax.axis_size(CLOSE), -1, rows_x), CLOSE), axis=0)
    gram = jnp.sum(swap(copies(gram, FAR), FAR), axis=0)
    gram = swap(copies(gram, CLOSE), CLOSE).reshape(rows_x, rows_x)

    merged, kept, sent = call(
        functools.partial(second_kernel, species=species, rows_x=rows_x, parts=parts_y),
        (vm(merged_rows, full_y),) + (vm(parts_y * (parts_y + 1) // 4 * LANES, LANES),) * 2,
        core,
        gram,
        start_first,
        data,
        scratch=[(rank_one, rows_x)],
        scalars=1,
    )
    gram = kept + lax.ppermute(sent, "gc", exchange)
    plane = lax.axis_size(PLANE)
    gram = jnp.sum(swap(gram.reshape(-1, 4, LANES), PLANE).reshape(plane, -1, 4, LANES), axis=0)
    gram = jnp.sum(swap(copies(gram, RING), RING), axis=0)
    own = swap(copies(gram, PLANE).reshape(-1, 4, LANES), PLANE).reshape(-1, LANES)
    other = lax.ppermute(own, "gc", exchange)

    near = lax.axis_size("gl")
    row_groups = lax.axis_size("gw") * 4
    sent = call(
        functools.partial(third_kernel, parts=parts_y),
        vm(lax.axis_size("gh"), near, lax.axis_size(("gu", "gv")), row_groups, LANES),
        core,
        own,
        other,
        start_second,
        merged,
        scratch=[(rank_two, merged_rows)],
        scalars=1,
    )
    own = swap(sent.reshape(chips, 4, LANES), CHIPS).reshape(chips * 4, LANES)
    other = lax.ppermute(own, "gc", exchange)

    spread_shape = vm(lax.axis_size(NEAR), rank_three, cells_z)
    cut = vm(cells_z, 4 * LANES, dtype=jnp.bfloat16)
    pieces, high, low = call(
        functools.partial(start_third_kernel, parts=4),
        (spread_shape, cut, cut),
        start_third,
        own,
        other,
    )
    for repeat in range(ITERS - 1):
        pieces = call(step_third_kernel, spread_shape, swap(pieces, NEAR), high, low)
    gx = lax.axis_index(("gu", "gv"))
    at = ((gx // 4) * 16 + (gx % 4) * 2 + lax.axis_index("gh")).astype(jnp.int32).reshape(1)
    return call(
        functools.partial(core_kernel, parts=4),
        jax.ShapeDtypeStruct((2, 4, rank_three), jnp.float32),
        core,
        at,
        swap(pieces, NEAR),
        high,
        low,
        scratch=[(merged_rows, rank_three)],
        scalars=2,
    )


def solution(mesh):
    gx, gy, gz = mesh.devices.shape
    fine = Mesh(mesh.devices.reshape(2, gx // 2, 2, gy // 2, gz // 2, 2), FINE)
    in_specs = (P(None, ("gu", "gv", "gw", "gc"), ("gh", "gl"), None), P(), P(), P(), P())
    out_specs = P(("gu", "gv", "gh", "gl"), ("gw", "gc"), None)
    return jax.shard_map(shards, mesh=fine, in_specs=in_specs, out_specs=out_specs, check_vma=False)
```

```python
import functools

import jax
import jax.numpy as jnp
from jax import lax
from jax.experimental import pallas as pl
from jax.experimental.pallas import tpu as pltpu
from jax.sharding import Mesh, PartitionSpec as P

ITERS = 2
LANES = 128
PANEL = 16
VMEM_BYTES = 20 << 20
FINE = ("gu", "gv", "gk", "gh", "gl", "gw", "gc")
CHIPS = ("gh", "gl", "gu", "gv", "gk", "gw")
ORDER = CHIPS + ("gc",)
NEAR = ("gl", "gw")
CLOSE = ("gl", "gw", "gc")
FAR = ("gh", "gu", "gv", "gk")
BLOCK = ("gk", "gl", "gw")
BEYOND = ("gu", "gh", "gv")

highest = lax.Precision.HIGHEST
NN = ((1,), (0,))
NT = ((1,), (1,))
TN = ((0,), (0,))


def mm(a, b, dims):
    return lax.dot_general(a, b, (dims, ((), ())), precision=highest, preferred_element_type=jnp.float32)


def halves(x):
    high = x.astype(jnp.bfloat16)
    return high, (x - high.astype(jnp.float32)).astype(jnp.bfloat16)


def mm3(a, b, dims):
    def dot(x, y):
        return lax.dot_general(x, y, (dims, ((), ())), preferred_element_type=jnp.float32)

    size = a[0].shape[0]
    both = dot(jnp.concatenate(a, axis=0), b[0])
    return both[:size] + (both[size:] + dot(a[0], b[1]))


def orthonormal_rows(wide):
    rank = wide.shape[0]
    inner = mm(wide, wide, NT)
    shape = (rank, rank)
    row_id = lax.broadcasted_iota(jnp.int32, shape, 0)
    inverse = (row_id == lax.broadcasted_iota(jnp.int32, shape, 1)).astype(jnp.float32)
    pivots = jnp.ones(shape, jnp.float32)
    for start in range(0, rank, PANEL):
        columns = [jnp.broadcast_to(inner[:, start + j : start + j + 1], shape) for j in range(PANEL)]
        for j in range(PANEL):
            k = start + j
            pivot = jnp.broadcast_to(columns[j][k : k + 1, :], shape)
            pivots = jnp.where(row_id == k, pivot, pivots)
            if k == rank - 1:
                break
            factor = jnp.where(row_id > k, columns[j] * (1.0 / pivot), 0.0)
            for i in range(j + 1, PANEL):
                columns[i] = columns[i] - factor * columns[i][k : k + 1, :]
            if start + PANEL < rank:
                inner = inner - factor * inner[k : k + 1, :]
            inverse = inverse - factor * inverse[k : k + 1, :]
    return mm(inverse * (1.0 / jnp.sqrt(pivots)), wide, NN)


def send_field_kernel(
    order_ref, core_ref, field_hbm, first_hbm, second_hbm, third_hbm, out_ref, first_ref, second_ref, third_ref, field_ref,
    raw_ref, rows_ref, placed_ref, sems, start_sems, *, brick_len
):
    species, cells_y, cells_z = field_hbm.shape
    loads = [pltpu.make_async_copy(field_hbm.at[s], field_ref.at[s], sems.at[s]) for s in range(species)]
    pairs = (third_hbm, raw_ref), (second_hbm, second_ref), (first_hbm, first_ref)
    starts = [pltpu.make_async_copy(source, target, start_sems.at[i]) for i, (source, target) in enumerate(pairs)]
    for load in starts[:1] + loads + starts[1:]:
        load.start()
    lane = lax.broadcasted_iota(jnp.int32, (1, cells_z), 1)
    brick = lane // brick_len
    place = jnp.zeros((1, cells_z), jnp.int32)
    for b in range(cells_z // brick_len):
        place = jnp.where(brick == b, order_ref[b] * brick_len, place)
    grid_z = (place + lane % brick_len).astype(jnp.float32)
    taper = 0.5 + 1.5 * grid_z / (cells_z - 1)
    starts[0].wait()
    rows_ref[...] = raw_ref[...].T
    for b in range(cells_z // brick_len):
        at = pl.multiple_of(order_ref[b] * brick_len, brick_len)
        placed_ref[b * brick_len : (b + 1) * brick_len, :] = rows_ref[pl.ds(at, brick_len), :]
    core = core_ref[0]
    half = cells_z // 2
    third_ref[:, :half] = placed_ref[pl.ds(core, half, stride=2), :].T
    third_ref[:, half:] = placed_ref[pl.ds(1 - core, half, stride=2), :].T
    for s in range(species):
        loads[s].wait()
        for j in range(cells_z // LANES):
            cut = slice(j * LANES, (j + 1) * LANES)
            block = field_ref[s, :, cut] * taper[:, cut]
            out_ref[pl.ds(j * LANES * species + s, LANES, stride=species), :] = block.T
    for load in starts[1:]:
        load.wait()


def fibre(ref, s, species, rows_x, parts):
    return jnp.concatenate(
        [ref[pl.ds(yq * rows_x * species + s, rows_x, stride=species), :] for yq in range(parts)], axis=1
    )


def gram_first_kernel(data_ref, out_ref, *, species, rows_x, parts):
    total = jnp.zeros(out_ref.shape, jnp.float32)
    for s in range(species):
        cut = halves(fibre(data_ref, s, species, rows_x, parts))
        total = total + mm3(cut, cut, NT)
    out_ref[...] = total


def second_kernel(
    core_ref, gram_ref, start_ref, data_ref, merged_ref, kept_ref, sent_ref, rows_ref, *, species, rows_x, parts
):
    gram = gram_ref[...]
    current = start_ref[...]
    for repeat in range(ITERS):
        current = orthonormal_rows(mm(current, gram, NN))
    rank = current.shape[0]
    rows_ref[...] = current
    current = halves(jnp.concatenate([rows_ref[pl.ds(i, rank // 4, stride=4), :] for i in range(4)], axis=0))
    half = rank // 2
    for s in range(species):
        product = mm3(current, halves(fibre(data_ref, s, species, rows_x, parts)), NN)
        merged_ref[s * half : (s + 1) * half, :] = product[:half]
        merged_ref[(species + s) * half : (species + s + 1) * half, :] = product[half:]
    merged = merged_ref[...]
    flipped = halves(merged.T)
    merged = halves(merged)
    blocks = []
    for i in range(parts):
        cut = slice(i * LANES, (i + 1) * LANES)
        product = mm3([x[cut] for x in flipped], [x[:, i * LANES :] for x in merged], NN)
        blocks += [product[:, j * LANES : (j + 1) * LANES] for j in range(parts - i)]
    count = len(blocks) // 2
    for i in range(count):
        rows = slice(i * LANES, (i + 1) * LANES)
        kept_ref[rows, :] = jnp.where(core_ref[0] == 0, blocks[i], blocks[count + i])
        sent_ref[rows, :] = jnp.where(core_ref[0] == 0, blocks[count + i], blocks[i])


def symmetric_of(core, own_ref, other_ref, parts):
    pairs = (own_ref, other_ref), (other_ref, own_ref)
    blocks = []
    for first, second in pairs:
        for i in range(own_ref.shape[0] // LANES):
            rows = slice(i * LANES, (i + 1) * LANES)
            blocks.append(jnp.where(core == 0, first[rows, :], second[rows, :]))
    upper = {}
    for i in range(parts):
        for j in range(i, parts):
            upper[i, j] = blocks[len(upper)]
    lines = [[upper[i, j] if i <= j else upper[j, i].T for j in range(parts)] for i in range(parts)]
    return jnp.concatenate([jnp.concatenate(line, axis=1) for line in lines], axis=0)


def third_kernel(core_ref, own_ref, other_ref, start_ref, merged_ref, out_ref, rows_ref, *, parts):
    gram = halves(symmetric_of(core_ref[0], own_ref, other_ref, parts))
    current = start_ref[...]
    for repeat in range(ITERS):
        current = orthonormal_rows(mm3(halves(current), gram, NN))
    rows_ref[...] = mm(current, merged_ref[...], NT)
    rank = rows_ref.shape[0]
    even = rows_ref[pl.ds(0, rank // 2, stride=2), :]
    odd = rows_ref[pl.ds(1, rank // 2, stride=2), :]
    low = lax.broadcasted_iota(jnp.int32, even.shape, 1) < LANES // 2
    first = jnp.where(low, even, pltpu.roll(odd, LANES // 2, 1))
    second = jnp.where(low, pltpu.roll(even, LANES // 2, 1), odd)
    per_low = out_ref.shape[2]
    for h in range(out_ref.shape[0]):
        for i in range(per_low):
            out_ref[h, 0, i] = first
            out_ref[h, 1, i] = second


def columns_of(own_ref, other_ref, parts):
    size = own_ref.shape[0] // parts
    return jnp.concatenate(
        [
            jnp.concatenate([ref[pl.ds(q, size, stride=parts), :] for q in range(parts)], axis=1)
            for ref in (own_ref, other_ref)
        ],
        axis=0,
    )


def spread(out_ref, wide):
    for i in range(out_ref.shape[0]):
        out_ref[i] = wide


def start_third_kernel(start_ref, own_ref, other_ref, out_ref, high_ref, low_ref, *, parts):
    data = halves(columns_of(own_ref, other_ref, parts))
    high_ref[...], low_ref[...] = data
    inner = mm3(halves(start_ref[...]), data, NN)
    spread(out_ref, mm3(halves(inner), data, NT))


def total_of(parts_ref):
    total = parts_ref[0]
    for i in range(1, parts_ref.shape[0]):
        total = total + parts_ref[i]
    return total


def step_third_kernel(parts_ref, high_ref, low_ref, out_ref):
    current = orthonormal_rows(total_of(parts_ref))
    data = high_ref[...], low_ref[...]
    inner = mm3(halves(current), data, NN)
    spread(out_ref, mm3(halves(inner), data, NT))


def core_kernel(core_ref, at_ref, parts_ref, high_ref, low_ref, out_ref, rows_ref, *, parts):
    current = halves(orthonormal_rows(total_of(parts_ref)))
    here = parts // 2
    for jj in range(here):
        cut = pl.ds(pl.multiple_of((core_ref[0] * here + jj) * LANES, LANES), LANES)
        rows_ref[...] = mm3(current, (high_ref[:, cut], low_ref[:, cut]), NN).T
        for e in range(2):
            for b in range(out_ref.shape[0]):
                out_ref[b, 2 * jj + e, :] = rows_ref[at_ref[0] + e * (LANES // 2) + 8 * b, :]


def call(kernel, out_shape, *args, scratch=(), scalars=0, in_hbm=0):
    vmem = pl.BlockSpec(memory_space=pltpu.VMEM)
    smem = pl.BlockSpec(memory_space=pltpu.SMEM)
    hbm = pl.BlockSpec(memory_space=pltpu.HBM)
    lead = scalars + in_hbm
    return pl.pallas_call(
        kernel,
        out_shape=out_shape,
        in_specs=[smem] * scalars + [hbm] * in_hbm + [vmem] * (len(args) - lead),
        out_specs=jax.tree.map(lambda _: vmem, out_shape),
        compiler_params=pltpu.CompilerParams(vmem_limit_bytes=None if in_hbm else VMEM_BYTES),
        scratch_shapes=[pltpu.VMEM(s, jnp.float32) if isinstance(s, tuple) else s for s in scratch],
    )(*args[:lead], *[pltpu.with_memory_space_constraint(a, pltpu.VMEM) for a in args[lead:]])


def vm(*shape, dtype=jnp.float32):
    return pltpu.VMEM(shape, dtype)


def swap(pieces, axes):
    return lax.all_to_all(pieces, axes, split_axis=0, concat_axis=0, tiled=True)


def copies(piece, axes):
    return jnp.broadcast_to(piece, (lax.axis_size(axes),) + piece.shape)


def shards(field, brick_order, start_first, start_second, start_third):
    species, rows_here, cells_y, cells_z = field.shape
    rows_x, rank_one = start_first.shape
    full_y, rank_two = start_second.shape
    rank_three = start_third.shape[1]
    brick_len = cells_z // brick_order.shape[0]
    merged_rows = species * rank_one
    devices = lax.axis_size(ORDER)
    chips = lax.axis_size(CHIPS)
    parts_y = full_y // LANES
    core = lax.axis_index("gc").astype(jnp.int32).reshape(1)
    exchange = [(0, 1), (1, 0)]

    sent, start_first, start_second, start_third = call(
        functools.partial(send_field_kernel, brick_len=brick_len),
        (vm(cells_z * species, cells_y), vm(rank_one, rows_x), vm(rank_two, full_y), vm(rank_three, cells_z)),
        brick_order,
        core,
        field.reshape(species, cells_y, cells_z),
        start_first.T,
        start_second.T,
        start_third.T,
        scratch=[
            (species, cells_y, cells_z),
            (rank_three, cells_z),
            (cells_z, rank_three),
            (cells_z, rank_three),
            pltpu.SemaphoreType.DMA((species,)),
            pltpu.SemaphoreType.DMA((3,)),
        ],
        scalars=2,
        in_hbm=4,
    )
    data = swap(sent.reshape(devices, species, cells_y), ORDER).reshape(devices * species, cells_y)

    gram = call(
        functools.partial(gram_first_kernel, species=species, rows_x=rows_x, parts=parts_y), vm(rows_x, rows_x), data
    )
    gram = jnp.sum(swap(gram.reshape(lax.axis_size(CLOSE), -1, rows_x), CLOSE), axis=0)
    gram = jnp.sum(swap(copies(gram, FAR), FAR), axis=0)
    gram = swap(copies(gram, CLOSE), CLOSE).reshape(rows_x, rows_x)

    merged, kept, sent = call(
        functools.partial(second_kernel, species=species, rows_x=rows_x, parts=parts_y),
        (vm(merged_rows, full_y),) + (vm(parts_y * (parts_y + 1) // 4 * LANES, LANES),) * 2,
        core,
        gram,
        start_first,
        data,
        scratch=[(rank_one, rows_x)],
        scalars=1,
    )
    gram = kept + lax.ppermute(sent, "gc", exchange)
    gram = jnp.sum(swap(gram.reshape(lax.axis_size(BLOCK), -1, LANES), BLOCK), axis=0)
    gram = jnp.sum(swap(copies(gram, BEYOND), BEYOND), axis=0)
    own = swap(copies(gram, BLOCK), BLOCK).reshape(-1, LANES)
    other = lax.ppermute(own, "gc", exchange)

    near = lax.axis_size("gl")
    row_groups = lax.axis_size("gw") * 4
    sent = call(
        functools.partial(third_kernel, parts=parts_y),
        vm(lax.axis_size("gh"), near, lax.axis_size(("gu", "gv", "gk")), row_groups, LANES),
        core,
        own,
        other,
        start_second,
        merged,
        scratch=[(rank_two, merged_rows)],
        scalars=1,
    )
    own = swap(sent.reshape(chips, 4, LANES), CHIPS).reshape(chips * 4, LANES)
    other = lax.ppermute(own, "gc", exchange)

    spread_shape = vm(lax.axis_size(NEAR), rank_three, cells_z)
    cut = vm(cells_z, 4 * LANES, dtype=jnp.bfloat16)
    pieces, high, low = call(
        functools.partial(start_third_kernel, parts=4),
        (spread_shape, cut, cut),
        start_third,
        own,
        other,
    )
    for repeat in range(ITERS - 1):
        pieces = call(step_third_kernel, spread_shape, swap(pieces, NEAR), high, low)
    gx = lax.axis_index(("gu", "gv", "gk"))
    at = ((gx // 4) * 16 + (gx % 4) * 2 + lax.axis_index("gh")).astype(jnp.int32).reshape(1)
    return call(
        functools.partial(core_kernel, parts=4),
        jax.ShapeDtypeStruct((2, 4, rank_three), jnp.float32),
        core,
        at,
        swap(pieces, NEAR),
        high,
        low,
        scratch=[(merged_rows, rank_three)],
        scalars=2,
    )


def solution(mesh):
    gx, gy, gz = mesh.devices.shape
    fine = Mesh(mesh.devices.reshape(2, gx // 4, 2, 2, gy // 2, gz // 2, 2), FINE)
    in_specs = (P(None, ("gu", "gv", "gk", "gw", "gc"), ("gh", "gl"), None), P(), P(), P(), P())
    out_specs = P(("gu", "gv", "gk", "gh", "gl"), ("gw", "gc"), None)
    return jax.shard_map(shards, mesh=fine, in_specs=in_specs, out_specs=out_specs, check_vma=False)
```

```python
import functools

import jax
import jax.numpy as jnp
from jax import lax
from jax.experimental import pallas as pl
from jax.experimental.pallas import tpu as pltpu
from jax.sharding import Mesh, PartitionSpec as P

ITERS = 2
LANES = 128
PANEL = 16
VMEM_BYTES = 20 << 20
FINE = ("gu", "gv", "gk", "gh", "gl", "gw", "gp", "gc")
CHIPS = ("gh", "gl", "gu", "gv", "gk", "gw", "gp")
ORDER = CHIPS + ("gc",)
NEAR = ("gl", "gk", "gp")
CLOSE = ("gl", "gw", "gp", "gc")
FAR = ("gh", "gu", "gv", "gk")
BLOCK = ("gk", "gl", "gw", "gp")
BEYOND = ("gu", "gh", "gv")

highest = lax.Precision.HIGHEST
NN = ((1,), (0,))
NT = ((1,), (1,))
TN = ((0,), (0,))


def mm(a, b, dims):
    return lax.dot_general(a, b, (dims, ((), ())), precision=highest, preferred_element_type=jnp.float32)


def halves(x):
    high = x.astype(jnp.bfloat16)
    return high, (x - high.astype(jnp.float32)).astype(jnp.bfloat16)


def mm3(a, b, dims):
    def dot(x, y):
        return lax.dot_general(x, y, (dims, ((), ())), preferred_element_type=jnp.float32)

    size = a[0].shape[0]
    both = dot(jnp.concatenate(a, axis=0), b[0])
    return both[:size] + (both[size:] + dot(a[0], b[1]))


def orthonormal_rows(wide):
    rank = wide.shape[0]
    inner = mm(wide, wide, NT)
    shape = (rank, rank)
    row_id = lax.broadcasted_iota(jnp.int32, shape, 0)
    inverse = (row_id == lax.broadcasted_iota(jnp.int32, shape, 1)).astype(jnp.float32)
    pivots = jnp.ones(shape, jnp.float32)
    for start in range(0, rank, PANEL):
        columns = [jnp.broadcast_to(inner[:, start + j : start + j + 1], shape) for j in range(PANEL)]
        for j in range(PANEL):
            k = start + j
            pivot = jnp.broadcast_to(columns[j][k : k + 1, :], shape)
            pivots = jnp.where(row_id == k, pivot, pivots)
            if k == rank - 1:
                break
            factor = jnp.where(row_id > k, columns[j] * (1.0 / pivot), 0.0)
            for i in range(j + 1, PANEL):
                columns[i] = columns[i] - factor * columns[i][k : k + 1, :]
            if start + PANEL < rank:
                inner = inner - factor * inner[k : k + 1, :]
            inverse = inverse - factor * inverse[k : k + 1, :]
    return mm(inverse * (1.0 / jnp.sqrt(pivots)), wide, NN)


def send_field_kernel(
    order_ref, core_ref, field_hbm, first_hbm, second_hbm, third_hbm, out_ref, first_ref, second_ref, third_ref, field_ref,
    raw_ref, rows_ref, placed_ref, sems, start_sems, *, brick_len
):
    species, cells_y, cells_z = field_hbm.shape
    loads = [pltpu.make_async_copy(field_hbm.at[s], field_ref.at[s], sems.at[s]) for s in range(species)]
    pairs = (third_hbm, raw_ref), (second_hbm, second_ref), (first_hbm, first_ref)
    starts = [pltpu.make_async_copy(source, target, start_sems.at[i]) for i, (source, target) in enumerate(pairs)]
    for load in starts[:1] + loads + starts[1:]:
        load.start()
    lane = lax.broadcasted_iota(jnp.int32, (1, cells_z), 1)
    brick = lane // brick_len
    place = jnp.zeros((1, cells_z), jnp.int32)
    for b in range(cells_z // brick_len):
        place = jnp.where(brick == b, order_ref[b] * brick_len, place)
    grid_z = (place + lane % brick_len).astype(jnp.float32)
    taper = 0.5 + 1.5 * grid_z / (cells_z - 1)
    starts[0].wait()
    rows_ref[...] = raw_ref[...].T
    for b in range(cells_z // brick_len):
        at = pl.multiple_of(order_ref[b] * brick_len, brick_len)
        placed_ref[b * brick_len : (b + 1) * brick_len, :] = rows_ref[pl.ds(at, brick_len), :]
    core = (core_ref[0] & 1)
    half = cells_z // 2
    third_ref[:, :half] = placed_ref[pl.ds(core, half, stride=2), :].T
    third_ref[:, half:] = placed_ref[pl.ds(1 - core, half, stride=2), :].T
    for s in range(species):
        loads[s].wait()
        for j in range(cells_z // LANES):
            cut = slice(j * LANES, (j + 1) * LANES)
            block = field_ref[s, :, cut] * taper[:, cut]
            out_ref[pl.ds(j * LANES * species + s, LANES, stride=species), :] = block.T
    for load in starts[1:]:
        load.wait()


def fibre(ref, s, species, rows_x, parts):
    return jnp.concatenate(
        [ref[pl.ds(yq * rows_x * species + s, rows_x, stride=species), :] for yq in range(parts)], axis=1
    )


def gram_first_kernel(data_ref, out_ref, *, species, rows_x, parts):
    total = jnp.zeros(out_ref.shape, jnp.float32)
    for s in range(species):
        cut = halves(fibre(data_ref, s, species, rows_x, parts))
        total = total + mm3(cut, cut, NT)
    out_ref[...] = total


def second_kernel(
    core_ref, gram_ref, start_ref, data_ref, merged_ref, kept_ref, sent_ref, rows_ref, *, species, rows_x, parts
):
    gram = gram_ref[...]
    current = start_ref[...]
    for repeat in range(ITERS):
        current = orthonormal_rows(mm(current, gram, NN))
    rank = current.shape[0]
    rows_ref[...] = current
    quarter = rank // 4
    order = [r for c in range(4) for r in range(rank) if (r >> 3 & 1) * 2 + (r >> 1 & 1) == c]
    current = halves(jnp.concatenate([rows_ref[r : r + 1, :] for r in order], axis=0))
    for s in range(species):
        product = mm3(current, halves(fibre(data_ref, s, species, rows_x, parts)), NN)
        for c in range(4):
            merged_ref[(c * species + s) * quarter : (c * species + s + 1) * quarter, :] = product[
                c * quarter : (c + 1) * quarter
            ]
    merged = merged_ref[...]
    flipped = halves(merged.T)
    merged = halves(merged)
    blocks = []
    for i in range(parts):
        cut = slice(i * LANES, (i + 1) * LANES)
        product = mm3([x[cut] for x in flipped], [x[:, i * LANES :] for x in merged], NN)
        blocks += [product[:, j * LANES : (j + 1) * LANES] for j in range(parts - i)]
    count = len(blocks) // 2
    for i in range(count):
        rows = slice(i * LANES, (i + 1) * LANES)
        kept_ref[rows, :] = jnp.where((core_ref[0] & 1) == 0, blocks[i], blocks[count + i])
        sent_ref[rows, :] = jnp.where((core_ref[0] & 1) == 0, blocks[count + i], blocks[i])


def symmetric_of(core, own_ref, other_ref, parts):
    pairs = (own_ref, other_ref), (other_ref, own_ref)
    blocks = []
    for first, second in pairs:
        for i in range(own_ref.shape[0] // LANES):
            rows = slice(i * LANES, (i + 1) * LANES)
            blocks.append(jnp.where(core == 0, first[rows, :], second[rows, :]))
    upper = {}
    for i in range(parts):
        for j in range(i, parts):
            upper[i, j] = blocks[len(upper)]
    lines = [[upper[i, j] if i <= j else upper[j, i].T for j in range(parts)] for i in range(parts)]
    return jnp.concatenate([jnp.concatenate(line, axis=1) for line in lines], axis=0)


def third_kernel(core_ref, own_ref, other_ref, start_ref, merged_ref, out_ref, rows_ref, *, parts):
    gram = halves(symmetric_of((core_ref[0] & 1), own_ref, other_ref, parts))
    current = start_ref[...]
    for repeat in range(ITERS):
        current = orthonormal_rows(mm3(halves(current), gram, NN))
    rows_ref[...] = mm(current, merged_ref[...], NT)
    quarter = LANES // 4
    groups = [rows_ref[pl.ds(e, rows_ref.shape[0] // 4, stride=4), :] for e in range(4)]
    group_id = lax.broadcasted_iota(jnp.int32, groups[0].shape, 1) // quarter
    for k in range(out_ref.shape[3]):
        for h in range(out_ref.shape[1]):
            c = k * 2 + h
            piece = pltpu.roll(groups[0], (4 - c) % 4 * quarter, 1) if c else groups[0]
            for e in range(1, 4):
                shift = (e - c) % 4 * quarter
                piece = jnp.where(group_id == e, pltpu.roll(groups[e], shift, 1) if shift else groups[e], piece)
            piece = jnp.concatenate([piece[0:2], piece[4:6], piece[2:4], piece[6:8]], axis=0)
            for i in range(out_ref.shape[0]):
                for j in range(out_ref.shape[2]):
                    for w in range(out_ref.shape[4]):
                        out_ref[i, h, j, k, w] = piece


def columns_of(own_ref, other_ref, parts):
    size = own_ref.shape[0] // parts
    return jnp.concatenate(
        [
            jnp.concatenate([ref[pl.ds(q, size, stride=parts), :] for q in range(parts)], axis=1)
            for ref in (own_ref, other_ref)
        ],
        axis=0,
    )


def spread(out_ref, wide):
    for i in range(out_ref.shape[0]):
        out_ref[i] = wide


def start_third_kernel(start_ref, own_ref, other_ref, out_ref, high_ref, low_ref, *, parts):
    data = halves(columns_of(own_ref, other_ref, parts))
    high_ref[...], low_ref[...] = data
    inner = mm3(halves(start_ref[...]), data, NN)
    spread(out_ref, mm3(halves(inner), data, NT))


def total_of(parts_ref):
    total = parts_ref[0]
    for i in range(1, parts_ref.shape[0]):
        total = total + parts_ref[i]
    return total


def step_third_kernel(parts_ref, high_ref, low_ref, out_ref):
    current = orthonormal_rows(total_of(parts_ref))
    data = high_ref[...], low_ref[...]
    inner = mm3(halves(current), data, NN)
    spread(out_ref, mm3(halves(inner), data, NT))


def core_kernel(place_ref, parts_ref, high_ref, low_ref, out_ref, rows_ref):
    current = halves(orthonormal_rows(total_of(parts_ref)))
    block = (place_ref[0] >> 1 & 1) * 2 + (place_ref[0] & 1)
    cut = pl.ds(pl.multiple_of(block * LANES, LANES), LANES)
    rows_ref[...] = mm3(current, (high_ref[:, cut], low_ref[:, cut]), NN).T
    at = place_ref[0] >> 2
    for e in range(out_ref.shape[1]):
        for b in range(out_ref.shape[0]):
            out_ref[b, e, :] = rows_ref[at + e * (LANES // 4) + b, :]


def call(kernel, out_shape, *args, scratch=(), scalars=0, in_hbm=0):
    vmem = pl.BlockSpec(memory_space=pltpu.VMEM)
    smem = pl.BlockSpec(memory_space=pltpu.SMEM)
    hbm = pl.BlockSpec(memory_space=pltpu.HBM)
    lead = scalars + in_hbm
    return pl.pallas_call(
        kernel,
        out_shape=out_shape,
        in_specs=[smem] * scalars + [hbm] * in_hbm + [vmem] * (len(args) - lead),
        out_specs=jax.tree.map(lambda _: vmem, out_shape),
        compiler_params=pltpu.CompilerParams(vmem_limit_bytes=None if in_hbm else VMEM_BYTES),
        scratch_shapes=[pltpu.VMEM(s, jnp.float32) if isinstance(s, tuple) else s for s in scratch],
    )(*args[:lead], *[pltpu.with_memory_space_constraint(a, pltpu.VMEM) for a in args[lead:]])


def vm(*shape, dtype=jnp.float32):
    return pltpu.VMEM(shape, dtype)


def swap(pieces, axes):
    return lax.all_to_all(pieces, axes, split_axis=0, concat_axis=0, tiled=True)


def copies(piece, axes):
    return jnp.broadcast_to(piece, (lax.axis_size(axes),) + piece.shape)


def shards(field, brick_order, start_first, start_second, start_third):
    species, rows_here, cells_y, cells_z = field.shape
    rows_x, rank_one = start_first.shape
    full_y, rank_two = start_second.shape
    rank_three = start_third.shape[1]
    brick_len = cells_z // brick_order.shape[0]
    merged_rows = species * rank_one
    devices = lax.axis_size(ORDER)
    chips = lax.axis_size(CHIPS)
    parts_y = full_y // LANES
    gx = lax.axis_index(("gu", "gv", "gk"))
    row = (gx >> 2) * 8 + (gx >> 1 & 1) * 4 + lax.axis_index("gh") * 2
    core = (row * 4 + lax.axis_index("gw") * 2 + lax.axis_index("gc")).astype(jnp.int32).reshape(1)
    exchange = [(0, 1), (1, 0)]

    sent, start_first, start_second, start_third = call(
        functools.partial(send_field_kernel, brick_len=brick_len),
        (vm(cells_z * species, cells_y), vm(rank_one, rows_x), vm(rank_two, full_y), vm(rank_three, cells_z)),
        brick_order,
        core,
        field.reshape(species, cells_y, cells_z),
        start_first.T,
        start_second.T,
        start_third.T,
        scratch=[
            (species, cells_y, cells_z),
            (rank_three, cells_z),
            (cells_z, rank_three),
            (cells_z, rank_three),
            pltpu.SemaphoreType.DMA((species,)),
            pltpu.SemaphoreType.DMA((3,)),
        ],
        scalars=2,
        in_hbm=4,
    )
    data = swap(sent.reshape(devices, species, cells_y), ORDER).reshape(devices * species, cells_y)

    gram = call(
        functools.partial(gram_first_kernel, species=species, rows_x=rows_x, parts=parts_y), vm(rows_x, rows_x), data
    )
    gram = jnp.sum(swap(gram.reshape(lax.axis_size(CLOSE), -1, rows_x), CLOSE), axis=0)
    gram = jnp.sum(swap(copies(gram, FAR), FAR), axis=0)
    gram = swap(copies(gram, CLOSE), CLOSE).reshape(rows_x, rows_x)

    merged, kept, sent = call(
        functools.partial(second_kernel, species=species, rows_x=rows_x, parts=parts_y),
        (vm(merged_rows, full_y),) + (vm(parts_y * (parts_y + 1) // 4 * LANES, LANES),) * 2,
        core,
        gram,
        start_first,
        data,
        scratch=[(rank_one, rows_x)],
        scalars=1,
    )
    gram = kept + lax.ppermute(sent, "gc", exchange)
    gram = jnp.sum(swap(gram.reshape(lax.axis_size(BLOCK), -1, LANES), BLOCK), axis=0)
    gram = jnp.sum(swap(copies(gram, BEYOND), BEYOND), axis=0)
    own = swap(copies(gram, BLOCK), BLOCK).reshape(-1, LANES)
    other = lax.ppermute(own, "gc", exchange)

    sent = call(
        functools.partial(third_kernel, parts=parts_y),
        vm(lax.axis_size("gh"), lax.axis_size("gl"), lax.axis_size(("gu", "gv")), lax.axis_size("gk"), 2, 8, LANES),
        core,
        own,
        other,
        start_second,
        merged,
        scratch=[(rank_two, merged_rows)],
        scalars=1,
    )
    own = swap(sent.reshape(chips, 4, LANES), CHIPS).reshape(chips * 4, LANES)
    other = lax.ppermute(own, "gc", exchange)

    spread_shape = vm(lax.axis_size(NEAR), rank_three, cells_z)
    cut = vm(cells_z, 4 * LANES, dtype=jnp.bfloat16)
    pieces, high, low = call(
        functools.partial(start_third_kernel, parts=4),
        (spread_shape, cut, cut),
        start_third,
        own,
        other,
    )
    for repeat in range(ITERS - 1):
        pieces = call(step_third_kernel, spread_shape, swap(pieces, NEAR), high, low)
    return call(
        core_kernel,
        jax.ShapeDtypeStruct((2, 4, rank_three), jnp.float32),
        core,
        swap(pieces, NEAR),
        high,
        low,
        scratch=[(merged_rows, rank_three)],
        scalars=1,
    )


def solution(mesh):
    gx, gy, gz = mesh.devices.shape
    fine = Mesh(mesh.devices.reshape(2, gx // 4, 2, 2, gy // 2, gz // 4, 2, 2), FINE)
    in_specs = (P(None, ("gu", "gv", "gk", "gw", "gp", "gc"), ("gh", "gl"), None), P(), P(), P(), P())
    out_specs = P(("gu", "gv", "gk", "gh", "gl"), ("gw", "gp", "gc"), None)
    return jax.shard_map(shards, mesh=fine, in_specs=in_specs, out_specs=out_specs, check_vma=False)
```

```python
import functools

import jax
import jax.numpy as jnp
from jax import lax
from jax.experimental import pallas as pl
from jax.experimental.pallas import tpu as pltpu
from jax.sharding import Mesh, PartitionSpec as P

ITERS = 2
LANES = 128
PANEL = 16
VMEM_BYTES = 20 << 20
FINE = ("gu", "gv", "gk", "gh", "gl", "gw", "gp", "gc")
CHIPS = ("gh", "gl", "gu", "gv", "gk", "gw", "gp")
ORDER = CHIPS + ("gc",)
NEAR = ("gl", "gk", "gp")
CLOSE = ("gl", "gw", "gp", "gc")
FAR = ("gh", "gu", "gv", "gk")
BLOCK = ("gk", "gl", "gw", "gp")
BEYOND = ("gu", "gh", "gv")

highest = lax.Precision.HIGHEST
NN = ((1,), (0,))
NT = ((1,), (1,))
TN = ((0,), (0,))


def mm(a, b, dims):
    return lax.dot_general(a, b, (dims, ((), ())), precision=highest, preferred_element_type=jnp.float32)


def halves(x):
    high = x.astype(jnp.bfloat16)
    return high, (x - high.astype(jnp.float32)).astype(jnp.bfloat16)


def mm3(a, b, dims):
    def dot(x, y):
        return lax.dot_general(x, y, (dims, ((), ())), preferred_element_type=jnp.float32)

    size = a[0].shape[0]
    both = dot(jnp.concatenate(a, axis=0), b[0])
    return both[:size] + (both[size:] + dot(a[0], b[1]))


def orthonormal_rows(wide):
    rank = wide.shape[0]
    inner = mm(wide, wide, NT)
    shape = (rank, rank)
    row_id = lax.broadcasted_iota(jnp.int32, shape, 0)
    inverse = (row_id == lax.broadcasted_iota(jnp.int32, shape, 1)).astype(jnp.float32)
    pivots = jnp.ones(shape, jnp.float32)
    for start in range(0, rank, PANEL):
        columns = [jnp.broadcast_to(inner[:, start + j : start + j + 1], shape) for j in range(PANEL)]
        for j in range(PANEL):
            k = start + j
            pivot = jnp.broadcast_to(columns[j][k : k + 1, :], shape)
            pivots = jnp.where(row_id == k, pivot, pivots)
            if k == rank - 1:
                break
            factor = jnp.where(row_id > k, columns[j] * (1.0 / pivot), 0.0)
            for i in range(j + 1, PANEL):
                columns[i] = columns[i] - factor * columns[i][k : k + 1, :]
            if start + PANEL < rank:
                inner = inner - factor * inner[k : k + 1, :]
            inverse = inverse - factor * inverse[k : k + 1, :]
    return mm(inverse * (1.0 / jnp.sqrt(pivots)), wide, NN)


def send_field_kernel(
    order_hbm, field_hbm, first_hbm, second_hbm, third_hbm, out_ref, first_ref, second_ref, third_ref, field_ref,
    raw_ref, rows_ref, placed_ref, order_ref, sems, start_sems, *, brick_len
):
    species, cells_y, cells_z = field_hbm.shape
    loads = [pltpu.make_async_copy(field_hbm.at[s], field_ref.at[s], sems.at[s]) for s in range(species)]
    pairs = (order_hbm, order_ref), (third_hbm, raw_ref), (second_hbm, second_ref), (first_hbm, first_ref)
    starts = [pltpu.make_async_copy(source, target, start_sems.at[i]) for i, (source, target) in enumerate(pairs)]
    for load in starts[:2] + loads + starts[2:]:
        load.start()
    starts[0].wait()
    lane = lax.broadcasted_iota(jnp.int32, (1, cells_z), 1)
    brick = lane // brick_len
    place = jnp.zeros((1, cells_z), jnp.int32)
    for b in range(cells_z // brick_len):
        place = jnp.where(brick == b, order_ref[b] * brick_len, place)
    grid_z = (place + lane % brick_len).astype(jnp.float32)
    taper = 0.5 + 1.5 * grid_z / (cells_z - 1)
    starts[1].wait()
    rows_ref[...] = raw_ref[...].T
    for b in range(cells_z // brick_len):
        at = pl.multiple_of(order_ref[b] * brick_len, brick_len)
        placed_ref[b * brick_len : (b + 1) * brick_len, :] = rows_ref[pl.ds(at, brick_len), :]
    core = lax.axis_index("gc")
    half = cells_z // 2
    third_ref[:, :half] = placed_ref[pl.ds(core, half, stride=2), :].T
    third_ref[:, half:] = placed_ref[pl.ds(1 - core, half, stride=2), :].T
    for s in range(species):
        loads[s].wait()
        for j in range(cells_z // LANES):
            cut = slice(j * LANES, (j + 1) * LANES)
            block = field_ref[s, :, cut] * taper[:, cut]
            out_ref[pl.ds(j * LANES * species + s, LANES, stride=species), :] = block.T
    for load in starts[2:]:
        load.wait()


def fibre(ref, s, species, rows_x, parts):
    return jnp.concatenate(
        [ref[pl.ds(yq * rows_x * species + s, rows_x, stride=species), :] for yq in range(parts)], axis=1
    )


def gram_first_kernel(data_ref, out_ref, *, species, rows_x, parts):
    total = jnp.zeros(out_ref.shape, jnp.float32)
    for s in range(species):
        cut = halves(fibre(data_ref, s, species, rows_x, parts))
        total = total + mm3(cut, cut, NT)
    out_ref[...] = total


def second_kernel(
    gram_ref, start_ref, data_ref, merged_ref, kept_ref, sent_ref, rows_ref, *, species, rows_x, parts
):
    gram = gram_ref[...]
    current = start_ref[...]
    for repeat in range(ITERS):
        current = orthonormal_rows(mm(current, gram, NN))
    rank = current.shape[0]
    rows_ref[...] = current
    quarter = rank // 4
    order = [r for c in range(4) for r in range(rank) if (r >> 3 & 1) * 2 + (r >> 1 & 1) == c]
    current = halves(jnp.concatenate([rows_ref[r : r + 1, :] for r in order], axis=0))
    for s in range(species):
        product = mm3(current, halves(fibre(data_ref, s, species, rows_x, parts)), NN)
        for c in range(4):
            merged_ref[(c * species + s) * quarter : (c * species + s + 1) * quarter, :] = product[
                c * quarter : (c + 1) * quarter
            ]
    merged = merged_ref[...]
    flipped = halves(merged.T)
    merged = halves(merged)
    blocks = []
    for i in range(parts):
        cut = slice(i * LANES, (i + 1) * LANES)
        product = mm3([x[cut] for x in flipped], [x[:, i * LANES :] for x in merged], NN)
        blocks += [product[:, j * LANES : (j + 1) * LANES] for j in range(parts - i)]
    count = len(blocks) // 2
    first = lax.axis_index("gc") == 0
    for i in range(count):
        rows = slice(i * LANES, (i + 1) * LANES)
        kept_ref[rows, :] = jnp.where(first, blocks[i], blocks[count + i])
        sent_ref[rows, :] = jnp.where(first, blocks[count + i], blocks[i])


def symmetric_of(core, own_ref, other_ref, parts):
    pairs = (own_ref, other_ref), (other_ref, own_ref)
    blocks = []
    for first, second in pairs:
        for i in range(own_ref.shape[0] // LANES):
            rows = slice(i * LANES, (i + 1) * LANES)
            blocks.append(jnp.where(core == 0, first[rows, :], second[rows, :]))
    upper = {}
    for i in range(parts):
        for j in range(i, parts):
            upper[i, j] = blocks[len(upper)]
    lines = [[upper[i, j] if i <= j else upper[j, i].T for j in range(parts)] for i in range(parts)]
    return jnp.concatenate([jnp.concatenate(line, axis=1) for line in lines], axis=0)


def third_kernel(own_ref, other_ref, start_ref, merged_ref, out_ref, rows_ref, *, parts):
    gram = halves(symmetric_of(lax.axis_index("gc"), own_ref, other_ref, parts))
    current = start_ref[...]
    for repeat in range(ITERS):
        current = orthonormal_rows(mm3(halves(current), gram, NN))
    rows_ref[...] = mm(current, merged_ref[...], NT)
    quarter = LANES // 4
    groups = [rows_ref[pl.ds(e, rows_ref.shape[0] // 4, stride=4), :] for e in range(4)]
    group_id = lax.broadcasted_iota(jnp.int32, groups[0].shape, 1) // quarter
    for k in range(out_ref.shape[3]):
        for h in range(out_ref.shape[1]):
            c = k * 2 + h
            piece = pltpu.roll(groups[0], (4 - c) % 4 * quarter, 1) if c else groups[0]
            for e in range(1, 4):
                shift = (e - c) % 4 * quarter
                piece = jnp.where(group_id == e, pltpu.roll(groups[e], shift, 1) if shift else groups[e], piece)
            piece = jnp.concatenate([piece[0:2], piece[4:6], piece[2:4], piece[6:8]], axis=0)
            for i in range(out_ref.shape[0]):
                for j in range(out_ref.shape[2]):
                    for w in range(out_ref.shape[4]):
                        out_ref[i, h, j, k, w] = piece


def columns_of(own_ref, other_ref, parts):
    size = own_ref.shape[0] // parts
    return jnp.concatenate(
        [
            jnp.concatenate([ref[pl.ds(q, size, stride=parts), :] for q in range(parts)], axis=1)
            for ref in (own_ref, other_ref)
        ],
        axis=0,
    )


def spread(out_ref, wide):
    for i in range(out_ref.shape[0]):
        out_ref[i] = wide


def start_third_kernel(start_ref, own_ref, other_ref, out_ref, high_ref, low_ref, *, parts):
    data = halves(columns_of(own_ref, other_ref, parts))
    high_ref[...], low_ref[...] = data
    inner = mm3(halves(start_ref[...]), data, NN)
    spread(out_ref, mm3(halves(inner), data, NT))


def total_of(parts_ref):
    total = parts_ref[0]
    for i in range(1, parts_ref.shape[0]):
        total = total + parts_ref[i]
    return total


def step_third_kernel(parts_ref, high_ref, low_ref, out_ref):
    current = orthonormal_rows(total_of(parts_ref))
    data = high_ref[...], low_ref[...]
    inner = mm3(halves(current), data, NN)
    spread(out_ref, mm3(halves(inner), data, NT))


def core_kernel(parts_ref, high_ref, low_ref, out_ref, rows_ref):
    current = halves(orthonormal_rows(total_of(parts_ref)))
    block = lax.axis_index("gw") * 2 + lax.axis_index("gc")
    cut = pl.ds(pl.multiple_of(block * LANES, LANES), LANES)
    rows_ref[...] = mm3(current, (high_ref[:, cut], low_ref[:, cut]), NN).T
    at = lax.axis_index("gu") * 16 + lax.axis_index("gv") * 4 + lax.axis_index("gh") * 2
    for e in range(out_ref.shape[1]):
        for b in range(out_ref.shape[0]):
            out_ref[b, e, :] = rows_ref[at + e * (LANES // 4) + b, :]


def call(kernel, out_shape, *args, scratch=(), in_hbm=0):
    vmem = pl.BlockSpec(memory_space=pltpu.VMEM)
    hbm = pl.BlockSpec(memory_space=pltpu.HBM)
    return pl.pallas_call(
        kernel,
        out_shape=out_shape,
        in_specs=[hbm] * in_hbm + [vmem] * (len(args) - in_hbm),
        out_specs=jax.tree.map(lambda _: vmem, out_shape),
        compiler_params=pltpu.CompilerParams(vmem_limit_bytes=None if in_hbm else VMEM_BYTES),
        scratch_shapes=[pltpu.VMEM(s, jnp.float32) if isinstance(s, tuple) else s for s in scratch],
    )(*args[:in_hbm], *[pltpu.with_memory_space_constraint(a, pltpu.VMEM) for a in args[in_hbm:]])


def vm(*shape, dtype=jnp.float32):
    return pltpu.VMEM(shape, dtype)


def swap(pieces, axes):
    return lax.all_to_all(pieces, axes, split_axis=0, concat_axis=0, tiled=True)


def copies(piece, axes):
    return jnp.broadcast_to(piece, (lax.axis_size(axes),) + piece.shape)


def shards(field, brick_order, start_first, start_second, start_third):
    species, rows_here, cells_y, cells_z = field.shape
    rows_x, rank_one = start_first.shape
    full_y, rank_two = start_second.shape
    rank_three = start_third.shape[1]
    brick_len = cells_z // brick_order.shape[0]
    merged_rows = species * rank_one
    devices = lax.axis_size(ORDER)
    chips = lax.axis_size(CHIPS)
    parts_y = full_y // LANES
    exchange = [(0, 1), (1, 0)]

    sent, start_first, start_second, start_third = call(
        functools.partial(send_field_kernel, brick_len=brick_len),
        (vm(cells_z * species, cells_y), vm(rank_one, rows_x), vm(rank_two, full_y), vm(rank_three, cells_z)),
        brick_order,
        field.reshape(species, cells_y, cells_z),
        start_first.T,
        start_second.T,
        start_third.T,
        scratch=[
            (species, cells_y, cells_z),
            (rank_three, cells_z),
            (cells_z, rank_three),
            (cells_z, rank_three),
            pltpu.SMEM(brick_order.shape, jnp.int32),
            pltpu.SemaphoreType.DMA((species,)),
            pltpu.SemaphoreType.DMA((4,)),
        ],
        in_hbm=5,
    )
    data = swap(sent.reshape(devices, species, cells_y), ORDER).reshape(devices * species, cells_y)

    gram = call(
        functools.partial(gram_first_kernel, species=species, rows_x=rows_x, parts=parts_y), vm(rows_x, rows_x), data
    )
    gram = jnp.sum(swap(gram.reshape(lax.axis_size(CLOSE), -1, rows_x), CLOSE), axis=0)
    gram = jnp.sum(swap(copies(gram, FAR), FAR), axis=0)
    gram = swap(copies(gram, CLOSE), CLOSE).reshape(rows_x, rows_x)

    merged, kept, sent = call(
        functools.partial(second_kernel, species=species, rows_x=rows_x, parts=parts_y),
        (vm(merged_rows, full_y),) + (vm(parts_y * (parts_y + 1) // 4 * LANES, LANES),) * 2,
        gram,
        start_first,
        data,
        scratch=[(rank_one, rows_x)],
    )
    gram = kept + lax.ppermute(sent, "gc", exchange)
    gram = jnp.sum(swap(gram.reshape(lax.axis_size(BLOCK), -1, LANES), BLOCK), axis=0)
    gram = jnp.sum(swap(copies(gram, BEYOND), BEYOND), axis=0)
    own = swap(copies(gram, BLOCK), BLOCK).reshape(-1, LANES)
    other = lax.ppermute(own, "gc", exchange)

    sent = call(
        functools.partial(third_kernel, parts=parts_y),
        vm(lax.axis_size("gh"), lax.axis_size("gl"), lax.axis_size(("gu", "gv")), lax.axis_size("gk"), 2, 8, LANES),
        own,
        other,
        start_second,
        merged,
        scratch=[(rank_two, merged_rows)],
    )
    own = swap(sent.reshape(chips, 4, LANES), CHIPS).reshape(chips * 4, LANES)
    other = lax.ppermute(own, "gc", exchange)

    spread_shape = vm(lax.axis_size(NEAR), rank_three, cells_z)
    cut = vm(cells_z, 4 * LANES, dtype=jnp.bfloat16)
    pieces, high, low = call(
        functools.partial(start_third_kernel, parts=4),
        (spread_shape, cut, cut),
        start_third,
        own,
        other,
    )
    for repeat in range(ITERS - 1):
        pieces = call(step_third_kernel, spread_shape, swap(pieces, NEAR), high, low)
    return call(
        core_kernel,
        jax.ShapeDtypeStruct((2, 4, rank_three), jnp.float32),
        swap(pieces, NEAR),
        high,
        low,
        scratch=[(merged_rows, rank_three)],
    )


def solution(mesh):
    gx, gy, gz = mesh.devices.shape
    fine = Mesh(mesh.devices.reshape(2, gx // 4, 2, 2, gy // 2, gz // 4, 2, 2), FINE)
    in_specs = (P(None, ("gu", "gv", "gk", "gw", "gp", "gc"), ("gh", "gl"), None), P(), P(), P(), P())
    out_specs = P(("gu", "gv", "gk", "gh", "gl"), ("gw", "gp", "gc"), None)
    return jax.shard_map(shards, mesh=fine, in_specs=in_specs, out_specs=out_specs, check_vma=False)
```

```python
import functools

import jax
import jax.numpy as jnp
from jax import lax
from jax.experimental import pallas as pl
from jax.experimental.pallas import tpu as pltpu
from jax.sharding import Mesh, PartitionSpec as P

ITERS = 2
LANES = 128
PANEL = 16
VMEM_BYTES = 20 << 20
FINE = ("gu", "gv", "gk", "gh", "gl", "gw", "gp", "gc")
CHIPS = ("gh", "gl", "gu", "gv", "gk", "gw", "gp")
ORDER = CHIPS + ("gc",)
NEAR = ("gl", "gk", "gp")
CLOSE = ("gk", "gl", "gw", "gp", "gc")
BLOCK = ("gk", "gl", "gw", "gp")
BEYOND = ("gu", "gh", "gv")

highest = lax.Precision.HIGHEST
NN = ((1,), (0,))
NT = ((1,), (1,))
TN = ((0,), (0,))


def mm(a, b, dims):
    return lax.dot_general(a, b, (dims, ((), ())), precision=highest, preferred_element_type=jnp.float32)


def halves(x):
    high = x.astype(jnp.bfloat16)
    return high, (x - high.astype(jnp.float32)).astype(jnp.bfloat16)


def mm3(a, b, dims):
    def dot(x, y):
        return lax.dot_general(x, y, (dims, ((), ())), preferred_element_type=jnp.float32)

    size = a[0].shape[0]
    both = dot(jnp.concatenate(a, axis=0), b[0])
    return both[:size] + (both[size:] + dot(a[0], b[1]))


def orthonormal_rows(wide):
    rank = wide.shape[0]
    inner = mm(wide, wide, NT)
    shape = (rank, rank)
    row_id = lax.broadcasted_iota(jnp.int32, shape, 0)
    inverse = (row_id == lax.broadcasted_iota(jnp.int32, shape, 1)).astype(jnp.float32)
    pivots = jnp.ones(shape, jnp.float32)
    for start in range(0, rank, PANEL):
        columns = [jnp.broadcast_to(inner[:, start + j : start + j + 1], shape) for j in range(PANEL)]
        for j in range(PANEL):
            k = start + j
            pivot = jnp.broadcast_to(columns[j][k : k + 1, :], shape)
            pivots = jnp.where(row_id == k, pivot, pivots)
            if k == rank - 1:
                break
            factor = jnp.where(row_id > k, columns[j] * (1.0 / pivot), 0.0)
            for i in range(j + 1, PANEL):
                columns[i] = columns[i] - factor * columns[i][k : k + 1, :]
            if start + PANEL < rank:
                inner = inner - factor * inner[k : k + 1, :]
            inverse = inverse - factor * inverse[k : k + 1, :]
    return mm(inverse * (1.0 / jnp.sqrt(pivots)), wide, NN)


def send_field_kernel(
    order_hbm, field_hbm, first_hbm, second_hbm, third_hbm, out_ref, first_ref, second_ref, third_ref, field_ref,
    raw_ref, rows_ref, placed_ref, order_ref, sems, start_sems, *, brick_len
):
    species, cells_y, cells_z = field_hbm.shape
    loads = [pltpu.make_async_copy(field_hbm.at[s], field_ref.at[s], sems.at[s]) for s in range(species)]
    pairs = (order_hbm, order_ref), (third_hbm, raw_ref), (second_hbm, second_ref), (first_hbm, first_ref)
    starts = [pltpu.make_async_copy(source, target, start_sems.at[i]) for i, (source, target) in enumerate(pairs)]
    for load in starts[:2] + loads + starts[2:]:
        load.start()
    starts[0].wait()
    lane = lax.broadcasted_iota(jnp.int32, (1, cells_z), 1)
    brick = lane // brick_len
    place = jnp.zeros((1, cells_z), jnp.int32)
    for b in range(cells_z // brick_len):
        place = jnp.where(brick == b, order_ref[b] * brick_len, place)
    grid_z = (place + lane % brick_len).astype(jnp.float32)
    taper = 0.5 + 1.5 * grid_z / (cells_z - 1)
    starts[1].wait()
    rows_ref[...] = raw_ref[...].T
    for b in range(cells_z // brick_len):
        at = pl.multiple_of(order_ref[b] * brick_len, brick_len)
        placed_ref[b * brick_len : (b + 1) * brick_len, :] = rows_ref[pl.ds(at, brick_len), :]
    core = lax.axis_index("gc")
    half = cells_z // 2
    third_ref[:, :half] = placed_ref[pl.ds(core, half, stride=2), :].T
    third_ref[:, half:] = placed_ref[pl.ds(1 - core, half, stride=2), :].T
    for s in range(species):
        loads[s].wait()
        for j in range(cells_z // LANES):
            cut = slice(j * LANES, (j + 1) * LANES)
            block = field_ref[s, :, cut] * taper[:, cut]
            out_ref[pl.ds(j * LANES * species + s, LANES, stride=species), :] = block.T
    for load in starts[2:]:
        load.wait()


def fibre(ref, s, species, rows_x, parts):
    return jnp.concatenate(
        [ref[pl.ds(yq * rows_x * species + s, rows_x, stride=species), :] for yq in range(parts)], axis=1
    )


def gram_first_kernel(data_ref, out_ref, *, species, rows_x, parts):
    total = jnp.zeros(out_ref.shape, jnp.float32)
    for s in range(species):
        cut = halves(fibre(data_ref, s, species, rows_x, parts))
        total = total + mm3(cut, cut, NT)
    out_ref[...] = total


def second_kernel(
    gram_ref, start_ref, data_ref, merged_ref, kept_ref, sent_ref, rows_ref, *, species, rows_x, parts
):
    gram = gram_ref[...]
    current = start_ref[...]
    for repeat in range(ITERS):
        current = orthonormal_rows(mm(current, gram, NN))
    rank = current.shape[0]
    rows_ref[...] = current
    quarter = rank // 4
    order = [r for c in range(4) for r in range(rank) if (r >> 3 & 1) * 2 + (r >> 1 & 1) == c]
    current = halves(jnp.concatenate([rows_ref[r : r + 1, :] for r in order], axis=0))
    for s in range(species):
        product = mm3(current, halves(fibre(data_ref, s, species, rows_x, parts)), NN)
        for c in range(4):
            merged_ref[(c * species + s) * quarter : (c * species + s + 1) * quarter, :] = product[
                c * quarter : (c + 1) * quarter
            ]
    merged = merged_ref[...]
    flipped = halves(merged.T)
    merged = halves(merged)
    blocks = []
    for i in range(parts):
        cut = slice(i * LANES, (i + 1) * LANES)
        product = mm3([x[cut] for x in flipped], [x[:, i * LANES :] for x in merged], NN)
        blocks += [product[:, j * LANES : (j + 1) * LANES] for j in range(parts - i)]
    count = len(blocks) // 2
    first = lax.axis_index("gc") == 0
    for i in range(count):
        rows = slice(i * LANES, (i + 1) * LANES)
        kept_ref[rows, :] = jnp.where(first, blocks[i], blocks[count + i])
        sent_ref[rows, :] = jnp.where(first, blocks[count + i], blocks[i])


def symmetric_of(core, own_ref, other_ref, parts):
    pairs = (own_ref, other_ref), (other_ref, own_ref)
    blocks = []
    for first, second in pairs:
        for i in range(own_ref.shape[0] // LANES):
            rows = slice(i * LANES, (i + 1) * LANES)
            blocks.append(jnp.where(core == 0, first[rows, :], second[rows, :]))
    upper = {}
    for i in range(parts):
        for j in range(i, parts):
            upper[i, j] = blocks[len(upper)]
    lines = [[upper[i, j] if i <= j else upper[j, i].T for j in range(parts)] for i in range(parts)]
    return jnp.concatenate([jnp.concatenate(line, axis=1) for line in lines], axis=0)


def third_kernel(own_ref, other_ref, start_ref, merged_ref, out_ref, rows_ref, *, parts):
    gram = halves(symmetric_of(lax.axis_index("gc"), own_ref, other_ref, parts))
    current = start_ref[...]
    for repeat in range(ITERS):
        current = orthonormal_rows(mm3(halves(current), gram, NN))
    rows_ref[...] = mm(current, merged_ref[...], NT)
    quarter = LANES // 4
    groups = [rows_ref[pl.ds(e, rows_ref.shape[0] // 4, stride=4), :] for e in range(4)]
    group_id = lax.broadcasted_iota(jnp.int32, groups[0].shape, 1) // quarter
    for k in range(out_ref.shape[3]):
        for h in range(out_ref.shape[1]):
            c = k * 2 + h
            piece = pltpu.roll(groups[0], (4 - c) % 4 * quarter, 1) if c else groups[0]
            for e in range(1, 4):
                shift = (e - c) % 4 * quarter
                piece = jnp.where(group_id == e, pltpu.roll(groups[e], shift, 1) if shift else groups[e], piece)
            piece = jnp.concatenate([piece[0:2], piece[4:6], piece[2:4], piece[6:8]], axis=0)
            for i in range(out_ref.shape[0]):
                for j in range(out_ref.shape[2]):
                    for w in range(out_ref.shape[4]):
                        out_ref[i, h, j, k, w] = piece


def columns_of(own_ref, other_ref, parts):
    size = own_ref.shape[0] // parts
    return jnp.concatenate(
        [
            jnp.concatenate([ref[pl.ds(q, size, stride=parts), :] for q in range(parts)], axis=1)
            for ref in (own_ref, other_ref)
        ],
        axis=0,
    )


def spread(out_ref, wide):
    for i in range(out_ref.shape[0]):
        out_ref[i] = wide


def start_third_kernel(start_ref, own_ref, other_ref, out_ref, high_ref, low_ref, *, parts):
    data = halves(columns_of(own_ref, other_ref, parts))
    high_ref[...], low_ref[...] = data
    inner = mm3(halves(start_ref[...]), data, NN)
    spread(out_ref, mm3(halves(inner), data, NT))


def total_of(parts_ref):
    total = parts_ref[0]
    for i in range(1, parts_ref.shape[0]):
        total = total + parts_ref[i]
    return total


def step_third_kernel(parts_ref, high_ref, low_ref, out_ref):
    current = orthonormal_rows(total_of(parts_ref))
    data = high_ref[...], low_ref[...]
    inner = mm3(halves(current), data, NN)
    spread(out_ref, mm3(halves(inner), data, NT))


def core_kernel(parts_ref, high_ref, low_ref, out_ref, rows_ref):
    current = halves(orthonormal_rows(total_of(parts_ref)))
    block = lax.axis_index("gw") * 2 + lax.axis_index("gc")
    cut = pl.ds(pl.multiple_of(block * LANES, LANES), LANES)
    rows_ref[...] = mm3(current, (high_ref[:, cut], low_ref[:, cut]), NN).T
    at = lax.axis_index("gu") * 16 + lax.axis_index("gv") * 4 + lax.axis_index("gh") * 2
    for e in range(out_ref.shape[1]):
        for b in range(out_ref.shape[0]):
            out_ref[b, e, :] = rows_ref[at + e * (LANES // 4) + b, :]


def call(kernel, out_shape, *args, scratch=(), in_hbm=0):
    vmem = pl.BlockSpec(memory_space=pltpu.VMEM)
    hbm = pl.BlockSpec(memory_space=pltpu.HBM)
    return pl.pallas_call(
        kernel,
        out_shape=out_shape,
        in_specs=[hbm] * in_hbm + [vmem] * (len(args) - in_hbm),
        out_specs=jax.tree.map(lambda _: vmem, out_shape),
        compiler_params=pltpu.CompilerParams(vmem_limit_bytes=None if in_hbm else VMEM_BYTES),
        scratch_shapes=[pltpu.VMEM(s, jnp.float32) if isinstance(s, tuple) else s for s in scratch],
    )(*args[:in_hbm], *[pltpu.with_memory_space_constraint(a, pltpu.VMEM) for a in args[in_hbm:]])


def vm(*shape, dtype=jnp.float32):
    return pltpu.VMEM(shape, dtype)


def swap(pieces, axes):
    return lax.all_to_all(pieces, axes, split_axis=0, concat_axis=0, tiled=True)


def copies(piece, axes):
    return jnp.broadcast_to(piece, (lax.axis_size(axes),) + piece.shape)


def shards(field, brick_order, start_first, start_second, start_third):
    species, rows_here, cells_y, cells_z = field.shape
    rows_x, rank_one = start_first.shape
    full_y, rank_two = start_second.shape
    rank_three = start_third.shape[1]
    brick_len = cells_z // brick_order.shape[0]
    merged_rows = species * rank_one
    devices = lax.axis_size(ORDER)
    chips = lax.axis_size(CHIPS)
    parts_y = full_y // LANES
    exchange = [(0, 1), (1, 0)]

    sent, start_first, start_second, start_third = call(
        functools.partial(send_field_kernel, brick_len=brick_len),
        (vm(cells_z * species, cells_y), vm(rank_one, rows_x), vm(rank_two, full_y), vm(rank_three, cells_z)),
        brick_order,
        field.reshape(species, cells_y, cells_z),
        start_first.T,
        start_second.T,
        start_third.T,
        scratch=[
            (species, cells_y, cells_z),
            (rank_three, cells_z),
            (cells_z, rank_three),
            (cells_z, rank_three),
            pltpu.SMEM(brick_order.shape, jnp.int32),
            pltpu.SemaphoreType.DMA((species,)),
            pltpu.SemaphoreType.DMA((4,)),
        ],
        in_hbm=5,
    )
    data = swap(sent.reshape(devices, species, cells_y), ORDER).reshape(devices * species, cells_y)

    gram = call(
        functools.partial(gram_first_kernel, species=species, rows_x=rows_x, parts=parts_y), vm(rows_x, rows_x), data
    )
    gram = jnp.sum(swap(gram.reshape(lax.axis_size(CLOSE), -1, rows_x), CLOSE), axis=0)
    gram = jnp.sum(swap(copies(gram, BEYOND), BEYOND), axis=0)
    gram = swap(copies(gram, CLOSE), CLOSE).reshape(rows_x, rows_x)

    merged, kept, sent = call(
        functools.partial(second_kernel, species=species, rows_x=rows_x, parts=parts_y),
        (vm(merged_rows, full_y),) + (vm(parts_y * (parts_y + 1) // 4 * LANES, LANES),) * 2,
        gram,
        start_first,
        data,
        scratch=[(rank_one, rows_x)],
    )
    gram = kept + lax.ppermute(sent, "gc", exchange)
    gram = jnp.sum(swap(gram.reshape(lax.axis_size(BLOCK), -1, LANES), BLOCK), axis=0)
    gram = jnp.sum(swap(copies(gram, BEYOND), BEYOND), axis=0)
    own = swap(copies(gram, BLOCK), BLOCK).reshape(-1, LANES)
    other = lax.ppermute(own, "gc", exchange)

    sent = call(
        functools.partial(third_kernel, parts=parts_y),
        vm(lax.axis_size("gh"), lax.axis_size("gl"), lax.axis_size(("gu", "gv")), lax.axis_size("gk"), 2, 8, LANES),
        own,
        other,
        start_second,
        merged,
        scratch=[(rank_two, merged_rows)],
    )
    own = swap(sent.reshape(chips, 4, LANES), CHIPS).reshape(chips * 4, LANES)
    other = lax.ppermute(own, "gc", exchange)

    spread_shape = vm(lax.axis_size(NEAR), rank_three, cells_z)
    cut = vm(cells_z, 4 * LANES, dtype=jnp.bfloat16)
    pieces, high, low = call(
        functools.partial(start_third_kernel, parts=4),
        (spread_shape, cut, cut),
        start_third,
        own,
        other,
    )
    for repeat in range(ITERS - 1):
        pieces = call(step_third_kernel, spread_shape, swap(pieces, NEAR), high, low)
    return call(
        core_kernel,
        jax.ShapeDtypeStruct((2, 4, rank_three), jnp.float32),
        swap(pieces, NEAR),
        high,
        low,
        scratch=[(merged_rows, rank_three)],
    )


def solution(mesh):
    gx, gy, gz = mesh.devices.shape
    fine = Mesh(mesh.devices.reshape(2, gx // 4, 2, 2, gy // 2, gz // 4, 2, 2), FINE)
    in_specs = (P(None, ("gu", "gv", "gk", "gw", "gp", "gc"), ("gh", "gl"), None), P(), P(), P(), P())
    out_specs = P(("gu", "gv", "gk", "gh", "gl"), ("gw", "gp", "gc"), None)
    return jax.shard_map(shards, mesh=fine, in_specs=in_specs, out_specs=out_specs, check_vma=False)
```

```python
import functools

import jax
import jax.numpy as jnp
from jax import lax
from jax.experimental import pallas as pl
from jax.experimental.pallas import tpu as pltpu
from jax.sharding import Mesh, PartitionSpec as P

ITERS = 2
LANES = 128
PANEL = 16
VMEM_BYTES = 20 << 20
FINE = ("gu", "gv", "gk", "gh", "gl", "gw", "gp", "gc")
CHIPS = ("gh", "gl", "gu", "gv", "gk", "gw", "gp")
ORDER = CHIPS + ("gc",)
NEAR = ("gk", "gp", "gl")
CLOSE = ("gw", "gl", "gp", "gc")
FAR = ("gv", "gu", "gk", "gh")
BLOCK = ("gw", "gk", "gp", "gl")
BEYOND = ("gv", "gu", "gh")

highest = lax.Precision.HIGHEST
NN = ((1,), (0,))
NT = ((1,), (1,))
TN = ((0,), (0,))


def mm(a, b, dims):
    return lax.dot_general(a, b, (dims, ((), ())), precision=highest, preferred_element_type=jnp.float32)


def halves(x):
    high = x.astype(jnp.bfloat16)
    return high, (x - high.astype(jnp.float32)).astype(jnp.bfloat16)


def mm3(a, b, dims):
    def dot(x, y):
        return lax.dot_general(x, y, (dims, ((), ())), preferred_element_type=jnp.float32)

    size = a[0].shape[0]
    both = dot(jnp.concatenate(a, axis=0), b[0])
    return both[:size] + (both[size:] + dot(a[0], b[1]))


def orthonormal_rows(wide):
    rank = wide.shape[0]
    inner = mm(wide, wide, NT)
    shape = (rank, rank)
    row_id = lax.broadcasted_iota(jnp.int32, shape, 0)
    inverse = (row_id == lax.broadcasted_iota(jnp.int32, shape, 1)).astype(jnp.float32)
    pivots = jnp.ones(shape, jnp.float32)
    for start in range(0, rank, PANEL):
        columns = [jnp.broadcast_to(inner[:, start + j : start + j + 1], shape) for j in range(PANEL)]
        for j in range(PANEL):
            k = start + j
            pivot = jnp.broadcast_to(columns[j][k : k + 1, :], shape)
            pivots = jnp.where(row_id == k, pivot, pivots)
            if k == rank - 1:
                break
            factor = jnp.where(row_id > k, columns[j] * (1.0 / pivot), 0.0)
            for i in range(j + 1, PANEL):
                columns[i] = columns[i] - factor * columns[i][k : k + 1, :]
            if start + PANEL < rank:
                inner = inner - factor * inner[k : k + 1, :]
            inverse = inverse - factor * inverse[k : k + 1, :]
    return mm(inverse * (1.0 / jnp.sqrt(pivots)), wide, NN)


def send_field_kernel(
    order_hbm, field_hbm, first_hbm, second_hbm, third_hbm, out_ref, first_ref, second_ref, third_ref, field_ref,
    raw_ref, rows_ref, placed_ref, order_ref, sems, start_sems, *, brick_len
):
    species, cells_y, cells_z = field_hbm.shape
    loads = [pltpu.make_async_copy(field_hbm.at[s], field_ref.at[s], sems.at[s]) for s in range(species)]
    pairs = (order_hbm, order_ref), (third_hbm, raw_ref), (second_hbm, second_ref), (first_hbm, first_ref)
    starts = [pltpu.make_async_copy(source, target, start_sems.at[i]) for i, (source, target) in enumerate(pairs)]
    for load in starts[:2] + loads + starts[2:]:
        load.start()
    starts[0].wait()
    lane = lax.broadcasted_iota(jnp.int32, (1, cells_z), 1)
    brick = lane // brick_len
    place = jnp.zeros((1, cells_z), jnp.int32)
    for b in range(cells_z // brick_len):
        place = jnp.where(brick == b, order_ref[b] * brick_len, place)
    grid_z = (place + lane % brick_len).astype(jnp.float32)
    taper = 0.5 + 1.5 * grid_z / (cells_z - 1)
    starts[1].wait()
    rows_ref[...] = raw_ref[...].T
    for b in range(cells_z // brick_len):
        at = pl.multiple_of(order_ref[b] * brick_len, brick_len)
        placed_ref[b * brick_len : (b + 1) * brick_len, :] = rows_ref[pl.ds(at, brick_len), :]
    core = lax.axis_index("gc")
    half = cells_z // 2
    third_ref[:, :half] = placed_ref[pl.ds(core, half, stride=2), :].T
    third_ref[:, half:] = placed_ref[pl.ds(1 - core, half, stride=2), :].T
    for s in range(species):
        loads[s].wait()
        for j in range(cells_z // LANES):
            cut = slice(j * LANES, (j + 1) * LANES)
            block = field_ref[s, :, cut] * taper[:, cut]
            out_ref[pl.ds(j * LANES * species + s, LANES, stride=species), :] = block.T
    for load in starts[2:]:
        load.wait()


def fibre(ref, s, species, rows_x, parts):
    return jnp.concatenate(
        [ref[pl.ds(yq * rows_x * species + s, rows_x, stride=species), :] for yq in range(parts)], axis=1
    )


def gram_first_kernel(data_ref, out_ref, *, species, rows_x, parts):
    total = jnp.zeros(out_ref.shape, jnp.float32)
    for s in range(species):
        cut = halves(fibre(data_ref, s, species, rows_x, parts))
        total = total + mm3(cut, cut, NT)
    out_ref[...] = total


def second_kernel(
    gram_ref, start_ref, data_ref, merged_ref, kept_ref, sent_ref, rows_ref, *, species, rows_x, parts
):
    gram = gram_ref[...]
    current = start_ref[...]
    for repeat in range(ITERS):
        current = orthonormal_rows(mm(current, gram, NN))
    rank = current.shape[0]
    rows_ref[...] = current
    quarter = rank // 4
    order = [r for c in range(4) for r in range(rank) if (r >> 3 & 1) * 2 + (r >> 1 & 1) == c]
    current = halves(jnp.concatenate([rows_ref[r : r + 1, :] for r in order], axis=0))
    for s in range(species):
        product = mm3(current, halves(fibre(data_ref, s, species, rows_x, parts)), NN)
        for c in range(4):
            merged_ref[(c * species + s) * quarter : (c * species + s + 1) * quarter, :] = product[
                c * quarter : (c + 1) * quarter
            ]
    merged = merged_ref[...]
    flipped = halves(merged.T)
    merged = halves(merged)
    blocks = []
    for i in range(parts):
        cut = slice(i * LANES, (i + 1) * LANES)
        product = mm3([x[cut] for x in flipped], [x[:, i * LANES :] for x in merged], NN)
        blocks += [product[:, j * LANES : (j + 1) * LANES] for j in range(parts - i)]
    count = len(blocks) // 2
    first = lax.axis_index("gc") == 0
    for i in range(count):
        rows = slice(i * LANES, (i + 1) * LANES)
        kept_ref[rows, :] = jnp.where(first, blocks[i], blocks[count + i])
        sent_ref[rows, :] = jnp.where(first, blocks[count + i], blocks[i])


def symmetric_of(core, own_ref, other_ref, parts):
    pairs = (own_ref, other_ref), (other_ref, own_ref)
    blocks = []
    for first, second in pairs:
        for i in range(own_ref.shape[0] // LANES):
            rows = slice(i * LANES, (i + 1) * LANES)
            blocks.append(jnp.where(core == 0, first[rows, :], second[rows, :]))
    upper = {}
    for i in range(parts):
        for j in range(i, parts):
            upper[i, j] = blocks[len(upper)]
    lines = [[upper[i, j] if i <= j else upper[j, i].T for j in range(parts)] for i in range(parts)]
    return jnp.concatenate([jnp.concatenate(line, axis=1) for line in lines], axis=0)


def third_kernel(own_ref, other_ref, start_ref, merged_ref, out_ref, rows_ref, *, parts):
    gram = halves(symmetric_of(lax.axis_index("gc"), own_ref, other_ref, parts))
    current = start_ref[...]
    for repeat in range(ITERS):
        current = orthonormal_rows(mm3(halves(current), gram, NN))
    rows_ref[...] = mm3(halves(current), halves(merged_ref[...]), NT)
    quarter = LANES // 4
    groups = [rows_ref[pl.ds(e, rows_ref.shape[0] // 4, stride=4), :] for e in range(4)]
    group_id = lax.broadcasted_iota(jnp.int32, groups[0].shape, 1) // quarter
    for k in range(out_ref.shape[3]):
        for h in range(out_ref.shape[1]):
            c = k * 2 + h
            piece = pltpu.roll(groups[0], (4 - c) % 4 * quarter, 1) if c else groups[0]
            for e in range(1, 4):
                shift = (e - c) % 4 * quarter
                piece = jnp.where(group_id == e, pltpu.roll(groups[e], shift, 1) if shift else groups[e], piece)
            piece = jnp.concatenate([piece[0:2], piece[4:6], piece[2:4], piece[6:8]], axis=0)
            for i in range(out_ref.shape[0]):
                for j in range(out_ref.shape[2]):
                    for w in range(out_ref.shape[4]):
                        out_ref[i, h, j, k, w] = piece


def columns_of(own_ref, other_ref, parts):
    size = own_ref.shape[0] // parts
    return jnp.concatenate(
        [
            jnp.concatenate([ref[pl.ds(q, size, stride=parts), :] for q in range(parts)], axis=1)
            for ref in (own_ref, other_ref)
        ],
        axis=0,
    )


def spread(out_ref, wide):
    for i in range(out_ref.shape[0]):
        out_ref[i] = wide


def start_third_kernel(start_ref, own_ref, other_ref, out_ref, high_ref, low_ref, *, parts):
    data = halves(columns_of(own_ref, other_ref, parts))
    high_ref[...], low_ref[...] = data
    inner = mm3(halves(start_ref[...]), data, NN)
    spread(out_ref, mm3(halves(inner), data, NT))


def total_of(parts_ref):
    total = parts_ref[0]
    for i in range(1, parts_ref.shape[0]):
        total = total + parts_ref[i]
    return total


def step_third_kernel(parts_ref, high_ref, low_ref, out_ref):
    current = orthonormal_rows(total_of(parts_ref))
    data = high_ref[...], low_ref[...]
    inner = mm3(halves(current), data, NN)
    spread(out_ref, mm3(halves(inner), data, NT))


def core_kernel(parts_ref, high_ref, low_ref, out_ref, rows_ref):
    current = halves(orthonormal_rows(total_of(parts_ref)))
    block = lax.axis_index("gw") * 2 + lax.axis_index("gc")
    cut = pl.ds(pl.multiple_of(block * LANES, LANES), LANES)
    rows_ref[...] = mm3(current, (high_ref[:, cut], low_ref[:, cut]), NN).T
    at = lax.axis_index("gu") * 16 + lax.axis_index("gv") * 4 + lax.axis_index("gh") * 2
    for e in range(out_ref.shape[1]):
        for b in range(out_ref.shape[0]):
            out_ref[b, e, :] = rows_ref[at + e * (LANES // 4) + b, :]


def call(kernel, out_shape, *args, scratch=(), in_hbm=0):
    vmem = pl.BlockSpec(memory_space=pltpu.VMEM)
    hbm = pl.BlockSpec(memory_space=pltpu.HBM)
    return pl.pallas_call(
        kernel,
        out_shape=out_shape,
        in_specs=[hbm] * in_hbm + [vmem] * (len(args) - in_hbm),
        out_specs=jax.tree.map(lambda _: vmem, out_shape),
        compiler_params=pltpu.CompilerParams(vmem_limit_bytes=None if in_hbm else VMEM_BYTES),
        scratch_shapes=[pltpu.VMEM(s, jnp.float32) if isinstance(s, tuple) else s for s in scratch],
    )(*args[:in_hbm], *[pltpu.with_memory_space_constraint(a, pltpu.VMEM) for a in args[in_hbm:]])


def vm(*shape, dtype=jnp.float32):
    return pltpu.VMEM(shape, dtype)


def swap(pieces, axes):
    return lax.all_to_all(pieces, axes, split_axis=0, concat_axis=0, tiled=True)


def copies(piece, axes):
    return jnp.broadcast_to(piece, (lax.axis_size(axes),) + piece.shape)


def shards(field, brick_order, start_first, start_second, start_third):
    species, rows_here, cells_y, cells_z = field.shape
    rows_x, rank_one = start_first.shape
    full_y, rank_two = start_second.shape
    rank_three = start_third.shape[1]
    brick_len = cells_z // brick_order.shape[0]
    merged_rows = species * rank_one
    devices = lax.axis_size(ORDER)
    chips = lax.axis_size(CHIPS)
    parts_y = full_y // LANES
    exchange = [(0, 1), (1, 0)]

    sent, start_first, start_second, start_third = call(
        functools.partial(send_field_kernel, brick_len=brick_len),
        (vm(cells_z * species, cells_y), vm(rank_one, rows_x), vm(rank_two, full_y), vm(rank_three, cells_z)),
        brick_order,
        field.reshape(species, cells_y, cells_z),
        start_first.T,
        start_second.T,
        start_third.T,
        scratch=[
            (species, cells_y, cells_z),
            (rank_three, cells_z),
            (cells_z, rank_three),
            (cells_z, rank_three),
            pltpu.SMEM(brick_order.shape, jnp.int32),
            pltpu.SemaphoreType.DMA((species,)),
            pltpu.SemaphoreType.DMA((4,)),
        ],
        in_hbm=5,
    )
    data = swap(sent.reshape(devices, species, cells_y), ORDER).reshape(devices * species, cells_y)

    gram = call(
        functools.partial(gram_first_kernel, species=species, rows_x=rows_x, parts=parts_y), vm(rows_x, rows_x), data
    )
    gram = jnp.sum(swap(gram.reshape(lax.axis_size(CLOSE), -1, rows_x), CLOSE), axis=0)
    gram = jnp.sum(swap(copies(gram, FAR), FAR), axis=0)
    gram = swap(copies(gram, CLOSE), CLOSE).reshape(rows_x, rows_x)

    merged, kept, sent = call(
        functools.partial(second_kernel, species=species, rows_x=rows_x, parts=parts_y),
        (vm(merged_rows, full_y),) + (vm(parts_y * (parts_y + 1) // 4 * LANES, LANES),) * 2,
        gram,
        start_first,
        data,
        scratch=[(rank_one, rows_x)],
    )
    gram = kept + lax.ppermute(sent, "gc", exchange)
    gram = jnp.sum(swap(gram.reshape(lax.axis_size(BLOCK), -1, LANES), BLOCK), axis=0)
    gram = jnp.sum(swap(copies(gram, BEYOND), BEYOND), axis=0)
    own = swap(copies(gram, BLOCK), BLOCK).reshape(-1, LANES)
    other = lax.ppermute(own, "gc", exchange)

    sent = call(
        functools.partial(third_kernel, parts=parts_y),
        vm(lax.axis_size("gh"), lax.axis_size("gl"), lax.axis_size(("gu", "gv")), lax.axis_size("gk"), 2, 8, LANES),
        own,
        other,
        start_second,
        merged,
        scratch=[(rank_two, merged_rows)],
    )
    own = swap(sent.reshape(chips, 4, LANES), CHIPS).reshape(chips * 4, LANES)
    other = lax.ppermute(own, "gc", exchange)

    spread_shape = vm(lax.axis_size(NEAR), rank_three, cells_z)
    cut = vm(cells_z, 4 * LANES, dtype=jnp.bfloat16)
    pieces, high, low = call(
        functools.partial(start_third_kernel, parts=4),
        (spread_shape, cut, cut),
        start_third,
        own,
        other,
    )
    for repeat in range(ITERS - 1):
        pieces = call(step_third_kernel, spread_shape, swap(pieces, NEAR), high, low)
    return call(
        core_kernel,
        jax.ShapeDtypeStruct((2, 4, rank_three), jnp.float32),
        swap(pieces, NEAR),
        high,
        low,
        scratch=[(merged_rows, rank_three)],
    )


def solution(mesh):
    gx, gy, gz = mesh.devices.shape
    fine = Mesh(mesh.devices.reshape(2, gx // 4, 2, 2, gy // 2, gz // 4, 2, 2), FINE)
    in_specs = (P(None, ("gu", "gv", "gk", "gw", "gp", "gc"), ("gh", "gl"), None), P(), P(), P(), P())
    out_specs = P(("gu", "gv", "gk", "gh", "gl"), ("gw", "gp", "gc"), None)
    return jax.shard_map(shards, mesh=fine, in_specs=in_specs, out_specs=out_specs, check_vma=False)
```

```python
import functools

import jax
import jax.numpy as jnp
from jax import lax
from jax.experimental import pallas as pl
from jax.experimental.pallas import tpu as pltpu
from jax.sharding import Mesh, PartitionSpec as P

ITERS = 2
LANES = 128
PANEL = 16
VMEM_BYTES = 20 << 20
FINE = ("gu", "gv", "gk", "gh", "gl", "gw", "gp", "gc")
CHIPS = ("gh", "gl", "gu", "gv", "gk", "gw", "gp")
ORDER = CHIPS + ("gc",)
NEAR = ("gl", "gk", "gp")
CLOSE = ("gw", "gl", "gp", "gc")
FAR = ("gh", "gu", "gv", "gk")
BLOCK = ("gw", "gk", "gp", "gl")
BEYOND = ("gv", "gu", "gh")

highest = lax.Precision.HIGHEST
NN = ((1,), (0,))
NT = ((1,), (1,))
TN = ((0,), (0,))


def mm(a, b, dims):
    return lax.dot_general(a, b, (dims, ((), ())), precision=highest, preferred_element_type=jnp.float32)


def halves(x):
    high = x.astype(jnp.bfloat16)
    return high, (x - high.astype(jnp.float32)).astype(jnp.bfloat16)


def mm3(a, b, dims):
    def dot(x, y):
        return lax.dot_general(x, y, (dims, ((), ())), preferred_element_type=jnp.float32)

    size = a[0].shape[0]
    both = dot(jnp.concatenate(a, axis=0), b[0])
    return both[:size] + (both[size:] + dot(a[0], b[1]))


def orthonormal_rows(wide):
    rank = wide.shape[0]
    inner = mm(wide, wide, NT)
    shape = (rank, rank)
    row_id = lax.broadcasted_iota(jnp.int32, shape, 0)
    inverse = (row_id == lax.broadcasted_iota(jnp.int32, shape, 1)).astype(jnp.float32)
    pivots = jnp.ones(shape, jnp.float32)
    for start in range(0, rank, PANEL):
        columns = [jnp.broadcast_to(inner[:, start + j : start + j + 1], shape) for j in range(PANEL)]
        for j in range(PANEL):
            k = start + j
            pivot = jnp.broadcast_to(columns[j][k : k + 1, :], shape)
            pivots = jnp.where(row_id == k, pivot, pivots)
            if k == rank - 1:
                break
            factor = jnp.where(row_id > k, columns[j] * (1.0 / pivot), 0.0)
            for i in range(j + 1, PANEL):
                columns[i] = columns[i] - factor * columns[i][k : k + 1, :]
            if start + PANEL < rank:
                inner = inner - factor * inner[k : k + 1, :]
            inverse = inverse - factor * inverse[k : k + 1, :]
    return mm(inverse * (1.0 / jnp.sqrt(pivots)), wide, NN)


def send_field_kernel(
    order_hbm, field_hbm, first_hbm, second_hbm, third_hbm, out_ref, first_ref, second_ref, third_ref, field_ref,
    raw_ref, rows_ref, placed_ref, order_ref, sems, start_sems, *, brick_len
):
    species, cells_y, cells_z = field_hbm.shape
    loads = [pltpu.make_async_copy(field_hbm.at[s], field_ref.at[s], sems.at[s]) for s in range(species)]
    pairs = (order_hbm, order_ref), (third_hbm, raw_ref), (second_hbm, second_ref), (first_hbm, first_ref)
    starts = [pltpu.make_async_copy(source, target, start_sems.at[i]) for i, (source, target) in enumerate(pairs)]
    for load in starts[:2] + loads + starts[2:]:
        load.start()
    starts[0].wait()
    lane = lax.broadcasted_iota(jnp.int32, (1, cells_z), 1)
    brick = lane // brick_len
    place = jnp.zeros((1, cells_z), jnp.int32)
    for b in range(cells_z // brick_len):
        place = jnp.where(brick == b, order_ref[b] * brick_len, place)
    grid_z = (place + lane % brick_len).astype(jnp.float32)
    taper = 0.5 + 1.5 * grid_z / (cells_z - 1)
    starts[1].wait()
    rows_ref[...] = raw_ref[...].T
    for b in range(cells_z // brick_len):
        at = pl.multiple_of(order_ref[b] * brick_len, brick_len)
        placed_ref[b * brick_len : (b + 1) * brick_len, :] = rows_ref[pl.ds(at, brick_len), :]
    core = lax.axis_index("gc")
    half = cells_z // 2
    third_ref[:, :half] = placed_ref[pl.ds(core, half, stride=2), :].T
    third_ref[:, half:] = placed_ref[pl.ds(1 - core, half, stride=2), :].T
    for s in range(species):
        loads[s].wait()
        for j in range(cells_z // LANES):
            cut = slice(j * LANES, (j + 1) * LANES)
            block = field_ref[s, :, cut] * taper[:, cut]
            out_ref[pl.ds(j * LANES * species + s, LANES, stride=species), :] = block.T
    for load in starts[2:]:
        load.wait()


def fibre(ref, s, species, rows_x, parts):
    return jnp.concatenate(
        [ref[pl.ds(yq * rows_x * species + s, rows_x, stride=species), :] for yq in range(parts)], axis=1
    )


def gram_first_kernel(data_ref, out_ref, *, species, rows_x, parts):
    total = jnp.zeros(out_ref.shape, jnp.float32)
    for s in range(species):
        cut = halves(fibre(data_ref, s, species, rows_x, parts))
        total = total + mm3(cut, cut, NT)
    out_ref[...] = total


def second_kernel(
    gram_ref, start_ref, data_ref, merged_ref, kept_ref, sent_ref, rows_ref, *, species, rows_x, parts
):
    gram = gram_ref[...]
    current = start_ref[...]
    for repeat in range(ITERS):
        current = orthonormal_rows(mm(current, gram, NN))
    rank = current.shape[0]
    rows_ref[...] = current
    quarter = rank // 4
    order = [r for c in range(4) for r in range(rank) if (r >> 3 & 1) * 2 + (r >> 1 & 1) == c]
    current = halves(jnp.concatenate([rows_ref[r : r + 1, :] for r in order], axis=0))
    for s in range(species):
        product = mm3(current, halves(fibre(data_ref, s, species, rows_x, parts)), NN)
        for c in range(4):
            merged_ref[(c * species + s) * quarter : (c * species + s + 1) * quarter, :] = product[
                c * quarter : (c + 1) * quarter
            ]
    merged = merged_ref[...]
    flipped = halves(merged.T)
    merged = halves(merged)
    blocks = []
    for i in range(parts):
        cut = slice(i * LANES, (i + 1) * LANES)
        product = mm3([x[cut] for x in flipped], [x[:, i * LANES :] for x in merged], NN)
        blocks += [product[:, j * LANES : (j + 1) * LANES] for j in range(parts - i)]
    count = len(blocks) // 2
    first = lax.axis_index("gc") == 0
    for i in range(count):
        rows = slice(i * LANES, (i + 1) * LANES)
        kept_ref[rows, :] = jnp.where(first, blocks[i], blocks[count + i])
        sent_ref[rows, :] = jnp.where(first, blocks[count + i], blocks[i])


def symmetric_of(core, own_ref, other_ref, parts):
    pairs = (own_ref, other_ref), (other_ref, own_ref)
    blocks = []
    for first, second in pairs:
        for i in range(own_ref.shape[0] // LANES):
            rows = slice(i * LANES, (i + 1) * LANES)
            blocks.append(jnp.where(core == 0, first[rows, :], second[rows, :]))
    upper = {}
    for i in range(parts):
        for j in range(i, parts):
            upper[i, j] = blocks[len(upper)]
    lines = [[upper[i, j] if i <= j else upper[j, i].T for j in range(parts)] for i in range(parts)]
    return jnp.concatenate([jnp.concatenate(line, axis=1) for line in lines], axis=0)


def third_kernel(own_ref, other_ref, start_ref, merged_ref, out_ref, rows_ref, *, parts):
    gram = halves(symmetric_of(lax.axis_index("gc"), own_ref, other_ref, parts))
    current = start_ref[...]
    for repeat in range(ITERS):
        current = orthonormal_rows(mm3(halves(current), gram, NN))
    rows_ref[...] = mm3(halves(current), halves(merged_ref[...]), NT)
    quarter = LANES // 4
    groups = [rows_ref[pl.ds(e, rows_ref.shape[0] // 4, stride=4), :] for e in range(4)]
    group_id = lax.broadcasted_iota(jnp.int32, groups[0].shape, 1) // quarter
    for k in range(out_ref.shape[3]):
        for h in range(out_ref.shape[1]):
            c = k * 2 + h
            piece = pltpu.roll(groups[0], (4 - c) % 4 * quarter, 1) if c else groups[0]
            for e in range(1, 4):
                shift = (e - c) % 4 * quarter
                piece = jnp.where(group_id == e, pltpu.roll(groups[e], shift, 1) if shift else groups[e], piece)
            piece = jnp.concatenate([piece[0:2], piece[4:6], piece[2:4], piece[6:8]], axis=0)
            for i in range(out_ref.shape[0]):
                for j in range(out_ref.shape[2]):
                    for w in range(out_ref.shape[4]):
                        out_ref[i, h, j, k, w] = piece


def columns_of(own_ref, other_ref, parts):
    size = own_ref.shape[0] // parts
    return jnp.concatenate(
        [
            jnp.concatenate([ref[pl.ds(q, size, stride=parts), :] for q in range(parts)], axis=1)
            for ref in (own_ref, other_ref)
        ],
        axis=0,
    )


def spread(out_ref, wide):
    for i in range(out_ref.shape[0]):
        out_ref[i] = wide


def start_third_kernel(start_ref, own_ref, other_ref, out_ref, high_ref, low_ref, *, parts):
    data = halves(columns_of(own_ref, other_ref, parts))
    high_ref[...], low_ref[...] = data
    inner = mm3(halves(start_ref[...]), data, NN)
    spread(out_ref, mm3(halves(inner), data, NT))


def total_of(parts_ref):
    total = parts_ref[0]
    for i in range(1, parts_ref.shape[0]):
        total = total + parts_ref[i]
    return total


def step_third_kernel(parts_ref, high_ref, low_ref, out_ref):
    current = orthonormal_rows(total_of(parts_ref))
    data = high_ref[...], low_ref[...]
    inner = mm3(halves(current), data, NN)
    spread(out_ref, mm3(halves(inner), data, NT))


def core_kernel(parts_ref, high_ref, low_ref, out_ref, rows_ref):
    current = halves(orthonormal_rows(total_of(parts_ref)))
    block = lax.axis_index("gw") * 2 + lax.axis_index("gc")
    cut = pl.ds(pl.multiple_of(block * LANES, LANES), LANES)
    rows_ref[...] = mm3(current, (high_ref[:, cut], low_ref[:, cut]), NN).T
    at = lax.axis_index("gu") * 16 + lax.axis_index("gv") * 4 + lax.axis_index("gh") * 2
    for e in range(out_ref.shape[1]):
        for b in range(out_ref.shape[0]):
            out_ref[b, e, :] = rows_ref[at + e * (LANES // 4) + b, :]


def call(kernel, out_shape, *args, scratch=(), in_hbm=0):
    vmem = pl.BlockSpec(memory_space=pltpu.VMEM)
    hbm = pl.BlockSpec(memory_space=pltpu.HBM)
    return pl.pallas_call(
        kernel,
        out_shape=out_shape,
        in_specs=[hbm] * in_hbm + [vmem] * (len(args) - in_hbm),
        out_specs=jax.tree.map(lambda _: vmem, out_shape),
        compiler_params=pltpu.CompilerParams(vmem_limit_bytes=None if in_hbm else VMEM_BYTES),
        scratch_shapes=[pltpu.VMEM(s, jnp.float32) if isinstance(s, tuple) else s for s in scratch],
    )(*args[:in_hbm], *[pltpu.with_memory_space_constraint(a, pltpu.VMEM) for a in args[in_hbm:]])


def vm(*shape, dtype=jnp.float32):
    return pltpu.VMEM(shape, dtype)


def swap(pieces, axes):
    return lax.all_to_all(pieces, axes, split_axis=0, concat_axis=0, tiled=True)


def copies(piece, axes):
    return jnp.broadcast_to(piece, (lax.axis_size(axes),) + piece.shape)


def shards(field, brick_order, start_first, start_second, start_third):
    species, rows_here, cells_y, cells_z = field.shape
    rows_x, rank_one = start_first.shape
    full_y, rank_two = start_second.shape
    rank_three = start_third.shape[1]
    brick_len = cells_z // brick_order.shape[0]
    merged_rows = species * rank_one
    devices = lax.axis_size(ORDER)
    chips = lax.axis_size(CHIPS)
    parts_y = full_y // LANES
    exchange = [(0, 1), (1, 0)]

    sent, start_first, start_second, start_third = call(
        functools.partial(send_field_kernel, brick_len=brick_len),
        (vm(cells_z * species, cells_y), vm(rank_one, rows_x), vm(rank_two, full_y), vm(rank_three, cells_z)),
        brick_order,
        field.reshape(species, cells_y, cells_z),
        start_first.T,
        start_second.T,
        start_third.T,
        scratch=[
            (species, cells_y, cells_z),
            (rank_three, cells_z),
            (cells_z, rank_three),
            (cells_z, rank_three),
            pltpu.SMEM(brick_order.shape, jnp.int32),
            pltpu.SemaphoreType.DMA((species,)),
            pltpu.SemaphoreType.DMA((4,)),
        ],
        in_hbm=5,
    )
    data = swap(sent.reshape(devices, species, cells_y), ORDER).reshape(devices * species, cells_y)

    gram = call(
        functools.partial(gram_first_kernel, species=species, rows_x=rows_x, parts=parts_y), vm(rows_x, rows_x), data
    )
    gram = jnp.sum(swap(gram.reshape(lax.axis_size(CLOSE), -1, rows_x), CLOSE), axis=0)
    gram = jnp.sum(swap(copies(gram, FAR), FAR), axis=0)
    gram = swap(copies(gram, CLOSE), CLOSE).reshape(rows_x, rows_x)

    merged, kept, sent = call(
        functools.partial(second_kernel, species=species, rows_x=rows_x, parts=parts_y),
        (vm(merged_rows, full_y),) + (vm(parts_y * (parts_y + 1) // 4 * LANES, LANES),) * 2,
        gram,
        start_first,
        data,
        scratch=[(rank_one, rows_x)],
    )
    gram = kept + lax.ppermute(sent, "gc", exchange)
    gram = jnp.sum(swap(gram.reshape(lax.axis_size(BLOCK), -1, LANES), BLOCK), axis=0)
    gram = jnp.sum(swap(copies(gram, BEYOND), BEYOND), axis=0)
    own = swap(copies(gram, BLOCK), BLOCK).reshape(-1, LANES)
    other = lax.ppermute(own, "gc", exchange)

    sent = call(
        functools.partial(third_kernel, parts=parts_y),
        vm(lax.axis_size("gh"), lax.axis_size("gl"), lax.axis_size(("gu", "gv")), lax.axis_size("gk"), 2, 8, LANES),
        own,
        other,
        start_second,
        merged,
        scratch=[(rank_two, merged_rows)],
    )
    own = swap(sent.reshape(chips, 4, LANES), CHIPS).reshape(chips * 4, LANES)
    other = lax.ppermute(own, "gc", exchange)

    spread_shape = vm(lax.axis_size(NEAR), rank_three, cells_z)
    cut = vm(cells_z, 4 * LANES, dtype=jnp.bfloat16)
    pieces, high, low = call(
        functools.partial(start_third_kernel, parts=4),
        (spread_shape, cut, cut),
        start_third,
        own,
        other,
    )
    for repeat in range(ITERS - 1):
        pieces = call(step_third_kernel, spread_shape, swap(pieces, NEAR), high, low)
    return call(
        core_kernel,
        jax.ShapeDtypeStruct((2, 4, rank_three), jnp.float32),
        swap(pieces, NEAR),
        high,
        low,
        scratch=[(merged_rows, rank_three)],
    )


def solution(mesh):
    gx, gy, gz = mesh.devices.shape
    fine = Mesh(mesh.devices.reshape(2, gx // 4, 2, 2, gy // 2, gz // 4, 2, 2), FINE)
    in_specs = (P(None, ("gu", "gv", "gk", "gw", "gp", "gc"), ("gh", "gl"), None), P(), P(), P(), P())
    out_specs = P(("gu", "gv", "gk", "gh", "gl"), ("gw", "gp", "gc"), None)
    return jax.shard_map(shards, mesh=fine, in_specs=in_specs, out_specs=out_specs, check_vma=False)
```

```python
import functools

import jax
import jax.numpy as jnp
from jax import lax
from jax.experimental import pallas as pl
from jax.experimental.pallas import tpu as pltpu
from jax.sharding import Mesh, PartitionSpec as P

ITERS = 2
LANES = 128
PANEL = 16
VMEM_BYTES = 20 << 20
FINE = ("gu", "gv", "gk", "gh", "gl", "gw", "gp", "gc")
CHIPS = ("gh", "gl", "gu", "gv", "gk", "gw", "gp")
ORDER = CHIPS + ("gc",)
NEAR = ("gl", "gk", "gp")
CLOSE = ("gw", "gl", "gp", "gc")
FAR = ("gh", "gu", "gv", "gk")
BLOCK = ("gw", "gk", "gp", "gl")
BEYOND = ("gv", "gu", "gh")

highest = lax.Precision.HIGHEST
NN = ((1,), (0,))
NT = ((1,), (1,))
TN = ((0,), (0,))


def mm(a, b, dims):
    return lax.dot_general(a, b, (dims, ((), ())), precision=highest, preferred_element_type=jnp.float32)


def halves(x):
    high = x.astype(jnp.bfloat16)
    return high, (x - high.astype(jnp.float32)).astype(jnp.bfloat16)


def mm3(a, b, dims):
    def dot(x, y):
        return lax.dot_general(x, y, (dims, ((), ())), preferred_element_type=jnp.float32)

    size = a[0].shape[0]
    both = dot(jnp.concatenate(a, axis=0), b[0])
    return both[:size] + (both[size:] + dot(a[0], b[1]))


def orthonormal_rows(wide):
    rank = wide.shape[0]
    inner = mm(wide, wide, NT)
    shape = (rank, rank)
    row_id = lax.broadcasted_iota(jnp.int32, shape, 0)
    inverse = (row_id == lax.broadcasted_iota(jnp.int32, shape, 1)).astype(jnp.float32)
    pivots = jnp.ones(shape, jnp.float32)
    for start in range(0, rank, PANEL):
        columns = [jnp.broadcast_to(inner[:, start + j : start + j + 1], shape) for j in range(PANEL)]
        for j in range(PANEL):
            k = start + j
            pivot = jnp.broadcast_to(columns[j][k : k + 1, :], shape)
            pivots = jnp.where(row_id == k, pivot, pivots)
            if k == rank - 1:
                break
            factor = jnp.where(row_id > k, columns[j] * (1.0 / pivot), 0.0)
            for i in range(j + 1, PANEL):
                columns[i] = columns[i] - factor * columns[i][k : k + 1, :]
            if start + PANEL < rank:
                inner = inner - factor * inner[k : k + 1, :]
            inverse = inverse - factor * inverse[k : k + 1, :]
    return mm(inverse * (1.0 / jnp.sqrt(pivots)), wide, NN)


def send_field_kernel(
    order_hbm, field_hbm, first_hbm, second_hbm, out_ref, first_ref, second_ref, field_ref, order_ref, sems, start_sems, *, brick_len
):
    species, cells_y, cells_z = field_hbm.shape
    loads = [pltpu.make_async_copy(field_hbm.at[s], field_ref.at[s], sems.at[s]) for s in range(species)]
    pairs = (order_hbm, order_ref), (second_hbm, second_ref), (first_hbm, first_ref)
    starts = [pltpu.make_async_copy(source, target, start_sems.at[i]) for i, (source, target) in enumerate(pairs)]
    for load in starts[:1] + loads + starts[1:]:
        load.start()
    starts[0].wait()
    lane = lax.broadcasted_iota(jnp.int32, (1, cells_z), 1)
    brick = lane // brick_len
    place = jnp.zeros((1, cells_z), jnp.int32)
    for b in range(cells_z // brick_len):
        place = jnp.where(brick == b, order_ref[b] * brick_len, place)
    grid_z = (place + lane % brick_len).astype(jnp.float32)
    taper = 0.5 + 1.5 * grid_z / (cells_z - 1)
    for s in range(species):
        loads[s].wait()
        for j in range(cells_z // LANES):
            cut = slice(j * LANES, (j + 1) * LANES)
            block = field_ref[s, :, cut] * taper[:, cut]
            out_ref[pl.ds(j * LANES * species + s, LANES, stride=species), :] = block.T
    for load in starts[1:]:
        load.wait()


def place_third_kernel(order_hbm, third_hbm, third_ref, raw_ref, rows_ref, placed_ref, order_ref, sems, *, brick_len):
    loads = [
        pltpu.make_async_copy(source, target, sems.at[i])
        for i, (source, target) in enumerate(((order_hbm, order_ref), (third_hbm, raw_ref)))
    ]
    for load in loads:
        load.start()
    for load in loads:
        load.wait()
    size = rows_ref.shape[0]
    rows_ref[...] = raw_ref[...].T
    for b in range(size // brick_len):
        at = pl.multiple_of(order_ref[b] * brick_len, brick_len)
        placed_ref[b * brick_len : (b + 1) * brick_len, :] = rows_ref[pl.ds(at, brick_len), :]
    core = lax.axis_index("gc")
    half = size // 2
    third_ref[:, :half] = placed_ref[pl.ds(core, half, stride=2), :].T
    third_ref[:, half:] = placed_ref[pl.ds(1 - core, half, stride=2), :].T


def fibre(ref, s, species, rows_x, parts):
    return jnp.concatenate(
        [ref[pl.ds(yq * rows_x * species + s, rows_x, stride=species), :] for yq in range(parts)], axis=1
    )


def gram_first_kernel(data_ref, out_ref, *, species, rows_x, parts):
    total = jnp.zeros(out_ref.shape, jnp.float32)
    for s in range(species):
        cut = halves(fibre(data_ref, s, species, rows_x, parts))
        total = total + mm3(cut, cut, NT)
    out_ref[...] = total


def second_kernel(
    gram_ref, start_ref, data_ref, merged_ref, kept_ref, sent_ref, rows_ref, *, species, rows_x, parts
):
    gram = gram_ref[...]
    current = start_ref[...]
    for repeat in range(ITERS):
        current = orthonormal_rows(mm(current, gram, NN))
    rank = current.shape[0]
    rows_ref[...] = current
    quarter = rank // 4
    order = [r for c in range(4) for r in range(rank) if (r >> 3 & 1) * 2 + (r >> 1 & 1) == c]
    current = halves(jnp.concatenate([rows_ref[r : r + 1, :] for r in order], axis=0))
    for s in range(species):
        product = mm3(current, halves(fibre(data_ref, s, species, rows_x, parts)), NN)
        for c in range(4):
            merged_ref[(c * species + s) * quarter : (c * species + s + 1) * quarter, :] = product[
                c * quarter : (c + 1) * quarter
            ]
    merged = merged_ref[...]
    flipped = halves(merged.T)
    merged = halves(merged)
    blocks = []
    for i in range(parts):
        cut = slice(i * LANES, (i + 1) * LANES)
        product = mm3([x[cut] for x in flipped], [x[:, i * LANES :] for x in merged], NN)
        blocks += [product[:, j * LANES : (j + 1) * LANES] for j in range(parts - i)]
    count = len(blocks) // 2
    first = lax.axis_index("gc") == 0
    for i in range(count):
        rows = slice(i * LANES, (i + 1) * LANES)
        kept_ref[rows, :] = jnp.where(first, blocks[i], blocks[count + i])
        sent_ref[rows, :] = jnp.where(first, blocks[count + i], blocks[i])


def symmetric_of(core, own_ref, other_ref, parts):
    pairs = (own_ref, other_ref), (other_ref, own_ref)
    blocks = []
    for first, second in pairs:
        for i in range(own_ref.shape[0] // LANES):
            rows = slice(i * LANES, (i + 1) * LANES)
            blocks.append(jnp.where(core == 0, first[rows, :], second[rows, :]))
    upper = {}
    for i in range(parts):
        for j in range(i, parts):
            upper[i, j] = blocks[len(upper)]
    lines = [[upper[i, j] if i <= j else upper[j, i].T for j in range(parts)] for i in range(parts)]
    return jnp.concatenate([jnp.concatenate(line, axis=1) for line in lines], axis=0)


def third_kernel(own_ref, other_ref, start_ref, merged_ref, out_ref, rows_ref, *, parts):
    gram = halves(symmetric_of(lax.axis_index("gc"), own_ref, other_ref, parts))
    current = start_ref[...]
    for repeat in range(ITERS):
        current = orthonormal_rows(mm3(halves(current), gram, NN))
    rows_ref[...] = mm3(halves(current), halves(merged_ref[...]), NT)
    quarter = LANES // 4
    groups = [rows_ref[pl.ds(e, rows_ref.shape[0] // 4, stride=4), :] for e in range(4)]
    group_id = lax.broadcasted_iota(jnp.int32, groups[0].shape, 1) // quarter
    for k in range(out_ref.shape[3]):
        for h in range(out_ref.shape[1]):
            c = k * 2 + h
            piece = pltpu.roll(groups[0], (4 - c) % 4 * quarter, 1) if c else groups[0]
            for e in range(1, 4):
                shift = (e - c) % 4 * quarter
                piece = jnp.where(group_id == e, pltpu.roll(groups[e], shift, 1) if shift else groups[e], piece)
            piece = jnp.concatenate([piece[0:2], piece[4:6], piece[2:4], piece[6:8]], axis=0)
            for i in range(out_ref.shape[0]):
                for j in range(out_ref.shape[2]):
                    for w in range(out_ref.shape[4]):
                        out_ref[i, h, j, k, w] = piece


def columns_of(own_ref, other_ref, parts):
    size = own_ref.shape[0] // parts
    return jnp.concatenate(
        [
            jnp.concatenate([ref[pl.ds(q, size, stride=parts), :] for q in range(parts)], axis=1)
            for ref in (own_ref, other_ref)
        ],
        axis=0,
    )


def spread(out_ref, wide):
    for i in range(out_ref.shape[0]):
        out_ref[i] = wide


def start_third_kernel(start_ref, own_ref, other_ref, out_ref, high_ref, low_ref, *, parts):
    data = halves(columns_of(own_ref, other_ref, parts))
    high_ref[...], low_ref[...] = data
    inner = mm3(halves(start_ref[...]), data, NN)
    spread(out_ref, mm3(halves(inner), data, NT))


def total_of(parts_ref):
    total = parts_ref[0]
    for i in range(1, parts_ref.shape[0]):
        total = total + parts_ref[i]
    return total


def step_third_kernel(parts_ref, high_ref, low_ref, out_ref):
    current = orthonormal_rows(total_of(parts_ref))
    data = high_ref[...], low_ref[...]
    inner = mm3(halves(current), data, NN)
    spread(out_ref, mm3(halves(inner), data, NT))


def core_kernel(parts_ref, high_ref, low_ref, out_ref, rows_ref):
    current = halves(orthonormal_rows(total_of(parts_ref)))
    block = lax.axis_index("gw") * 2 + lax.axis_index("gc")
    cut = pl.ds(pl.multiple_of(block * LANES, LANES), LANES)
    rows_ref[...] = mm3(current, (high_ref[:, cut], low_ref[:, cut]), NN).T
    at = lax.axis_index("gu") * 16 + lax.axis_index("gv") * 4 + lax.axis_index("gh") * 2
    for e in range(out_ref.shape[1]):
        for b in range(out_ref.shape[0]):
            out_ref[b, e, :] = rows_ref[at + e * (LANES // 4) + b, :]


def call(kernel, out_shape, *args, scratch=(), in_hbm=0, limit=None):
    vmem = pl.BlockSpec(memory_space=pltpu.VMEM)
    hbm = pl.BlockSpec(memory_space=pltpu.HBM)
    return pl.pallas_call(
        kernel,
        out_shape=out_shape,
        in_specs=[hbm] * in_hbm + [vmem] * (len(args) - in_hbm),
        out_specs=jax.tree.map(lambda _: vmem, out_shape),
        compiler_params=pltpu.CompilerParams(vmem_limit_bytes=limit if in_hbm else VMEM_BYTES),
        scratch_shapes=[pltpu.VMEM(s, jnp.float32) if isinstance(s, tuple) else s for s in scratch],
    )(*args[:in_hbm], *[pltpu.with_memory_space_constraint(a, pltpu.VMEM) for a in args[in_hbm:]])


def vm(*shape, dtype=jnp.float32):
    return pltpu.VMEM(shape, dtype)


def swap(pieces, axes):
    return lax.all_to_all(pieces, axes, split_axis=0, concat_axis=0, tiled=True)


def copies(piece, axes):
    return jnp.broadcast_to(piece, (lax.axis_size(axes),) + piece.shape)


def shards(field, brick_order, start_first, start_second, start_third):
    species, rows_here, cells_y, cells_z = field.shape
    rows_x, rank_one = start_first.shape
    full_y, rank_two = start_second.shape
    rank_three = start_third.shape[1]
    brick_len = cells_z // brick_order.shape[0]
    merged_rows = species * rank_one
    devices = lax.axis_size(ORDER)
    chips = lax.axis_size(CHIPS)
    parts_y = full_y // LANES
    exchange = [(0, 1), (1, 0)]

    sent, start_first, start_second = call(
        functools.partial(send_field_kernel, brick_len=brick_len),
        (vm(cells_z * species, cells_y), vm(rank_one, rows_x), vm(rank_two, full_y)),
        brick_order,
        field.reshape(species, cells_y, cells_z),
        start_first.T,
        start_second.T,
        scratch=[
            (species, cells_y, cells_z),
            pltpu.SMEM(brick_order.shape, jnp.int32),
            pltpu.SemaphoreType.DMA((species,)),
            pltpu.SemaphoreType.DMA((3,)),
        ],
        in_hbm=4,
    )
    data = swap(sent.reshape(devices, species, cells_y), ORDER).reshape(devices * species, cells_y)

    gram = call(
        functools.partial(gram_first_kernel, species=species, rows_x=rows_x, parts=parts_y), vm(rows_x, rows_x), data
    )
    gram = jnp.sum(swap(gram.reshape(lax.axis_size(CLOSE), -1, rows_x), CLOSE), axis=0)
    gram = jnp.sum(swap(copies(gram, FAR), FAR), axis=0)
    gram = swap(copies(gram, CLOSE), CLOSE).reshape(rows_x, rows_x)

    merged, kept, sent = call(
        functools.partial(second_kernel, species=species, rows_x=rows_x, parts=parts_y),
        (vm(merged_rows, full_y),) + (vm(parts_y * (parts_y + 1) // 4 * LANES, LANES),) * 2,
        gram,
        start_first,
        data,
        scratch=[(rank_one, rows_x)],
    )
    swapped = lax.ppermute(sent, "gc", exchange)
    raw_third, kept = lax.optimization_barrier((start_third.T, kept))
    start_third = call(
        functools.partial(place_third_kernel, brick_len=brick_len),
        vm(rank_three, cells_z),
        brick_order,
        raw_third,
        scratch=[
            (rank_three, cells_z),
            (cells_z, rank_three),
            (cells_z, rank_three),
            pltpu.SMEM(brick_order.shape, jnp.int32),
            pltpu.SemaphoreType.DMA((2,)),
        ],
        in_hbm=2,
        limit=VMEM_BYTES,
    )
    kept, start_third = lax.optimization_barrier((kept, start_third))
    gram = kept + swapped
    gram = jnp.sum(swap(gram.reshape(lax.axis_size(BLOCK), -1, LANES), BLOCK), axis=0)
    gram = jnp.sum(swap(copies(gram, BEYOND), BEYOND), axis=0)
    own = swap(copies(gram, BLOCK), BLOCK).reshape(-1, LANES)
    other = lax.ppermute(own, "gc", exchange)

    sent = call(
        functools.partial(third_kernel, parts=parts_y),
        vm(lax.axis_size("gh"), lax.axis_size("gl"), lax.axis_size(("gu", "gv")), lax.axis_size("gk"), 2, 8, LANES),
        own,
        other,
        start_second,
        merged,
        scratch=[(rank_two, merged_rows)],
    )
    own = swap(sent.reshape(chips, 4, LANES), CHIPS).reshape(chips * 4, LANES)
    other = lax.ppermute(own, "gc", exchange)

    spread_shape = vm(lax.axis_size(NEAR), rank_three, cells_z)
    cut = vm(cells_z, 4 * LANES, dtype=jnp.bfloat16)
    pieces, high, low = call(
        functools.partial(start_third_kernel, parts=4),
        (spread_shape, cut, cut),
        start_third,
        own,
        other,
    )
    for repeat in range(ITERS - 1):
        pieces = call(step_third_kernel, spread_shape, swap(pieces, NEAR), high, low)
    return call(
        core_kernel,
        jax.ShapeDtypeStruct((2, 4, rank_three), jnp.float32),
        swap(pieces, NEAR),
        high,
        low,
        scratch=[(merged_rows, rank_three)],
    )


def solution(mesh):
    gx, gy, gz = mesh.devices.shape
    fine = Mesh(mesh.devices.reshape(2, gx // 4, 2, 2, gy // 2, gz // 4, 2, 2), FINE)
    in_specs = (P(None, ("gu", "gv", "gk", "gw", "gp", "gc"), ("gh", "gl"), None), P(), P(), P(), P())
    out_specs = P(("gu", "gv", "gk", "gh", "gl"), ("gw", "gp", "gc"), None)
    return jax.shard_map(shards, mesh=fine, in_specs=in_specs, out_specs=out_specs, check_vma=False)
```

```python
import functools

import jax
import jax.numpy as jnp
from jax import lax
from jax.experimental import pallas as pl
from jax.experimental.pallas import tpu as pltpu
from jax.sharding import Mesh, PartitionSpec as P

ITERS = 2
LANES = 128
PANEL = 16
VMEM_BYTES = 20 << 20
FINE = ("gu", "gv", "gk", "gh", "gl", "gw", "gp", "gc")
CHIPS = ("gh", "gl", "gu", "gv", "gk", "gw", "gp")
ORDER = CHIPS + ("gc",)
NEAR = ("gl", "gk", "gp")
CLOSE = ("gw", "gl", "gp", "gc")
FAR = ("gh", "gu", "gv", "gk")
BLOCK = ("gw", "gk", "gp", "gl")
BEYOND = ("gv", "gu", "gh")

highest = lax.Precision.HIGHEST
NN = ((1,), (0,))
NT = ((1,), (1,))
TN = ((0,), (0,))


def mm(a, b, dims):
    return lax.dot_general(a, b, (dims, ((), ())), precision=highest, preferred_element_type=jnp.float32)


def halves(x):
    high = x.astype(jnp.bfloat16)
    return high, (x - high.astype(jnp.float32)).astype(jnp.bfloat16)


def mm3(a, b, dims):
    def dot(x, y):
        return lax.dot_general(x, y, (dims, ((), ())), preferred_element_type=jnp.float32)

    size = a[0].shape[0]
    both = dot(jnp.concatenate(a, axis=0), b[0])
    return both[:size] + (both[size:] + dot(a[0], b[1]))


def orthonormal_rows(wide):
    rank = wide.shape[0]
    inner = mm(wide, wide, NT)
    shape = (rank, rank)
    row_id = lax.broadcasted_iota(jnp.int32, shape, 0)
    inverse = (row_id == lax.broadcasted_iota(jnp.int32, shape, 1)).astype(jnp.float32)
    pivots = jnp.ones(shape, jnp.float32)
    for start in range(0, rank, PANEL):
        columns = [jnp.broadcast_to(inner[:, start + j : start + j + 1], shape) for j in range(PANEL)]
        for j in range(PANEL):
            k = start + j
            pivot = jnp.broadcast_to(columns[j][k : k + 1, :], shape)
            pivots = jnp.where(row_id == k, pivot, pivots)
            if k == rank - 1:
                break
            factor = jnp.where(row_id > k, columns[j] * (1.0 / pivot), 0.0)
            for i in range(j + 1, PANEL):
                columns[i] = columns[i] - factor * columns[i][k : k + 1, :]
            if start + PANEL < rank:
                inner = inner - factor * inner[k : k + 1, :]
            inverse = inverse - factor * inverse[k : k + 1, :]
    return mm(inverse * (1.0 / jnp.sqrt(pivots)), wide, NN)


def send_field_kernel(
    order_hbm, field_hbm, first_hbm, second_hbm, out_ref, first_ref, second_ref, field_ref, order_ref, sems, start_sems, *, brick_len
):
    species, cells_y, cells_z = field_hbm.shape
    loads = [pltpu.make_async_copy(field_hbm.at[s], field_ref.at[s], sems.at[s]) for s in range(species)]
    pairs = (order_hbm, order_ref), (second_hbm, second_ref), (first_hbm, first_ref)
    starts = [pltpu.make_async_copy(source, target, start_sems.at[i]) for i, (source, target) in enumerate(pairs)]
    for load in starts[:1] + loads + starts[1:]:
        load.start()
    starts[0].wait()
    lane = lax.broadcasted_iota(jnp.int32, (1, cells_z), 1)
    brick = lane // brick_len
    place = jnp.zeros((1, cells_z), jnp.int32)
    for b in range(cells_z // brick_len):
        place = jnp.where(brick == b, order_ref[b] * brick_len, place)
    grid_z = (place + lane % brick_len).astype(jnp.float32)
    taper = 0.5 + 1.5 * grid_z / (cells_z - 1)
    for s in range(species):
        loads[s].wait()
        for j in range(cells_z // LANES):
            cut = slice(j * LANES, (j + 1) * LANES)
            block = field_ref[s, :, cut] * taper[:, cut]
            out_ref[pl.ds(j * LANES * species + s, LANES, stride=species), :] = block.T
    for load in starts[1:]:
        load.wait()


def place_third_kernel(order_hbm, third_hbm, third_ref, raw_ref, rows_ref, placed_ref, order_ref, sems, *, brick_len):
    loads = [
        pltpu.make_async_copy(source, target, sems.at[i])
        for i, (source, target) in enumerate(((order_hbm, order_ref), (third_hbm, raw_ref)))
    ]
    for load in loads:
        load.start()
    for load in loads:
        load.wait()
    size = rows_ref.shape[0]
    rows_ref[...] = raw_ref[...].T
    for b in range(size // brick_len):
        at = pl.multiple_of(order_ref[b] * brick_len, brick_len)
        placed_ref[b * brick_len : (b + 1) * brick_len, :] = rows_ref[pl.ds(at, brick_len), :]
    core = lax.axis_index("gc")
    half = size // 2
    third_ref[:, :half] = placed_ref[pl.ds(core, half, stride=2), :].T
    third_ref[:, half:] = placed_ref[pl.ds(1 - core, half, stride=2), :].T


def fibre(ref, s, species, rows_x, parts):
    return jnp.concatenate(
        [ref[pl.ds(yq * rows_x * species + s, rows_x, stride=species), :] for yq in range(parts)], axis=1
    )


def gram_first_kernel(data_ref, out_ref, *, species, rows_x, parts):
    total = jnp.zeros(out_ref.shape, jnp.float32)
    for s in range(species):
        cut = halves(fibre(data_ref, s, species, rows_x, parts))
        total = total + mm3(cut, cut, NT)
    out_ref[...] = total


def second_kernel(
    gram_ref, start_ref, data_ref, high_ref, low_ref, kept_ref, sent_ref, rows_ref, merged_ref, *, species, rows_x, parts
):
    gram = gram_ref[...]
    current = start_ref[...]
    for repeat in range(ITERS):
        current = orthonormal_rows(mm(current, gram, NN))
    rank = current.shape[0]
    rows_ref[...] = current
    quarter = rank // 4
    order = [r for c in range(4) for r in range(rank) if (r >> 3 & 1) * 2 + (r >> 1 & 1) == c]
    current = halves(jnp.concatenate([rows_ref[r : r + 1, :] for r in order], axis=0))
    for s in range(species):
        product = mm3(current, halves(fibre(data_ref, s, species, rows_x, parts)), NN)
        for c in range(4):
            merged_ref[(c * species + s) * quarter : (c * species + s + 1) * quarter, :] = product[
                c * quarter : (c + 1) * quarter
            ]
    merged = merged_ref[...]
    flipped = halves(merged.T)
    merged = halves(merged)
    high_ref[...], low_ref[...] = merged
    blocks = []
    for i in range(parts):
        cut = slice(i * LANES, (i + 1) * LANES)
        product = mm3([x[cut] for x in flipped], [x[:, i * LANES :] for x in merged], NN)
        blocks += [product[:, j * LANES : (j + 1) * LANES] for j in range(parts - i)]
    count = len(blocks) // 2
    first = lax.axis_index("gc") == 0
    for i in range(count):
        rows = slice(i * LANES, (i + 1) * LANES)
        kept_ref[rows, :] = jnp.where(first, blocks[i], blocks[count + i])
        sent_ref[rows, :] = jnp.where(first, blocks[count + i], blocks[i])


def symmetric_of(core, own_ref, other_ref, parts):
    pairs = (own_ref, other_ref), (other_ref, own_ref)
    blocks = []
    for first, second in pairs:
        for i in range(own_ref.shape[0] // LANES):
            rows = slice(i * LANES, (i + 1) * LANES)
            blocks.append(jnp.where(core == 0, first[rows, :], second[rows, :]))
    upper = {}
    for i in range(parts):
        for j in range(i, parts):
            upper[i, j] = blocks[len(upper)]
    lines = [[upper[i, j] if i <= j else upper[j, i].T for j in range(parts)] for i in range(parts)]
    return jnp.concatenate([jnp.concatenate(line, axis=1) for line in lines], axis=0)


def third_kernel(own_ref, other_ref, start_ref, high_ref, low_ref, out_ref, rows_ref, *, parts):
    gram = halves(symmetric_of(lax.axis_index("gc"), own_ref, other_ref, parts))
    current = start_ref[...]
    for repeat in range(ITERS):
        current = orthonormal_rows(mm3(halves(current), gram, NN))
    rows_ref[...] = mm3(halves(current), (high_ref[...], low_ref[...]), NT)
    quarter = LANES // 4
    groups = [rows_ref[pl.ds(e, rows_ref.shape[0] // 4, stride=4), :] for e in range(4)]
    group_id = lax.broadcasted_iota(jnp.int32, groups[0].shape, 1) // quarter
    for k in range(out_ref.shape[3]):
        for h in range(out_ref.shape[1]):
            c = k * 2 + h
            piece = pltpu.roll(groups[0], (4 - c) % 4 * quarter, 1) if c else groups[0]
            for e in range(1, 4):
                shift = (e - c) % 4 * quarter
                piece = jnp.where(group_id == e, pltpu.roll(groups[e], shift, 1) if shift else groups[e], piece)
            piece = jnp.concatenate([piece[0:2], piece[4:6], piece[2:4], piece[6:8]], axis=0)
            for i in range(out_ref.shape[0]):
                for j in range(out_ref.shape[2]):
                    for w in range(out_ref.shape[4]):
                        out_ref[i, h, j, k, w] = piece


def columns_of(ref, parts):
    size = ref.shape[0] // parts
    return jnp.concatenate([ref[pl.ds(q, size, stride=parts), :] for q in range(parts)], axis=1)


def own_third_kernel(own_ref, high_ref, low_ref, *, parts):
    high_ref[...], low_ref[...] = halves(columns_of(own_ref, parts))


def spread(out_ref, wide):
    for i in range(out_ref.shape[0]):
        out_ref[i] = wide


def start_third_kernel(start_ref, own_high_ref, own_low_ref, other_ref, out_ref, high_ref, low_ref, *, parts):
    high, low = halves(columns_of(other_ref, parts))
    data = jnp.concatenate([own_high_ref[...], high], axis=0), jnp.concatenate([own_low_ref[...], low], axis=0)
    high_ref[...], low_ref[...] = data
    inner = mm3(halves(start_ref[...]), data, NN)
    spread(out_ref, mm3(halves(inner), data, NT))


def total_of(parts_ref):
    total = parts_ref[0]
    for i in range(1, parts_ref.shape[0]):
        total = total + parts_ref[i]
    return total


def step_third_kernel(parts_ref, high_ref, low_ref, out_ref):
    current = orthonormal_rows(total_of(parts_ref))
    data = high_ref[...], low_ref[...]
    inner = mm3(halves(current), data, NN)
    spread(out_ref, mm3(halves(inner), data, NT))


def core_kernel(parts_ref, high_ref, low_ref, out_ref, rows_ref):
    current = halves(orthonormal_rows(total_of(parts_ref)))
    block = lax.axis_index("gw") * 2 + lax.axis_index("gc")
    cut = pl.ds(pl.multiple_of(block * LANES, LANES), LANES)
    rows_ref[...] = mm3(current, (high_ref[:, cut], low_ref[:, cut]), NN).T
    at = lax.axis_index("gu") * 16 + lax.axis_index("gv") * 4 + lax.axis_index("gh") * 2
    for e in range(out_ref.shape[1]):
        for b in range(out_ref.shape[0]):
            out_ref[b, e, :] = rows_ref[at + e * (LANES // 4) + b, :]


def call(kernel, out_shape, *args, scratch=(), in_hbm=0, limit=None):
    vmem = pl.BlockSpec(memory_space=pltpu.VMEM)
    hbm = pl.BlockSpec(memory_space=pltpu.HBM)
    return pl.pallas_call(
        kernel,
        out_shape=out_shape,
        in_specs=[hbm] * in_hbm + [vmem] * (len(args) - in_hbm),
        out_specs=jax.tree.map(lambda _: vmem, out_shape),
        compiler_params=pltpu.CompilerParams(vmem_limit_bytes=limit if in_hbm else VMEM_BYTES),
        scratch_shapes=[pltpu.VMEM(s, jnp.float32) if isinstance(s, tuple) else s for s in scratch],
    )(*args[:in_hbm], *[pltpu.with_memory_space_constraint(a, pltpu.VMEM) for a in args[in_hbm:]])


def vm(*shape, dtype=jnp.float32):
    return pltpu.VMEM(shape, dtype)


def swap(pieces, axes):
    return lax.all_to_all(pieces, axes, split_axis=0, concat_axis=0, tiled=True)


def copies(piece, axes):
    return jnp.broadcast_to(piece, (lax.axis_size(axes),) + piece.shape)


def shards(field, brick_order, start_first, start_second, start_third):
    species, rows_here, cells_y, cells_z = field.shape
    rows_x, rank_one = start_first.shape
    full_y, rank_two = start_second.shape
    rank_three = start_third.shape[1]
    brick_len = cells_z // brick_order.shape[0]
    merged_rows = species * rank_one
    devices = lax.axis_size(ORDER)
    chips = lax.axis_size(CHIPS)
    parts_y = full_y // LANES
    exchange = [(0, 1), (1, 0)]

    sent, start_first, start_second = call(
        functools.partial(send_field_kernel, brick_len=brick_len),
        (vm(cells_z * species, cells_y), vm(rank_one, rows_x), vm(rank_two, full_y)),
        brick_order,
        field.reshape(species, cells_y, cells_z),
        start_first.T,
        start_second.T,
        scratch=[
            (species, cells_y, cells_z),
            pltpu.SMEM(brick_order.shape, jnp.int32),
            pltpu.SemaphoreType.DMA((species,)),
            pltpu.SemaphoreType.DMA((3,)),
        ],
        in_hbm=4,
    )
    data = swap(sent.reshape(devices, species, cells_y), ORDER).reshape(devices * species, cells_y)

    gram = call(
        functools.partial(gram_first_kernel, species=species, rows_x=rows_x, parts=parts_y), vm(rows_x, rows_x), data
    )
    gram = jnp.sum(swap(gram.reshape(lax.axis_size(CLOSE), -1, rows_x), CLOSE), axis=0)
    gram = jnp.sum(swap(copies(gram, FAR), FAR), axis=0)
    gram = swap(copies(gram, CLOSE), CLOSE).reshape(rows_x, rows_x)

    high, low, kept, sent = call(
        functools.partial(second_kernel, species=species, rows_x=rows_x, parts=parts_y),
        (vm(merged_rows, full_y, dtype=jnp.bfloat16),) * 2 + (vm(parts_y * (parts_y + 1) // 4 * LANES, LANES),) * 2,
        gram,
        start_first,
        data,
        scratch=[(rank_one, rows_x), (merged_rows, full_y)],
    )
    swapped = lax.ppermute(sent, "gc", exchange)
    raw_third, kept = lax.optimization_barrier((start_third.T, kept))
    start_third = call(
        functools.partial(place_third_kernel, brick_len=brick_len),
        vm(rank_three, cells_z),
        brick_order,
        raw_third,
        scratch=[
            (rank_three, cells_z),
            (cells_z, rank_three),
            (cells_z, rank_three),
            pltpu.SMEM(brick_order.shape, jnp.int32),
            pltpu.SemaphoreType.DMA((2,)),
        ],
        in_hbm=2,
        limit=VMEM_BYTES,
    )
    kept, start_third = lax.optimization_barrier((kept, start_third))
    gram = kept + swapped
    gram = jnp.sum(swap(gram.reshape(lax.axis_size(BLOCK), -1, LANES), BLOCK), axis=0)
    gram = jnp.sum(swap(copies(gram, BEYOND), BEYOND), axis=0)
    own = swap(copies(gram, BLOCK), BLOCK).reshape(-1, LANES)
    other = lax.ppermute(own, "gc", exchange)

    sent = call(
        functools.partial(third_kernel, parts=parts_y),
        vm(lax.axis_size("gh"), lax.axis_size("gl"), lax.axis_size(("gu", "gv")), lax.axis_size("gk"), 2, 8, LANES),
        own,
        other,
        start_second,
        high,
        low,
        scratch=[(rank_two, merged_rows)],
    )
    own = swap(sent.reshape(chips, 4, LANES), CHIPS).reshape(chips * 4, LANES)
    other = lax.ppermute(own, "gc", exchange)
    own_cut = vm(cells_z // 2, 4 * LANES, dtype=jnp.bfloat16)
    own_high, own_low = call(functools.partial(own_third_kernel, parts=4), (own_cut, own_cut), own)

    spread_shape = vm(lax.axis_size(NEAR), rank_three, cells_z)
    cut = vm(cells_z, 4 * LANES, dtype=jnp.bfloat16)
    pieces, high, low = call(
        functools.partial(start_third_kernel, parts=4),
        (spread_shape, cut, cut),
        start_third,
        own_high,
        own_low,
        other,
    )
    for repeat in range(ITERS - 1):
        pieces = call(step_third_kernel, spread_shape, swap(pieces, NEAR), high, low)
    return call(
        core_kernel,
        jax.ShapeDtypeStruct((2, 4, rank_three), jnp.float32),
        swap(pieces, NEAR),
        high,
        low,
        scratch=[(merged_rows, rank_three)],
    )


def solution(mesh):
    gx, gy, gz = mesh.devices.shape
    fine = Mesh(mesh.devices.reshape(2, gx // 4, 2, 2, gy // 2, gz // 4, 2, 2), FINE)
    in_specs = (P(None, ("gu", "gv", "gk", "gw", "gp", "gc"), ("gh", "gl"), None), P(), P(), P(), P())
    out_specs = P(("gu", "gv", "gk", "gh", "gl"), ("gw", "gp", "gc"), None)
    return jax.shard_map(shards, mesh=fine, in_specs=in_specs, out_specs=out_specs, check_vma=False)
```

```python
import functools

import jax
import jax.numpy as jnp
from jax import lax
from jax.experimental import pallas as pl
from jax.experimental.pallas import tpu as pltpu
from jax.sharding import Mesh, PartitionSpec as P

ITERS = 2
LANES = 128
PANEL = 16
VMEM_BYTES = 20 << 20
FINE = ("gu", "gv", "gk", "gh", "gl", "gw", "gp", "gc")
CHIPS = ("gh", "gl", "gu", "gv", "gk", "gw", "gp")
ORDER = CHIPS + ("gc",)
NEAR = ("gl", "gk", "gp")
CLOSE = ("gl", "gw", "gp", "gc")
FAR = ("gh", "gu", "gv", "gk")
BLOCK = ("gw", "gk", "gp", "gl")
BEYOND = ("gu", "gh", "gv")

highest = lax.Precision.HIGHEST
NN = ((1,), (0,))
NT = ((1,), (1,))
TN = ((0,), (0,))


def mm(a, b, dims):
    return lax.dot_general(a, b, (dims, ((), ())), precision=highest, preferred_element_type=jnp.float32)


def halves(x):
    high = x.astype(jnp.bfloat16)
    return high, (x - high.astype(jnp.float32)).astype(jnp.bfloat16)


def mm3(a, b, dims):
    def dot(x, y):
        return lax.dot_general(x, y, (dims, ((), ())), preferred_element_type=jnp.float32)

    size = a[0].shape[0]
    both = dot(jnp.concatenate(a, axis=0), b[0])
    return both[:size] + (both[size:] + dot(a[0], b[1]))


def orthonormal_rows(wide):
    rank = wide.shape[0]
    inner = mm(wide, wide, NT)
    shape = (rank, rank)
    row_id = lax.broadcasted_iota(jnp.int32, shape, 0)
    inverse = (row_id == lax.broadcasted_iota(jnp.int32, shape, 1)).astype(jnp.float32)
    pivots = jnp.ones(shape, jnp.float32)
    for start in range(0, rank, PANEL):
        columns = [jnp.broadcast_to(inner[:, start + j : start + j + 1], shape) for j in range(PANEL)]
        for j in range(PANEL):
            k = start + j
            pivot = jnp.broadcast_to(columns[j][k : k + 1, :], shape)
            pivots = jnp.where(row_id == k, pivot, pivots)
            if k == rank - 1:
                break
            factor = jnp.where(row_id > k, columns[j] * (1.0 / pivot), 0.0)
            for i in range(j + 1, PANEL):
                columns[i] = columns[i] - factor * columns[i][k : k + 1, :]
            if start + PANEL < rank:
                inner = inner - factor * inner[k : k + 1, :]
            inverse = inverse - factor * inverse[k : k + 1, :]
    return mm(inverse * (1.0 / jnp.sqrt(pivots)), wide, NN)


def send_field_kernel(
    order_hbm, field_hbm, first_hbm, second_hbm, out_ref, first_ref, second_ref, field_ref, order_ref, sems, start_sems, *, brick_len
):
    species, cells_y, cells_z = field_hbm.shape
    loads = [pltpu.make_async_copy(field_hbm.at[s], field_ref.at[s], sems.at[s]) for s in range(species)]
    pairs = (order_hbm, order_ref), (second_hbm, second_ref), (first_hbm, first_ref)
    starts = [pltpu.make_async_copy(source, target, start_sems.at[i]) for i, (source, target) in enumerate(pairs)]
    for load in starts[:1] + loads + starts[1:]:
        load.start()
    starts[0].wait()
    lane = lax.broadcasted_iota(jnp.int32, (1, cells_z), 1)
    brick = lane // brick_len
    place = jnp.zeros((1, cells_z), jnp.int32)
    for b in range(cells_z // brick_len):
        place = jnp.where(brick == b, order_ref[b] * brick_len, place)
    grid_z = (place + lane % brick_len).astype(jnp.float32)
    taper = 0.5 + 1.5 * grid_z / (cells_z - 1)
    for s in range(species):
        loads[s].wait()
        for j in range(cells_z // LANES):
            cut = slice(j * LANES, (j + 1) * LANES)
            block = field_ref[s, :, cut] * taper[:, cut]
            out_ref[pl.ds(j * LANES * species + s, LANES, stride=species), :] = block.T
    for load in starts[1:]:
        load.wait()


def place_third_kernel(order_hbm, third_hbm, third_ref, raw_ref, rows_ref, placed_ref, order_ref, sems, *, brick_len):
    loads = [
        pltpu.make_async_copy(source, target, sems.at[i])
        for i, (source, target) in enumerate(((order_hbm, order_ref), (third_hbm, raw_ref)))
    ]
    for load in loads:
        load.start()
    for load in loads:
        load.wait()
    size = rows_ref.shape[0]
    rows_ref[...] = raw_ref[...].T
    for b in range(size // brick_len):
        at = pl.multiple_of(order_ref[b] * brick_len, brick_len)
        placed_ref[b * brick_len : (b + 1) * brick_len, :] = rows_ref[pl.ds(at, brick_len), :]
    core = lax.axis_index("gc")
    half = size // 2
    third_ref[:, :half] = placed_ref[pl.ds(core, half, stride=2), :].T
    third_ref[:, half:] = placed_ref[pl.ds(1 - core, half, stride=2), :].T


def fibre(ref, s, species, rows_x, parts):
    return jnp.concatenate(
        [ref[pl.ds(yq * rows_x * species + s, rows_x, stride=species), :] for yq in range(parts)], axis=1
    )


def gram_first_kernel(data_ref, out_ref, *, species, rows_x, parts):
    total = jnp.zeros(out_ref.shape, jnp.float32)
    for s in range(species):
        cut = halves(fibre(data_ref, s, species, rows_x, parts))
        total = total + mm3(cut, cut, NT)
    out_ref[...] = total


def second_kernel(
    gram_ref, start_ref, data_ref, merged_ref, kept_ref, sent_ref, rows_ref, *, species, rows_x, parts
):
    gram = gram_ref[...]
    current = start_ref[...]
    for repeat in range(ITERS):
        current = orthonormal_rows(mm(current, gram, NN))
    rank = current.shape[0]
    rows_ref[...] = current
    quarter = rank // 4
    order = [r for c in range(4) for r in range(rank) if (r >> 3 & 1) * 2 + (r >> 1 & 1) == c]
    current = halves(jnp.concatenate([rows_ref[r : r + 1, :] for r in order], axis=0))
    for s in range(species):
        product = mm3(current, halves(fibre(data_ref, s, species, rows_x, parts)), NN)
        for c in range(4):
            merged_ref[(c * species + s) * quarter : (c * species + s + 1) * quarter, :] = product[
                c * quarter : (c + 1) * quarter
            ]
    merged = merged_ref[...]
    flipped = halves(merged.T)
    merged = halves(merged)
    blocks = []
    for i in range(parts):
        cut = slice(i * LANES, (i + 1) * LANES)
        product = mm3([x[cut] for x in flipped], [x[:, i * LANES :] for x in merged], NN)
        blocks += [product[:, j * LANES : (j + 1) * LANES] for j in range(parts - i)]
    count = len(blocks) // 2
    first = lax.axis_index("gc") == 0
    for i in range(count):
        rows = slice(i * LANES, (i + 1) * LANES)
        kept_ref[rows, :] = jnp.where(first, blocks[i], blocks[count + i])
        sent_ref[rows, :] = jnp.where(first, blocks[count + i], blocks[i])


def symmetric_of(core, own_ref, other_ref, parts):
    pairs = (own_ref, other_ref), (other_ref, own_ref)
    blocks = []
    for first, second in pairs:
        for i in range(own_ref.shape[0] // LANES):
            rows = slice(i * LANES, (i + 1) * LANES)
            blocks.append(jnp.where(core == 0, first[rows, :], second[rows, :]))
    upper = {}
    for i in range(parts):
        for j in range(i, parts):
            upper[i, j] = blocks[len(upper)]
    lines = [[upper[i, j] if i <= j else upper[j, i].T for j in range(parts)] for i in range(parts)]
    return jnp.concatenate([jnp.concatenate(line, axis=1) for line in lines], axis=0)


def third_kernel(own_ref, other_ref, start_ref, merged_ref, out_ref, rows_ref, *, parts):
    gram = halves(symmetric_of(lax.axis_index("gc"), own_ref, other_ref, parts))
    current = start_ref[...]
    for repeat in range(ITERS):
        current = orthonormal_rows(mm3(halves(current), gram, NN))
    rows_ref[...] = mm3(halves(current), halves(merged_ref[...]), NT)
    quarter = LANES // 4
    groups = [rows_ref[pl.ds(e, rows_ref.shape[0] // 4, stride=4), :] for e in range(4)]
    group_id = lax.broadcasted_iota(jnp.int32, groups[0].shape, 1) // quarter
    for k in range(out_ref.shape[3]):
        for h in range(out_ref.shape[1]):
            c = k * 2 + h
            piece = pltpu.roll(groups[0], (4 - c) % 4 * quarter, 1) if c else groups[0]
            for e in range(1, 4):
                shift = (e - c) % 4 * quarter
                piece = jnp.where(group_id == e, pltpu.roll(groups[e], shift, 1) if shift else groups[e], piece)
            piece = jnp.concatenate([piece[0:2], piece[4:6], piece[2:4], piece[6:8]], axis=0)
            for i in range(out_ref.shape[0]):
                for j in range(out_ref.shape[2]):
                    for w in range(out_ref.shape[4]):
                        out_ref[i, h, j, k, w] = piece


def columns_of(own_ref, other_ref, parts):
    size = own_ref.shape[0] // parts
    return jnp.concatenate(
        [
            jnp.concatenate([ref[pl.ds(q, size, stride=parts), :] for q in range(parts)], axis=1)
            for ref in (own_ref, other_ref)
        ],
        axis=0,
    )


def spread(out_ref, wide):
    for i in range(out_ref.shape[0]):
        out_ref[i] = wide


def start_third_kernel(start_ref, own_ref, other_ref, out_ref, high_ref, low_ref, *, parts):
    data = halves(columns_of(own_ref, other_ref, parts))
    high_ref[...], low_ref[...] = data
    inner = mm3(halves(start_ref[...]), data, NN)
    spread(out_ref, mm3(halves(inner), data, NT))


def total_of(parts_ref):
    total = parts_ref[0]
    for i in range(1, parts_ref.shape[0]):
        total = total + parts_ref[i]
    return total


def step_third_kernel(parts_ref, high_ref, low_ref, out_ref):
    current = orthonormal_rows(total_of(parts_ref))
    data = high_ref[...], low_ref[...]
    inner = mm3(halves(current), data, NN)
    spread(out_ref, mm3(halves(inner), data, NT))


def core_kernel(parts_ref, high_ref, low_ref, out_ref, rows_ref):
    current = halves(orthonormal_rows(total_of(parts_ref)))
    block = lax.axis_index("gw") * 2 + lax.axis_index("gc")
    cut = pl.ds(pl.multiple_of(block * LANES, LANES), LANES)
    rows_ref[...] = mm3(current, (high_ref[:, cut], low_ref[:, cut]), NN).T
    at = lax.axis_index("gu") * 16 + lax.axis_index("gv") * 4 + lax.axis_index("gh") * 2
    for e in range(out_ref.shape[1]):
        for b in range(out_ref.shape[0]):
            out_ref[b, e, :] = rows_ref[at + e * (LANES // 4) + b, :]


def call(kernel, out_shape, *args, scratch=(), in_hbm=0, limit=None):
    vmem = pl.BlockSpec(memory_space=pltpu.VMEM)
    hbm = pl.BlockSpec(memory_space=pltpu.HBM)
    return pl.pallas_call(
        kernel,
        out_shape=out_shape,
        in_specs=[hbm] * in_hbm + [vmem] * (len(args) - in_hbm),
        out_specs=jax.tree.map(lambda _: vmem, out_shape),
        compiler_params=pltpu.CompilerParams(vmem_limit_bytes=limit if in_hbm else VMEM_BYTES),
        scratch_shapes=[pltpu.VMEM(s, jnp.float32) if isinstance(s, tuple) else s for s in scratch],
    )(*args[:in_hbm], *[pltpu.with_memory_space_constraint(a, pltpu.VMEM) for a in args[in_hbm:]])


def vm(*shape, dtype=jnp.float32):
    return pltpu.VMEM(shape, dtype)


def swap(pieces, axes):
    return lax.all_to_all(pieces, axes, split_axis=0, concat_axis=0, tiled=True)


def copies(piece, axes):
    return jnp.broadcast_to(piece, (lax.axis_size(axes),) + piece.shape)


def shards(field, brick_order, start_first, start_second, start_third):
    species, rows_here, cells_y, cells_z = field.shape
    rows_x, rank_one = start_first.shape
    full_y, rank_two = start_second.shape
    rank_three = start_third.shape[1]
    brick_len = cells_z // brick_order.shape[0]
    merged_rows = species * rank_one
    devices = lax.axis_size(ORDER)
    chips = lax.axis_size(CHIPS)
    parts_y = full_y // LANES
    exchange = [(0, 1), (1, 0)]

    sent, start_first, start_second = call(
        functools.partial(send_field_kernel, brick_len=brick_len),
        (vm(cells_z * species, cells_y), vm(rank_one, rows_x), vm(rank_two, full_y)),
        brick_order,
        field.reshape(species, cells_y, cells_z),
        start_first.T,
        start_second.T,
        scratch=[
            (species, cells_y, cells_z),
            pltpu.SMEM(brick_order.shape, jnp.int32),
            pltpu.SemaphoreType.DMA((species,)),
            pltpu.SemaphoreType.DMA((3,)),
        ],
        in_hbm=4,
    )
    data = swap(sent.reshape(devices, species, cells_y), ORDER).reshape(devices * species, cells_y)

    gram = call(
        functools.partial(gram_first_kernel, species=species, rows_x=rows_x, parts=parts_y), vm(rows_x, rows_x), data
    )
    gram = jnp.sum(swap(gram.reshape(lax.axis_size(CLOSE), -1, rows_x), CLOSE), axis=0)
    gram = jnp.sum(swap(copies(gram, FAR), FAR), axis=0)
    gram = swap(copies(gram, CLOSE), CLOSE).reshape(rows_x, rows_x)

    merged, kept, sent = call(
        functools.partial(second_kernel, species=species, rows_x=rows_x, parts=parts_y),
        (vm(merged_rows, full_y),) + (vm(parts_y * (parts_y + 1) // 4 * LANES, LANES),) * 2,
        gram,
        start_first,
        data,
        scratch=[(rank_one, rows_x)],
    )
    swapped = lax.ppermute(sent, "gc", exchange)
    raw_third, kept = lax.optimization_barrier((start_third.T, kept))
    start_third = call(
        functools.partial(place_third_kernel, brick_len=brick_len),
        vm(rank_three, cells_z),
        brick_order,
        raw_third,
        scratch=[
            (rank_three, cells_z),
            (cells_z, rank_three),
            (cells_z, rank_three),
            pltpu.SMEM(brick_order.shape, jnp.int32),
            pltpu.SemaphoreType.DMA((2,)),
        ],
        in_hbm=2,
        limit=VMEM_BYTES,
    )
    kept, start_third = lax.optimization_barrier((kept, start_third))
    gram = kept + swapped
    gram = jnp.sum(swap(gram.reshape(lax.axis_size(BLOCK), -1, LANES), BLOCK), axis=0)
    gram = jnp.sum(swap(copies(gram, BEYOND), BEYOND), axis=0)
    own = swap(copies(gram, BLOCK), BLOCK).reshape(-1, LANES)
    other = lax.ppermute(own, "gc", exchange)

    sent = call(
        functools.partial(third_kernel, parts=parts_y),
        vm(lax.axis_size("gh"), lax.axis_size("gl"), lax.axis_size(("gu", "gv")), lax.axis_size("gk"), 2, 8, LANES),
        own,
        other,
        start_second,
        merged,
        scratch=[(rank_two, merged_rows)],
    )
    own = swap(sent.reshape(chips, 4, LANES), CHIPS).reshape(chips * 4, LANES)
    other = lax.ppermute(own, "gc", exchange)

    spread_shape = vm(lax.axis_size(NEAR), rank_three, cells_z)
    cut = vm(cells_z, 4 * LANES, dtype=jnp.bfloat16)
    pieces, high, low = call(
        functools.partial(start_third_kernel, parts=4),
        (spread_shape, cut, cut),
        start_third,
        own,
        other,
    )
    for repeat in range(ITERS - 1):
        pieces = call(step_third_kernel, spread_shape, swap(pieces, NEAR), high, low)
    return call(
        core_kernel,
        jax.ShapeDtypeStruct((2, 4, rank_three), jnp.float32),
        swap(pieces, NEAR),
        high,
        low,
        scratch=[(merged_rows, rank_three)],
    )


def solution(mesh):
    gx, gy, gz = mesh.devices.shape
    fine = Mesh(mesh.devices.reshape(2, gx // 4, 2, 2, gy // 2, gz // 4, 2, 2), FINE)
    in_specs = (P(None, ("gu", "gv", "gk", "gw", "gp", "gc"), ("gh", "gl"), None), P(), P(), P(), P())
    out_specs = P(("gu", "gv", "gk", "gh", "gl"), ("gw", "gp", "gc"), None)
    return jax.shard_map(shards, mesh=fine, in_specs=in_specs, out_specs=out_specs, check_vma=False)
```
